256 devices in a mesh: batch: 8 (over z_lo, core), seq: 32 (over y, z_hi, x).
Axes of the slice: x: 4, y: 4, z: 8 (z_hi: 2, z_lo: 4; z = z_hi * 4 + z_lo), core: 2. Of those that a mesh axis runs over, the one named last changes fastest.
Arguments:
- token_ids: int32 [8, 8192], P('batch', 'seq'), may hold values from 0 to 3
- complement: int32 [4], replicated, may hold values from 0 to 3, each once
- embedding: bfloat16 [4, 1024], replicated, may hold values from -6 to 6
- in_weight: bfloat16 [1024, 2176], replicated, may hold values from -0.1875 to 0.1875
- step_weight: bfloat16 [1024, 16], replicated, may hold values from -0.1875 to 0.1875
- conv_weight: float32 [2, 4, 1152], replicated, may hold values from -3 to 3
- conv_bias: float32 [2, 1152], replicated, may hold values from -3 to 3
- step_bias: float32 [2, 16], replicated, may hold values from -4 to -2
- decay_rate: float32 [2, 16], replicated, as said below
- skip_gain: float32 [2, 16], replicated, may hold values from 0.5 to 1.5
- norm_gain: float32 [2, 1024], replicated, may hold values from 0.1 to 1.9
- out_weight: bfloat16 [1024, 1024], P('seq', 'batch'), may hold values from -0.1875 to 0.1875
Outputs:
- mixer_output: bfloat16 [8, 8192, 1024], P('batch', 'seq')
The draws below stay inside these ranges and needn't reach their ends.
Inputs may be any that keep to these rules, and one draw needn't show every extreme that they name: `decay_rate`: positive decay rate of each head.
All inputs are finite; a program needn't handle non-finite values.
Results may differ from the reference program's by a relative error of at most 0.0084.
Values may be sent and summed in bfloat16 or wider, within the bound.
A program may use at most 192 MiB of HBM per device.

```python
import jax
import jax.numpy as jnp
from jax import lax

D = 1024
E = 1024
H = 16
HEADDIM = 64
N = 64
KCONV = 4
BLOCK = 256
GEN = 8
SEQ_LEN = 8192
CONVCH = 1152


def draw_decay_rate(key, part):
    key_slow, key_fast, key_order = jax.random.split(jax.random.fold_in(key, 7), 3)
    slow_rates = jnp.exp(jax.random.uniform(key_slow, (2, H), jnp.float32, jnp.log(3.0), jnp.log(20.0))) / SEQ_LEN
    fast_rates = jnp.exp(jax.random.uniform(key_fast, (2, H), jnp.float32, jnp.log(0.2), jnp.log(1.0)))
    ranks = jnp.stack([jax.random.permutation(jax.random.fold_in(key_order, 0), H), jax.random.permutation(jax.random.fold_in(key_order, 1), H)])
    keep_count = H // 2
    return jnp.where(ranks < keep_count, slow_rates, fast_rates).astype(jnp.float32)


def place_ends(array, rng, least, largest):
    place = [jax.random.randint(jax.random.fold_in(rng, axis), (), 0, length) for axis, length in enumerate(array.shape)]
    main_axis = array.shape.index(max(array.shape))
    next_to = place[:main_axis] + [(place[main_axis] + 1) % array.shape[main_axis]] + place[main_axis + 1:]
    return array.at[tuple(place)].set(least).at[tuple(next_to)].set(largest)


def shard_levels(key, dims, cuts, low, high):
    factor_of = 1.0
    for dim, parts in cuts:
        draws = jax.random.uniform(jax.random.fold_in(jax.random.fold_in(key, 6), dim), (parts,), jnp.float32, low / len(cuts), high / len(cuts))
        factor_of = factor_of * jnp.repeat(jnp.exp(draws), dims[dim] // parts).reshape((-1,) + (1,) * (len(dims) - 1 - dim))
    return factor_of


def noise(rng, extent, deviation, most, pieces=(), dtype=jnp.bfloat16):
    array = jax.random.normal(rng, extent, jnp.float32) * deviation
    if len(pieces) > 0:
        array = shard_levels(rng, extent, pieces, -0.22, 0.18) * array
    return jnp.clip(array, min=-most, max=most).astype(dtype)


def setup_inputs(seed: int = 0) -> dict:
    splits = jax.random.split(jax.random.key(seed), 13)
    return {
        "token_ids": place_ends(jax.random.randint(splits[0], (GEN, SEQ_LEN), 0, 4), jax.random.fold_in(splits[0], 1), 0, 3).astype(jnp.int32),
        "complement": jax.random.permutation(splits[1], 4).astype(jnp.int32),
        "embedding": noise(splits[2], (4, D), 1.0, 6.0),
        "in_weight": noise(splits[3], (D, E + CONVCH), D ** -0.5, 0.1875),
        "step_weight": noise(splits[4], (D, H), D ** -0.5, 0.1875),
        "conv_weight": noise(splits[5], (2, KCONV, CONVCH), KCONV ** -0.5, 3.0, (), jnp.float32),
        "conv_bias": noise(splits[6], (2, CONVCH), 0.5, 3.0, (), jnp.float32),
        "step_bias": jnp.clip(jax.random.uniform(splits[7], (2, H), jnp.float32, -4.0, -2.0), -4.0, -2.0),
        "decay_rate": draw_decay_rate(jax.random.fold_in(splits[12], 71), 0),
        "skip_gain": jnp.clip(jax.random.uniform(splits[9], (2, H), jnp.float32, 0.5, 1.5), 0.5, 1.5),
        "norm_gain": jnp.clip(1.0 + 0.18 * jax.random.normal(splits[10], (2, E), jnp.float32), 0.1, 1.9),
        "out_weight": noise(splits[11], (E, D), E ** -0.5, 0.1875, ((0, 32), (1, 8))),
    }


exact_mode = lax.Precision.HIGHEST
norm_epsilon = 1e-05

def block_step(carry_state, inputs):
    values, b_rows, c_rows, step_sizes, decays = inputs
    running = jnp.cumsum(decays, axis=1)
    spread = running[:, :, None] - running[:, None, :]
    positions = jnp.arange(running.shape[1])
    lower_mask = positions[:, None] >= positions[None, :]
    weights = jnp.exp(jnp.where(lower_mask[None], spread, -jnp.inf))
    scores = jnp.dot(c_rows.astype(jnp.bfloat16), b_rows.astype(jnp.bfloat16).T, preferred_element_type=jnp.float32)
    mixing = weights * scores[None] * step_sizes[:, None, :]
    inside = jnp.einsum('hts,shp->thp', mixing, values, precision=exact_mode)
    carried = jnp.einsum('tn,hpn->thp', c_rows, carry_state, precision=exact_mode)
    carried = carried * jnp.exp(running).T[:, :, None]
    to_end = jnp.exp(running[:, -1:] - running) * step_sizes
    fresh_state = jnp.einsum('hs,shp,sn->hpn', to_end, values, b_rows, precision=exact_mode)
    carry_state = carry_state * jnp.exp(running[:, -1])[:, None, None] + fresh_state
    return (carry_state, inside + carried)

def state_scan(values, b_rows, c_rows, step_sizes, decays, block_rows):
    length, head_count, head_width = values.shape
    block_count = length // block_rows
    blocks = (values.reshape(block_count, block_rows, head_count, head_width), b_rows.reshape(block_count, block_rows, -1), c_rows.reshape(block_count, block_rows, -1), step_sizes.reshape(block_count, block_rows, head_count).transpose(0, 2, 1), decays.reshape(block_count, block_rows, head_count).transpose(0, 2, 1))
    start_state = jnp.zeros((head_count, head_width, b_rows.shape[1]), jnp.float32)
    final_state, outputs = lax.scan(block_step, start_state, blocks)
    return (final_state, outputs.reshape(length, head_count, head_width))

def conv_rows(conv_input, weight_rows, bias_row):
    kernel = weight_rows.shape[0]
    length = conv_input.shape[0]
    padded = jnp.pad(conv_input, ((kernel - 1, 0), (0, 0)))
    conv_total = bias_row[None, :]
    for offset in range(kernel):
        conv_total = conv_total + weight_rows[offset][None, :] * padded[offset:offset + length].astype(jnp.float32)
    return jax.nn.silu(conv_total).astype(jnp.bfloat16)

def gated_norm(outputs, gate_rows, gain_row):
    gated = outputs * jax.nn.silu(gate_rows.astype(jnp.float32))
    scale = lax.rsqrt(lax.optimization_barrier(jnp.mean(gated * gated, axis=-1, keepdims=True)) + norm_epsilon)
    return gated * scale * gain_row[None, :]

def reference(token_ids, complement, embedding, in_weight, step_weight, conv_weight, conv_bias, step_bias, decay_rate, skip_gain, norm_gain, out_weight):

    def direction(conv_input, gate_rows, step_raw, set_index, falling):
        length = conv_input.shape[0]
        if falling:
            conv_input = conv_input[::-1]
            step_raw = step_raw[::-1]
        conved = conv_rows(conv_input, conv_weight[set_index], conv_bias[set_index])
        values = conved[:, :E].astype(jnp.float32).reshape(length, H, HEADDIM)
        b_rows = conved[:, E:E + N].astype(jnp.float32)
        c_rows = conved[:, E + N:].astype(jnp.float32)
        step_sizes = jax.nn.softplus(step_raw + step_bias[set_index][None, :])
        decays = -decay_rate[set_index][None, :] * step_sizes
        final_state, outputs = state_scan(values, b_rows, c_rows, step_sizes, decays, BLOCK)
        outputs = outputs + skip_gain[set_index][None, :, None] * values
        outputs = outputs.reshape(length, E)
        if falling:
            outputs = outputs[::-1]
        return gated_norm(outputs, gate_rows, norm_gain[set_index])

    def strand(strand_rows):
        projected = jnp.dot(strand_rows, in_weight, preferred_element_type=jnp.float32).astype(jnp.bfloat16)
        gate_rows = projected[:, :E]
        conv_input = projected[:, E:]
        step_raw = jnp.dot(strand_rows, step_weight, preferred_element_type=jnp.float32)
        rising = direction(conv_input, gate_rows, step_raw, 0, False)
        falling = direction(conv_input, gate_rows, step_raw, 1, True)
        mixed_rows = (rising + falling).astype(jnp.bfloat16)
        return jnp.dot(mixed_rows, out_weight, preferred_element_type=jnp.float32).astype(jnp.bfloat16)

    def one_genome(tokens):
        flipped = complement[tokens[::-1]]
        forward_out = strand(embedding[tokens])
        other_out = strand(embedding[flipped])
        return (forward_out.astype(jnp.float32) + other_out[::-1].astype(jnp.float32)).astype(jnp.bfloat16)
    return lax.map(one_genome, token_ids)
```

```python
from functools import partial

import jax
import jax.numpy as jnp
from jax import lax
from jax.experimental import pallas as pl
from jax.experimental.pallas import tpu as pltpu
from jax.sharding import PartitionSpec as P

D = 1024
E = 1024
H = 16
N = 64
CH = 1152
BLOCK = 256
GRAMS = 256
ROWS = 272
LOG2E = 1.4426950408889634
EPS = 1e-05
F32 = jnp.float32
BF16 = jnp.bfloat16
HIGH = lax.Precision.HIGHEST
STRAND = (0, 1, 0, 1)
SET = (0, 1, 1, 0)
RISING = (True, True, False, False)


def iota(shape, dim):
    return lax.broadcasted_iota(jnp.int32, shape, dim)


def silu(x):
    return x * jax.nn.sigmoid(x)


def dot(a, b, **kw):
    return jnp.dot(a, b, preferred_element_type=F32, **kw)


def dot_t(a, b):
    return lax.dot_general(a, b, (((1,), (1,)), ((), ())), preferred_element_type=F32)


def letter_tables(comp, emb_ref, inw_ref, stw_ref, small_refs, gate_hi, gate_lo, conv_in, coef, skip_rows):
    row = iota((16, 1), 0)
    letter = jnp.where(row < 4, row, 4)
    for v in range(4):
        letter = jnp.where(row == 8 + v, comp[v], letter)
    emb = emb_ref[...].astype(F32)
    rows = jnp.zeros((16, D), F32)
    for x in range(4):
        rows = jnp.where(letter == x, emb[x : x + 1], rows)
    rows = rows.astype(BF16)
    projected = dot(rows, inw_ref[...]).astype(BF16).astype(F32)
    gate = silu(projected[:, :E])
    hi = gate.astype(BF16)
    gate_hi[...] = hi
    gate_lo[...] = (gate - hi.astype(F32)).astype(BF16)
    conv_in[...] = projected[:, E:]

    step_raw = dot(rows, stw_ref[...])
    lane = iota((16, 128), 1)
    spread = jnp.where((lane % 16 == iota((16, 128), 0)) & (lane < 64), 1.0, 0.0)
    step_raw = dot(step_raw, spread, precision=HIGH)
    bias_ref, rate_ref, gain_ref = small_refs
    row8 = iota((8, H), 0)
    packed = jnp.zeros((8, H), F32)
    for at, ref in ((0, bias_ref), (2, rate_ref), (4, gain_ref)):
        for d in range(2):
            packed = jnp.where(row8 == at + d, ref[d : d + 1, :], packed)
    spread_small = dot(packed, spread, precision=HIGH)
    sd = iota((1, 128), 1) // 16
    second_set = (sd == 1) | (sd == 2)
    other = sd % 2 == 1
    bias = jnp.where(second_set, spread_small[1:2], spread_small[0:1])
    rate = jnp.where(second_set, spread_small[3:4], spread_small[2:3])
    x = jnp.where(other, step_raw[8:16], step_raw[0:8]) + bias
    step = jnp.maximum(x, 0.0) + jnp.log1p(jnp.exp(-jnp.abs(x)))
    coef[...] = jnp.zeros_like(coef)
    coef[0:8, :] = -rate * step * LOG2E
    coef[8:16, :] = jnp.maximum(jnp.log(step) * LOG2E, -1e30)
    wide = jnp.where(iota((H, E), 1) // 64 == iota((H, E), 0), 1.0, 0.0)
    skip_rows[...] = dot(packed, wide, precision=HIGH)


def gram_tables(edge_letters, conv_in, cw_ref, cb_ref, s01, s23, table):
    letters = conv_in[0:8, :]
    for d in range(2):
        taps = [cw_ref[d, k : k + 1, :] * letters for k in range(4)]
        bias = cb_ref[d : d + 1, :]
        for x in range(4):
            s01[4 * x : 4 * x + 4, :] = bias + taps[0][x : x + 1] + taps[1][0:4]
            s23[4 * x : 4 * x + 4, :] = taps[2][x : x + 1] + taps[3][0:4]
        low = s23[...]
        for i in range(16):
            table[d, 16 * i : 16 * i + 16, :] = silu(s01[i : i + 1, :] + low).astype(BF16)
        total = jnp.broadcast_to(bias, (16, CH))
        for k in (1, 2, 3):
            for x in range(4):
                total = total + jnp.where(edge_letters[d][k] == x, taps[k][x : x + 1], 0.0)
        total = jnp.where(iota((16, 1), 0) < 8, silu(total), 0.0)
        table[d, GRAMS:ROWS, :] = total.astype(BF16)


def shifted(tokens, amount):
    lane = iota(tokens.shape, 1)
    moved = pltpu.roll(tokens, amount % BLOCK, axis=1)
    if amount > 0:
        return jnp.where(lane < amount, pltpu.roll(moved, 1, axis=0), moved)
    return jnp.where(lane >= BLOCK + amount, pltpu.roll(moved, tokens.shape[0] - 1, axis=0), moved)


def mixer(here, comp, tok_ref, emb_ref, inw_ref, stw_ref, cw_ref, cb_ref, small_refs, ng_ref, sc, finish):
    blocks = tok_ref.shape[0]
    letter_tables(
        comp, emb_ref, inw_ref, stw_ref, small_refs, sc["gate_hi"], sc["gate_lo"], sc["conv_in"], sc["coef"], sc["skip_rows"]
    )
    tokens = tok_ref[...]
    others = jnp.zeros_like(tokens)
    for v in range(4):
        others = jnp.where(tokens == v, comp[v], others)

    block_at, lane_at = iota(tokens.shape, 0), iota(tokens.shape, 1)
    low_edge = (block_at == 0) & (lane_at < 3)
    high_edge = (block_at == blocks - 1) & (lane_at >= BLOCK - 3)
    for strand, letters in ((0, tokens), (1, others)):
        rise = 64 * shifted(letters, 3) + 16 * shifted(letters, 2) + 4 * shifted(letters, 1) + letters
        fall = 64 * shifted(letters, -3) + 16 * shifted(letters, -2) + 4 * shifted(letters, -1) + letters
        sc["words"][strand] = jnp.where(low_edge, GRAMS + 4 * strand + lane_at, rise)
        sc["words"][2 + strand] = jnp.where(high_edge, GRAMS + 4 * strand + BLOCK - 1 - lane_at, fall)

    edge_letters = []
    row = iota((16, 1), 0)

    def letter_of(source, block, lane):
        line = source[block : block + 1, :]
        return jnp.sum(jnp.where(iota(line.shape, 1) == lane, line, 0), axis=1, keepdims=True)

    low = [[letter_of(s, 0, j) for j in range(3)] for s in (tokens, others)]
    high = [[letter_of(s, blocks - 1, BLOCK - 1 - j) for j in range(3)] for s in (tokens, others)]
    for d in range(2):
        first, second = (low[0], high[1]) if d == 0 else (high[0], low[1])
        columns = {}
        for k in (1, 2, 3):
            column = jnp.full((16, 1), 4, jnp.int32)
            for strand, letters in ((0, first), (1, second)):
                for j in range(3):
                    at = j - (3 - k)
                    if at >= 0:
                        column = jnp.where(row == 4 * strand + j, letters[at], column)
            columns[k] = column
        edge_letters.append(columns)
    gram_tables(edge_letters, sc["conv_in"], cw_ref, cb_ref, sc["s01"], sc["s23"], sc["table"])

    for v in range(4):
        sc["one_hot"][v * blocks : (v + 1) * blocks, :] = jnp.where(tokens == v, 1.0, 0.0)
    one_hot = sc["one_hot"][...]
    upper = jnp.where(iota((BLOCK, BLOCK), 0) <= iota((BLOCK, BLOCK), 1), 1.0, 0.0)
    inside = dot(one_hot.astype(BF16), upper.astype(BF16))
    sc["inside"][...] = inside
    total = inside[:, BLOCK - 1 : BLOCK]
    rows = 4 * blocks
    a, b = iota((rows, rows), 0), iota((rows, rows), 1)
    aj, bj = a % blocks, b % blocks
    between = (a // blocks == b // blocks) & (((aj < bj) & (bj < here)) | ((here < bj) & (bj < aj)))
    passed = dot(jnp.where(between, 1.0, 0.0).astype(BF16), jnp.broadcast_to(total, inside.shape).astype(BF16))
    before = iota((rows, 1), 0) % blocks < here
    sc["away"][...] = passed + jnp.where(before, total - inside, inside - one_hot)

    coef = sc["coef"][...].T
    column = [coef[:, v : v + 1] for v in range(16)]

    def entry_weights(j, side):
        part = slice(32 * side, 32 * side + 32)
        power = jnp.zeros((32, BLOCK), F32)
        for v in range(4):
            power = power + column[v][part] * sc["away"][pl.ds(v * blocks + j, 1), :]
            power = power + column[8 + v][part] * sc["one_hot"][pl.ds(v * blocks + j, 1), :]
        return jnp.exp2(power).astype(BF16)

    def entering(j, acc, side):
        words = sc["words"][2 * side, pl.ds(j, 1), :]
        hit = jnp.where(iota((GRAMS, BLOCK), 0) == words, 1.0, 0.0).astype(BF16)
        return acc + dot_t(hit, entry_weights(j, side))

    lane = iota((GRAMS, GRAMS), 1)
    other_word = jnp.zeros((1, GRAMS), jnp.int32)
    for place in (64, 16, 4, 1):
        digit = (iota((1, GRAMS), 1) // place) % 4
        for v in range(4):
            other_word = other_word + jnp.where(digit == v, comp[v] * place, 0)
    swap = jnp.where(iota((GRAMS, GRAMS), 0) == other_word, 1.0, 0.0).astype(BF16)
    zero = jnp.zeros((GRAMS, 32), F32)
    for side in (0, 1):
        if side == 0:
            acc = lax.fori_loop(0, here, partial(entering, side=0), zero)
            present = here > 0
            edge_block = 0
        else:
            acc = lax.fori_loop(here + 1, blocks, partial(entering, side=1), zero)
            present = here < blocks - 1
            edge_block = blocks - 1
        acc = acc.astype(BF16)
        swapped = dot(swap, acc)
        lane32 = iota((GRAMS, 32), 1)
        sc["weigh"][side, 0:GRAMS, :] = jnp.where(lane32 < 16, acc.astype(F32), swapped).astype(BF16)
        edge = entry_weights(edge_block, side)
        r16, l16 = iota((16, BLOCK), 0), iota((16, BLOCK), 1)
        pos = l16 if side == 0 else BLOCK - 1 - l16
        pick = jnp.where((pos < 3) & ((r16 == pos) | (r16 == 4 + pos)) & present, 1.0, 0.0).astype(BF16)
        picked = dot_t(pick, edge)
        own = (iota((16, 32), 0) < 4) == (iota((16, 32), 1) < 16)
        sc["weigh"][side, GRAMS:ROWS, :] = jnp.where(own, picked, 0.0).astype(BF16)

    def line(name, v):
        return sc[name][pl.ds(v * blocks + here, 1), :]

    inner = [line("inside", v) for v in range(4)]
    mine = [line("one_hot", v) for v in range(4)]
    sc["run"][...] = jnp.zeros_like(sc["run"])
    for side in (0, 1):
        part = slice(32 * side, 32 * side + 32)
        power = jnp.zeros((32, BLOCK), F32)
        size = jnp.zeros((32, BLOCK), F32)
        for v in range(4):
            count = inner[v] if side == 0 else inner[v][:, BLOCK - 1 : BLOCK] - inner[v] + mine[v]
            power = power + column[v][part] * count
            size = size + column[8 + v][part] * mine[v]
        sc["run"][part, :] = power
        sc["from"][part, :] = power - size
    run = sc["run"][...].T
    for i in range(4):
        sc["local"][i : i + 1, :] = sc["words"][i, pl.ds(here, 1), :].astype(F32)
    sc["local"][4:5, :] = tok_ref[pl.ds(here, 1), :].astype(F32)
    sc["local"][5:128, :] = jnp.zeros((123, BLOCK), F32)
    local = sc["local"][...].T.astype(jnp.int32)
    letter = local[:, 4:5]
    for strand in range(2):
        hit = jnp.where(iota((BLOCK, 16), 1) == letter + 8 * strand, 1.0, 0.0).astype(BF16)
        sc["gate"][strand] = dot(hit, sc["gate_hi"][...]) + dot(hit, sc["gate_lo"][...])

    left = iota((BLOCK, 128), 1) < 64
    half = BLOCK // 2
    t_at, s_at = iota((BLOCK, BLOCK), 0), iota((BLOCK, BLOCK), 1)
    for sd in range(4):
        d, side = SET[sd], sd // 2
        rising = RISING[sd]
        hit = jnp.where(iota((BLOCK, ROWS), 1) == local[:, sd : sd + 1], 1.0, 0.0).astype(BF16)
        conved = dot(hit, sc["table"][d])
        sc["conved"][...] = conved.astype(BF16)
        tail = conved[:, E:]
        b_rows = tail[:, :64].astype(BF16)
        c_rows = pltpu.roll(tail, 64, axis=1)[:, :64].astype(BF16)
        scores = dot_t(c_rows, b_rows)
        reach = s_at <= t_at if rising else s_at >= t_at
        sc["scores"][...] = jnp.where(reach, scores, 0.0)

        place = jnp.where(iota((32, E), 0) == 16 * (sd % 2) + iota((32, E), 1) // 64, 1.0, 0.0).astype(BF16)
        weights = dot(sc["weigh"][side], place)
        weighted = (weights * sc["table"][d, :, 0:E].astype(F32)).astype(BF16)
        b_columns = sc["table"][d, :, E:CH].astype(F32).T.astype(BF16)
        state = dot(b_columns[0:64], weighted).astype(BF16)
        sc["carried"][...] = dot(c_rows, state)

        square = jnp.zeros((BLOCK, 128), F32)
        for pair in range(8):
            cols = slice(128 * pair, 128 * pair + 128)
            values = sc["conved"][:, cols]
            parts, reached = [], []
            for sub in range(2):
                h = 16 * sd + 2 * pair + sub
                to = run[:, h : h + 1]
                source = sc["from"][h : h + 1, :]
                rows_of = []
                for top in (True, False):
                    ts = slice(0, half) if top else slice(half, BLOCK)
                    whole = top != rising
                    ss = slice(0, BLOCK) if whole else ts
                    mixing = jnp.exp2(jnp.minimum(to[ts] - source[:, ss], 100.0)) * sc["scores"][ts, ss]
                    rows_of.append(dot(mixing.astype(BF16), values[ss]))
                parts.append(jnp.concatenate(rows_of, axis=0))
                reached.append(jnp.broadcast_to(to, (BLOCK, 128)))
            both = jnp.where(left, parts[0], parts[1])
            both = both + sc["carried"][:, cols] * jnp.exp2(jnp.where(left, reached[0], reached[1]))
            both = both + sc["skip_rows"][4 + d : 5 + d, cols] * values.astype(F32)
            gated = both * sc["gate"][STRAND[sd], :, cols]
            square = square + gated * gated
            sc["gated"][:, cols] = gated
        mean = jnp.sum(square, axis=1, keepdims=True) * (1.0 / E)
        normed = sc["gated"][...] * lax.rsqrt(mean + EPS) * ng_ref[d : d + 1, :]
        if sd == 0:
            sc["mixed"][...] = normed
        else:
            sc["mixed"][...] += normed
    finish(sc["mixed"][...].astype(BF16))


def scratch(blocks):
    return {
        "gate_hi": pltpu.VMEM((16, E), BF16),
        "gate_lo": pltpu.VMEM((16, E), BF16),
        "conv_in": pltpu.VMEM((16, CH), F32),
        "coef": pltpu.VMEM((128, 128), F32),
        "skip_rows": pltpu.VMEM((8, E), F32),
        "words": pltpu.VMEM((4, blocks, BLOCK), jnp.int32),
        "s01": pltpu.VMEM((16, CH), F32),
        "s23": pltpu.VMEM((16, CH), F32),
        "table": pltpu.VMEM((2, ROWS, CH), BF16),
        "one_hot": pltpu.VMEM((4 * blocks, BLOCK), F32),
        "inside": pltpu.VMEM((4 * blocks, BLOCK), F32),
        "away": pltpu.VMEM((4 * blocks, BLOCK), F32),
        "weigh": pltpu.VMEM((2, ROWS, 32), BF16),
        "run": pltpu.VMEM((128, BLOCK), F32),
        "from": pltpu.VMEM((64, BLOCK), F32),
        "local": pltpu.VMEM((128, BLOCK), F32),
        "gate": pltpu.VMEM((2, BLOCK, E), F32),
        "conved": pltpu.VMEM((BLOCK, CH), BF16),
        "scores": pltpu.VMEM((BLOCK, BLOCK), F32),
        "carried": pltpu.VMEM((BLOCK, E), F32),
        "gated": pltpu.VMEM((BLOCK, E), F32),
        "mixed": pltpu.VMEM((BLOCK, E), F32),
    }


def kernel(names, here_ref, comp_ref, tok, emb, inw, stw, cw, cb, sb, dr, sg, ng, wout, out, *scratch_refs):
    sc = dict(zip(names, scratch_refs))
    comp = [comp_ref[v] for v in range(4)]

    def finish(mixed):
        out[...] = dot(mixed, wout[...]).astype(BF16)

    mixer(here_ref[0], comp, tok, emb, inw, stw, cw, cb, (sb, dr, sg), ng, sc, finish)


def mix(here, comp, tok, emb, inw, stw, cw, cb, sb, dr, sg, ng, wout):
    shapes = scratch(tok.shape[0])
    vmem = pl.BlockSpec(memory_space=pltpu.VMEM)
    smem = pl.BlockSpec(memory_space=pltpu.SMEM)
    return pl.pallas_call(
        partial(kernel, tuple(shapes)),
        out_shape=jax.ShapeDtypeStruct((BLOCK, D), BF16),
        in_specs=[smem, smem] + [vmem] * 11,
        out_specs=vmem,
        scratch_shapes=list(shapes.values()),
        compiler_params=pltpu.CompilerParams(vmem_limit_bytes=60 << 20),
    )(here, comp, tok, emb, inw, stw, cw, cb, sb, dr, sg, ng, wout)


def on_device(tok, comp, emb, inw, stw, cw, cb, sb, dr, sg, ng, wout):
    here = lax.axis_index("seq").astype(jnp.int32).reshape(1)
    tokens = lax.all_gather(tok[0], "seq", axis=0, tiled=False)
    columns = lax.all_gather(wout, "batch", axis=1, tiled=True)
    whole = lax.all_gather(columns, "seq", axis=0, tiled=True)
    return mix(here, comp, tokens, emb, inw, stw, cw, cb, sb, dr, sg, ng, whole)[None]


def solution(mesh):
    placed = (P("batch", "seq"),) + (P(),) * 10 + (P("seq", "batch"),)
    return jax.shard_map(
        on_device, mesh=mesh, in_specs=placed, out_specs=P("batch", "seq", None), check_vma=False
    )
```

```python
from functools import partial

import jax
import jax.numpy as jnp
from jax import lax
from jax.experimental import pallas as pl
from jax.experimental.pallas import tpu as pltpu
from jax.sharding import PartitionSpec as P

D = 1024
E = 1024
H = 16
N = 64
CH = 1152
BLOCK = 256
GRAMS = 256
ROWS = 272
LOG2E = 1.4426950408889634
EPS = 1e-05
F32 = jnp.float32
BF16 = jnp.bfloat16
HIGH = lax.Precision.HIGHEST
STRAND = (0, 1, 0, 1)
SET = (0, 1, 1, 0)
RISING = (True, True, False, False)


def iota(shape, dim):
    return lax.broadcasted_iota(jnp.int32, shape, dim)


def silu(x):
    return x * jax.nn.sigmoid(x)


def dot(a, b, **kw):
    return jnp.dot(a, b, preferred_element_type=F32, **kw)


def dot_t(a, b):
    return lax.dot_general(a, b, (((1,), (1,)), ((), ())), preferred_element_type=F32)


def letter_tables(comp, emb_ref, inw_ref, stw_ref, small_refs, gate_hi, gate_lo, conv_in, coef, skip_rows):
    row = iota((16, 1), 0)
    letter = jnp.where(row < 4, row, 4)
    for v in range(4):
        letter = jnp.where(row == 8 + v, comp[v], letter)
    emb = emb_ref[...].astype(F32)
    rows = jnp.zeros((16, D), F32)
    for x in range(4):
        rows = jnp.where(letter == x, emb[x : x + 1], rows)
    rows = rows.astype(BF16)
    projected = dot(rows, inw_ref[...]).astype(BF16).astype(F32)
    gate = silu(projected[:, :E])
    hi = gate.astype(BF16)
    gate_hi[...] = hi
    gate_lo[...] = (gate - hi.astype(F32)).astype(BF16)
    conv_in[...] = projected[:, E:]

    step_raw = dot_t(rows, stw_ref[...])
    lane = iota((16, 128), 1)
    spread = jnp.where((lane % 16 == iota((16, 128), 0)) & (lane < 64), 1.0, 0.0)
    step_raw = dot(step_raw, spread, precision=HIGH)
    bias_ref, rate_ref, gain_ref = small_refs
    row8 = iota((8, H), 0)
    packed = jnp.zeros((8, H), F32)
    for at, ref in ((0, bias_ref), (2, rate_ref), (4, gain_ref)):
        for d in range(2):
            packed = jnp.where(row8 == at + d, ref[d : d + 1, :], packed)
    spread_small = dot(packed, spread, precision=HIGH)
    sd = iota((1, 128), 1) // 16
    second_set = (sd == 1) | (sd == 2)
    other = sd % 2 == 1
    bias = jnp.where(second_set, spread_small[1:2], spread_small[0:1])
    rate = jnp.where(second_set, spread_small[3:4], spread_small[2:3])
    x = jnp.where(other, step_raw[8:16], step_raw[0:8]) + bias
    step = jnp.maximum(x, 0.0) + jnp.log1p(jnp.exp(-jnp.abs(x)))
    coef[...] = jnp.zeros_like(coef)
    coef[0:8, :] = -rate * step * LOG2E
    coef[8:16, :] = jnp.maximum(jnp.log(step) * LOG2E, -1e30)
    wide = jnp.where(iota((H, E), 1) // 64 == iota((H, E), 0), 1.0, 0.0)
    skip_rows[...] = dot(packed, wide, precision=HIGH)


def gram_tables(conv_in, cw_ref, cb_ref, s01, s23, table):
    letters = conv_in[0:8, :]
    for d in range(2):
        taps = [cw_ref[d, k : k + 1, :] * letters for k in range(4)]
        bias = cb_ref[d : d + 1, :]
        for x in range(4):
            s01[4 * x : 4 * x + 4, :] = bias + taps[0][x : x + 1] + taps[1][0:4]
            s23[4 * x : 4 * x + 4, :] = taps[2][x : x + 1] + taps[3][0:4]
        low = s23[...]
        for i in range(16):
            table[d, 16 * i : 16 * i + 16, :] = silu(s01[i : i + 1, :] + low).astype(BF16)


def edge_tables(edge_letters, conv_in, cw_ref, cb_ref, table):
    letters = conv_in[0:8, :]
    for d in range(2):
        taps = [cw_ref[d, k : k + 1, :] * letters for k in range(4)]
        bias = cb_ref[d : d + 1, :]
        total = jnp.broadcast_to(bias, (16, CH))
        for k in (1, 2, 3):
            for x in range(4):
                total = total + jnp.where(edge_letters[d][k] == x, taps[k][x : x + 1], 0.0)
        total = jnp.where(iota((16, 1), 0) < 8, silu(total), 0.0)
        table[d, GRAMS:ROWS, :] = total.astype(BF16)


def shifted(tokens, amount):
    lane = iota(tokens.shape, 1)
    moved = pltpu.roll(tokens, amount % BLOCK, axis=1)
    if amount > 0:
        return jnp.where(lane < amount, pltpu.roll(moved, 1, axis=0), moved)
    return jnp.where(lane >= BLOCK + amount, pltpu.roll(moved, tokens.shape[0] - 1, axis=0), moved)


def mixer(here, comp, tokens, cw_ref, cb_ref, ng_ref, sc, between_scans):
    blocks = tokens.shape[0]
    others = jnp.zeros_like(tokens)
    for v in range(4):
        others = jnp.where(tokens == v, comp[v], others)

    block_at, lane_at = iota(tokens.shape, 0), iota(tokens.shape, 1)
    low_edge = (block_at == 0) & (lane_at < 3)
    high_edge = (block_at == blocks - 1) & (lane_at >= BLOCK - 3)
    for strand, letters in ((0, tokens), (1, others)):
        rise = 64 * shifted(letters, 3) + 16 * shifted(letters, 2) + 4 * shifted(letters, 1) + letters
        fall = 64 * shifted(letters, -3) + 16 * shifted(letters, -2) + 4 * shifted(letters, -1) + letters
        sc["words"][strand] = jnp.where(low_edge, GRAMS + 4 * strand + lane_at, rise)
        sc["words"][2 + strand] = jnp.where(high_edge, GRAMS + 4 * strand + BLOCK - 1 - lane_at, fall)

    edge_letters = []
    row = iota((16, 1), 0)

    def letter_of(source, block, lane):
        line = source[block : block + 1, :]
        return jnp.sum(jnp.where(iota(line.shape, 1) == lane, line, 0), axis=1, keepdims=True)

    low = [[letter_of(s, 0, j) for j in range(3)] for s in (tokens, others)]
    high = [[letter_of(s, blocks - 1, BLOCK - 1 - j) for j in range(3)] for s in (tokens, others)]
    for d in range(2):
        first, second = (low[0], high[1]) if d == 0 else (high[0], low[1])
        columns = {}
        for k in (1, 2, 3):
            column = jnp.full((16, 1), 4, jnp.int32)
            for strand, letters in ((0, first), (1, second)):
                for j in range(3):
                    at = j - (3 - k)
                    if at >= 0:
                        column = jnp.where(row == 4 * strand + j, letters[at], column)
            columns[k] = column
        edge_letters.append(columns)
    edge_tables(edge_letters, sc["conv_in"], cw_ref, cb_ref, sc["table"])

    for v in range(4):
        sc["one_hot"][v * blocks : (v + 1) * blocks, :] = jnp.where(tokens == v, 1.0, 0.0)
    one_hot = sc["one_hot"][...]
    upper = jnp.where(iota((BLOCK, BLOCK), 0) <= iota((BLOCK, BLOCK), 1), 1.0, 0.0)
    inside = dot(one_hot.astype(BF16), upper.astype(BF16))
    sc["inside"][...] = inside
    total = inside[:, BLOCK - 1 : BLOCK]
    rows = 4 * blocks
    a, b = iota((rows, rows), 0), iota((rows, rows), 1)
    aj, bj = a % blocks, b % blocks
    between = (a // blocks == b // blocks) & (((aj < bj) & (bj < here)) | ((here < bj) & (bj < aj)))
    passed = dot(jnp.where(between, 1.0, 0.0).astype(BF16), jnp.broadcast_to(total, inside.shape).astype(BF16))
    before = iota((rows, 1), 0) % blocks < here
    sc["away"][...] = passed + jnp.where(before, total - inside, inside - one_hot)

    coef = sc["coef"][...].T
    column = [coef[:, v : v + 1] for v in range(16)]

    for side in (0, 1):
        for v in range(4):
            part = slice(32 * side, 32 * side + 32)
            sc["spread"][side, v] = jnp.broadcast_to(column[v][part], (32, 128))
            sc["spread"][side, 4 + v] = jnp.broadcast_to(column[8 + v][part], (32, 128))

    def entry_weights(j, side):
        counts = [sc["away"][pl.ds(v * blocks + j, 1), :] for v in range(4)]
        letter = [sc["one_hot"][pl.ds(v * blocks + j, 1), :] for v in range(4)]
        halves = []
        for lanes in (slice(0, 128), slice(128, 256)):
            power = jnp.zeros((32, 128), F32)
            for v in range(4):
                power = power + sc["spread"][side, v] * counts[v][:, lanes]
                power = power + sc["spread"][side, 4 + v] * letter[v][:, lanes]
            halves.append(jnp.exp2(power))
        return jnp.concatenate(halves, axis=1)

    word_of_row = iota((GRAMS, BLOCK), 0).astype(F32).astype(BF16)
    group = 8

    def entering(step, acc):
        hits, powers = [], []
        for i in range(group):
            j = step * group + i
            side = jnp.where(j < here, 0, 1)
            words = sc["words"][2 * side, pl.ds(j, 1), :].astype(F32).astype(BF16)
            hits.append(jnp.where(word_of_row == words, jnp.ones((), BF16), jnp.zeros((), BF16)))
            power = entry_weights(j, side)
            both = [jnp.where(j < here, power, 0.0), jnp.where(j > here, power, 0.0)]
            powers.append(jnp.concatenate(both, axis=0).astype(BF16))
        return acc + dot_t(jnp.concatenate(hits, axis=1), jnp.concatenate(powers, axis=1))

    other_word = jnp.zeros((1, GRAMS), jnp.int32)
    for place in (64, 16, 4, 1):
        digit = (iota((1, GRAMS), 1) // place) % 4
        for v in range(4):
            other_word = other_word + jnp.where(digit == v, comp[v] * place, 0)
    swap = jnp.where(iota((GRAMS, GRAMS), 0) == other_word, 1.0, 0.0).astype(BF16)
    acc = lax.fori_loop(0, blocks // group, entering, jnp.zeros((GRAMS, 64), F32)).astype(BF16)
    swapped = dot(swap, acc)
    lane64 = iota((GRAMS, 64), 1)
    sc["weigh"][0:GRAMS, :] = jnp.where(lane64 % 32 < 16, acc.astype(F32), swapped).astype(BF16)
    edges = []
    for side in (0, 1):
        present = here > 0 if side == 0 else here < blocks - 1
        edge = entry_weights(0 if side == 0 else blocks - 1, side)
        edges.append(jnp.where(present, edge, 0.0).astype(BF16))
    own = (iota((16, 32), 0) < 4) == (iota((16, 32), 1) < 16)
    for side in (0, 1):
        r16, l16 = iota((16, BLOCK), 0), iota((16, BLOCK), 1)
        pos = l16 if side == 0 else BLOCK - 1 - l16
        pick = jnp.where((pos < 3) & ((r16 == pos) | (r16 == 4 + pos)), 1.0, 0.0).astype(BF16)
        picked = jnp.where(own, dot_t(pick, edges[side]), 0.0)
        sc["edge"][:, 32 * side : 32 * side + 32] = picked
    sc["weigh"][GRAMS:ROWS, :] = sc["edge"][...].astype(BF16)

    def line(name, v):
        return sc[name][pl.ds(v * blocks + here, 1), :]

    inner = [line("inside", v) for v in range(4)]
    mine = [line("one_hot", v) for v in range(4)]
    sc["run"][...] = jnp.zeros_like(sc["run"])
    for side in (0, 1):
        part = slice(32 * side, 32 * side + 32)
        power = jnp.zeros((32, BLOCK), F32)
        size = jnp.zeros((32, BLOCK), F32)
        for v in range(4):
            count = inner[v] if side == 0 else inner[v][:, BLOCK - 1 : BLOCK] - inner[v] + mine[v]
            power = power + column[v][part] * count
            size = size + column[8 + v][part] * mine[v]
        sc["run"][part, :] = power
        sc["from"][part, :] = power - size
    run = sc["run"][...].T
    for i in range(4):
        sc["local"][i : i + 1, :] = sc["words"][i, pl.ds(here, 1), :].astype(F32)
    sc["local"][4:5, :] = sc["tokens"][pl.ds(here, 1), :].astype(F32)
    sc["local"][5:128, :] = jnp.zeros((123, BLOCK), F32)
    local = sc["local"][...].T.astype(jnp.int32)
    letter = local[:, 4:5]
    for strand in range(2):
        hit = jnp.where(iota((BLOCK, 16), 1) == letter + 8 * strand, 1.0, 0.0).astype(BF16)
        sc["gate"][strand] = dot(hit, sc["gate_hi"][...]) + dot(hit, sc["gate_lo"][...])

    left = iota((BLOCK, 128), 1) < 64
    half = BLOCK // 2
    t_at, s_at = iota((BLOCK, BLOCK), 0), iota((BLOCK, BLOCK), 1)
    for sd in range(4):
        d, side = SET[sd], sd // 2
        rising = RISING[sd]
        hit = jnp.where(iota((BLOCK, ROWS), 1) == local[:, sd : sd + 1], 1.0, 0.0).astype(BF16)
        conved = dot(hit, sc["table"][d])
        sc["conved"][...] = conved.astype(BF16)
        tail = conved[:, E:]
        b_rows = tail[:, :64].astype(BF16)
        c_rows = pltpu.roll(tail, 64, axis=1)[:, :64].astype(BF16)
        scores = dot_t(c_rows, b_rows)
        reach = s_at <= t_at if rising else s_at >= t_at
        sc["scores"][...] = jnp.where(reach, scores, 0.0)

        place = jnp.where(iota((64, E), 0) == 16 * sd + iota((64, E), 1) // 64, 1.0, 0.0).astype(BF16)
        weights = dot(sc["weigh"][...], place)
        weighted = (weights * sc["table"][d, :, 0:E].astype(F32)).astype(BF16)
        b_columns = sc["table"][d, :, E:CH].astype(F32).T.astype(BF16)
        state = dot(b_columns[0:64], weighted).astype(BF16)
        sc["carried"][...] = dot(c_rows, state)

        square = jnp.zeros((BLOCK, 128), F32)
        for pair in range(8):
            cols = slice(128 * pair, 128 * pair + 128)
            values = sc["conved"][:, cols]
            parts, reached = [], []
            for sub in range(2):
                h = 16 * sd + 2 * pair + sub
                to = run[:, h : h + 1]
                source = sc["from"][h : h + 1, :]
                rows_of = []
                for top in (True, False):
                    ts = slice(0, half) if top else slice(half, BLOCK)
                    whole = top != rising
                    ss = slice(0, BLOCK) if whole else ts
                    mixing = jnp.exp2(jnp.minimum(to[ts] - source[:, ss], 100.0)) * sc["scores"][ts, ss]
                    rows_of.append(dot(mixing.astype(BF16), values[ss]))
                parts.append(jnp.concatenate(rows_of, axis=0))
                reached.append(jnp.broadcast_to(to, (BLOCK, 128)))
            both = jnp.where(left, parts[0], parts[1])
            both = both + sc["carried"][:, cols] * jnp.exp2(jnp.where(left, reached[0], reached[1]))
            both = both + sc["skip_rows"][4 + d : 5 + d, cols] * values.astype(F32)
            gated = both * sc["gate"][STRAND[sd], :, cols]
            square = square + gated * gated
            sc["gated"][:, cols] = gated
        mean = jnp.sum(square, axis=1, keepdims=True) * (1.0 / E)
        normed = sc["gated"][...] * lax.rsqrt(mean + EPS) * ng_ref[d : d + 1, :]
        if sd == 0:
            sc["mixed"][...] = normed
        else:
            sc["mixed"][...] += normed
        between_scans(sd)
    return sc["mixed"][...].astype(BF16)


def scratch(blocks):
    return {
        "gate_hi": pltpu.VMEM((16, E), BF16),
        "gate_lo": pltpu.VMEM((16, E), BF16),
        "conv_in": pltpu.VMEM((16, CH), F32),
        "coef": pltpu.VMEM((128, 128), F32),
        "skip_rows": pltpu.VMEM((8, E), F32),
        "words": pltpu.VMEM((4, blocks, BLOCK), jnp.int32),
        "s01": pltpu.VMEM((16, CH), F32),
        "s23": pltpu.VMEM((16, CH), F32),
        "table": pltpu.VMEM((2, ROWS, CH), BF16),
        "one_hot": pltpu.VMEM((4 * blocks, BLOCK), F32),
        "inside": pltpu.VMEM((4 * blocks, BLOCK), F32),
        "away": pltpu.VMEM((4 * blocks, BLOCK), F32),
        "weigh": pltpu.VMEM((ROWS, 64), BF16),
        "edge": pltpu.VMEM((16, 64), F32),
        "spread": pltpu.VMEM((2, 8, 32, 128), F32),
        "tokens": pltpu.VMEM((blocks, BLOCK), jnp.int32),
        "run": pltpu.VMEM((128, BLOCK), F32),
        "from": pltpu.VMEM((64, BLOCK), F32),
        "local": pltpu.VMEM((128, BLOCK), F32),
        "gate": pltpu.VMEM((2, BLOCK, E), F32),
        "conved": pltpu.VMEM((BLOCK, CH), BF16),
        "scores": pltpu.VMEM((BLOCK, BLOCK), F32),
        "carried": pltpu.VMEM((BLOCK, E), F32),
        "gated": pltpu.VMEM((BLOCK, E), F32),
        "mixed": pltpu.VMEM((BLOCK, E), F32),
    }


MESH = pl.DeviceIdType.MESH
PARAMS = 10


def kernel(names, *refs):
    params, shard = refs[:PARAMS], refs[PARAMS]
    tok, out = refs[PARAMS + 1], refs[PARAMS + 2]
    sc = dict(zip(names, refs[PARAMS + 3 :]))
    batch, here = lax.axis_index("batch"), lax.axis_index("seq")
    z_low, core = lax.div(batch, 2), lax.rem(batch, 2)
    y, z_high, x = lax.div(here, 8), lax.rem(lax.div(here, 4), 2), lax.rem(here, 4)
    z, plane = z_high * 4 + z_low, y * 4 + x
    received, wall = sc["received"], sc["wall"]

    def on_z(other):
        return (lax.rem(other, 4) * 2 + core, y * 8 + lax.div(other, 4) * 4 + x)

    def on_plane(other):
        return (batch, lax.div(other, 4) * 8 + z_high * 4 + lax.rem(other, 4))

    partner = (z_low * 2 + 1 - core, here)

    barrier = pltpu.get_barrier_semaphore()

    def greet(device):
        pl.semaphore_signal(barrier, inc=1, device_id=device, device_id_type=MESH)

    def greet_seq(k, _):
        greet((batch, lax.rem(here + k, 32)))
        return 0

    def greet_z(k, _):
        greet((lax.rem(z_low + k, 4) * 2 + core, y * 8 + x))
        greet((lax.rem(z_low + k, 4) * 2 + core, y * 8 + 4 + x))
        return 0

    lax.fori_loop(1, 32, greet_seq, 0)
    lax.fori_loop(1, 4, greet_z, 0)
    greet(partner)

    fetch = [
        pltpu.make_async_copy(tok, received.at[here], sc["own_sem"].at[0]),
        pltpu.make_async_copy(shard, wall.at[core, plane, z], sc["own_sem"].at[1]),
    ]
    held = []
    for i, ref in enumerate(params):
        held.append(sc[f"held{i}"])
        fetch.append(pltpu.make_async_copy(ref, held[i], sc["own_sem"].at[2 + i]))
    for copy in fetch:
        copy.start()
    for copy in fetch:
        copy.wait()
    comp_ref, emb, inw, stw, cw, cb, sb, dr, sg, ng = held[:10]
    comp = [comp_ref[v] for v in range(4)]
    letter_tables(
        comp, emb, inw, stw, (sb, dr, sg), sc["gate_hi"], sc["gate_lo"], sc["conv_in"], sc["coef"], sc["skip_rows"]
    )
    gram_tables(sc["conv_in"], cw, cb, sc["s01"], sc["s23"], sc["table"])
    pl.semaphore_wait(barrier, 38)

    def token_copy(k, owner, device):
        return pltpu.make_async_remote_copy(
            received.at[owner], received.at[owner], sc["token_send"].at[k], sc["token_recv"].at[owner], device, MESH
        )

    def z_copy(k, owner, device):
        piece = wall.at[core, plane, owner]
        return pltpu.make_async_remote_copy(piece, piece, sc["z_send"].at[k], sc["z_recv"].at[owner], device, MESH)

    def plane_copy(k, owner, device):
        piece = wall.at[core, owner]
        return pltpu.make_async_remote_copy(
            piece, piece, sc["plane_send"].at[k], sc["plane_recv"].at[owner], device, MESH
        )

    def core_copy(side, owner):
        piece = wall.at[side, owner]
        return pltpu.make_async_remote_copy(
            piece, piece, sc["core_send"].at[owner], sc["core_recv"].at[owner], partner, MESH
        )

    def each(count, act):
        def go(k, _):
            act(k)
            return 0

        lax.fori_loop(1, count, go, 0)

    def seq_peer(k):
        return lax.rem(here + k, 32)

    def z_peer(k):
        return lax.rem(z + k, 8)

    def plane_peer(k):
        return lax.rem(plane + k, 16)

    each(8, lambda k: z_copy(k, z, on_z(z_peer(k))).start())
    each(32, lambda k: token_copy(k, here, (batch, seq_peer(k))).start())
    each(8, lambda k: z_copy(k, z_peer(k), on_z(z_peer(k))).wait_recv())
    each(16, lambda k: plane_copy(k, plane, on_plane(plane_peer(k))).start())
    core_copy(core, plane).start()
    each(32, lambda k: token_copy(k, seq_peer(k), (batch, seq_peer(k))).wait_recv())
    for j in range(32):
        sc["tokens"][j : j + 1, :] = received[j]

    def between_scans(sd):
        if sd == 2:
            def pass_on(k):
                plane_copy(k, plane_peer(k), on_plane(plane_peer(k))).wait_recv()
                core_copy(core, plane_peer(k)).start()

            each(16, pass_on)

    mixed = mixer(here, comp, sc["tokens"][...], cw, cb, ng, sc, between_scans)
    lax.fori_loop(0, 16, lambda q, c: (core_copy(1 - core, q).wait_recv(), c)[1], 0)
    order = [(4 * (s // 8) + s % 4, 4 * ((s // 4) % 2)) for s in range(32)]
    for low in range(4):
        sides = [jnp.concatenate([wall[c, p, h + low] for p, h in order], axis=0) for c in range(2)]
        out[:, 256 * low : 256 * low + 256] = dot(mixed, jnp.concatenate(sides, axis=1)).astype(BF16)

    each(8, lambda k: z_copy(k, z, on_z(z_peer(k))).wait_send())
    each(32, lambda k: token_copy(k, here, (batch, seq_peer(k))).wait_send())
    each(16, lambda k: plane_copy(k, plane, on_plane(plane_peer(k))).wait_send())
    lax.fori_loop(0, 16, lambda q, c: (core_copy(core, q).wait_send(), c)[1], 0)


def on_device(tok, comp, emb, inw, stw, cw, cb, sb, dr, sg, ng, wout):
    params = [comp, emb, inw, stw.T, cw, cb, sb, dr, sg, ng]
    shapes = scratch(32)
    shapes["received"] = pltpu.VMEM((32, 1, BLOCK), jnp.int32)
    shapes["wall"] = pltpu.VMEM((2, 16, 8, 32, 128), BF16)
    shapes["own_sem"] = pltpu.SemaphoreType.DMA((2 + PARAMS,))
    for name, count in (("token", 32), ("z", 8), ("plane", 16), ("core", 16)):
        shapes[name + "_send"] = pltpu.SemaphoreType.DMA((count,))
        shapes[name + "_recv"] = pltpu.SemaphoreType.DMA((count,))
    for i, value in enumerate(params):
        space = pltpu.SMEM if value.ndim == 1 else pltpu.VMEM
        shapes[f"held{i}"] = space(value.shape, value.dtype)
    anywhere = pl.BlockSpec(memory_space=pl.ANY)
    out = pl.pallas_call(
        partial(kernel, tuple(shapes)),
        out_shape=jax.ShapeDtypeStruct((BLOCK, D), BF16),
        in_specs=[anywhere] * (PARAMS + 2),
        out_specs=pl.BlockSpec(memory_space=pltpu.VMEM),
        scratch_shapes=list(shapes.values()),
        compiler_params=pltpu.CompilerParams(
            collective_id=0, has_side_effects=True, vmem_limit_bytes=60 << 20
        ),
    )(*params, wout, tok)
    return out[None]


def solution(mesh):
    placed = (P("batch", "seq"),) + (P(),) * 10 + (P("seq", "batch"),)
    return jax.shard_map(
        on_device, mesh=mesh, in_specs=placed, out_specs=P("batch", "seq", None), check_vma=False
    )
```

```python
from functools import partial

import jax
import jax.numpy as jnp
from jax import lax
from jax.experimental import pallas as pl
from jax.experimental.pallas import tpu as pltpu
from jax.sharding import PartitionSpec as P

D = 1024
E = 1024
H = 16
N = 64
CH = 1152
BLOCK = 256
GRAMS = 256
ROWS = 272
LOG2E = 1.4426950408889634
EPS = 1e-05
F32 = jnp.float32
BF16 = jnp.bfloat16
HIGH = lax.Precision.HIGHEST
STRAND = (0, 1, 0, 1)
SET = (0, 1, 1, 0)
RISING = (True, True, False, False)


def iota(shape, dim):
    return lax.broadcasted_iota(jnp.int32, shape, dim)


def silu(x):
    return x * jax.nn.sigmoid(x)


def dot(a, b, **kw):
    return jnp.dot(a, b, preferred_element_type=F32, **kw)


def dot_t(a, b):
    return lax.dot_general(a, b, (((1,), (1,)), ((), ())), preferred_element_type=F32)


def letter_tables(comp, emb_ref, inw_ref, stw_ref, small_refs, gate_parts, conv_in, coef, skip_rows):
    row = iota((16, 1), 0)
    letter = jnp.where(row < 4, row, 4)
    for v in range(4):
        letter = jnp.where(row == 8 + v, comp[v], letter)
    emb = emb_ref[...].astype(F32)
    rows = jnp.zeros((16, D), F32)
    for x in range(4):
        rows = jnp.where(letter == x, emb[x : x + 1], rows)
    rows = rows.astype(BF16)
    projected = dot(rows, inw_ref[...]).astype(BF16).astype(F32)
    gate = silu(projected[:, :E])
    hi = gate.astype(BF16)
    gate_parts[0:16, :] = hi
    gate_parts[16:32, :] = (gate - hi.astype(F32)).astype(BF16)
    conv_in[...] = projected[:, E:]

    step_raw = dot_t(rows, stw_ref[...])
    lane = iota((16, 128), 1)
    spread = jnp.where((lane % 16 == iota((16, 128), 0)) & (lane < 64), 1.0, 0.0)
    step_raw = dot(step_raw, spread, precision=HIGH)
    bias_ref, rate_ref, gain_ref = small_refs
    row8 = iota((8, H), 0)
    packed = jnp.zeros((8, H), F32)
    for at, ref in ((0, bias_ref), (2, rate_ref), (4, gain_ref)):
        for d in range(2):
            packed = jnp.where(row8 == at + d, ref[d : d + 1, :], packed)
    spread_small = dot(packed, spread, precision=HIGH)
    sd = iota((1, 128), 1) // 16
    second_set = (sd == 1) | (sd == 2)
    other = sd % 2 == 1
    bias = jnp.where(second_set, spread_small[1:2], spread_small[0:1])
    rate = jnp.where(second_set, spread_small[3:4], spread_small[2:3])
    x = jnp.where(other, step_raw[8:16], step_raw[0:8]) + bias
    step = jnp.maximum(x, 0.0) + jnp.log1p(jnp.exp(-jnp.abs(x)))
    coef[...] = jnp.zeros_like(coef)
    coef[0:8, :] = -rate * step * LOG2E
    coef[8:16, :] = jnp.maximum(jnp.log(step) * LOG2E, -1e30)
    wide = jnp.where(iota((H, E), 1) // 64 == iota((H, E), 0), 1.0, 0.0)
    skip_rows[...] = dot(packed, wide, precision=HIGH)


def gram_tables(conv_in, cw_ref, cb_ref, s01, s23, table):
    letters = conv_in[0:8, :]
    for d in range(2):
        taps = [cw_ref[d, k : k + 1, :] * letters for k in range(4)]
        bias = cb_ref[d : d + 1, :]
        for x in range(4):
            s01[4 * x : 4 * x + 4, :] = bias + taps[0][x : x + 1] + taps[1][0:4]
            s23[4 * x : 4 * x + 4, :] = taps[2][x : x + 1] + taps[3][0:4]
        low = s23[...]
        for i in range(16):
            table[d, 16 * i : 16 * i + 16, :] = silu(s01[i : i + 1, :] + low).astype(BF16)


def edge_tables(edge_letters, conv_in, cw_ref, cb_ref, table):
    letters = conv_in[0:8, :]
    for d in range(2):
        taps = [cw_ref[d, k : k + 1, :] * letters for k in range(4)]
        bias = cb_ref[d : d + 1, :]
        total = jnp.broadcast_to(bias, (16, CH))
        for k in (1, 2, 3):
            for x in range(4):
                total = total + jnp.where(edge_letters[d][k] == x, taps[k][x : x + 1], 0.0)
        total = jnp.where(iota((16, 1), 0) < 8, silu(total), 0.0)
        table[d, GRAMS:ROWS, :] = total.astype(BF16)


def shifted(tokens, amount):
    lane = iota(tokens.shape, 1)
    moved = pltpu.roll(tokens, amount % BLOCK, axis=1)
    if amount > 0:
        return jnp.where(lane < amount, pltpu.roll(moved, 1, axis=0), moved)
    return jnp.where(lane >= BLOCK + amount, pltpu.roll(moved, tokens.shape[0] - 1, axis=0), moved)


def local_counts(mine, sc):
    hot = jnp.concatenate([jnp.where(mine == v, 1.0, 0.0) for v in range(4)] + [jnp.zeros((4, BLOCK), F32)], axis=0)
    upper = jnp.where(iota((BLOCK, BLOCK), 0) <= iota((BLOCK, BLOCK), 1), 1.0, 0.0)
    count = dot(hot.astype(BF16), upper.astype(BF16))
    coef = sc["coef"][...].T
    sc["run"][...] = jnp.zeros_like(sc["run"])
    for side in (0, 1):
        part = slice(32 * side, 32 * side + 32)
        power = jnp.zeros((32, BLOCK), F32)
        size = jnp.zeros((32, BLOCK), F32)
        for v in range(4):
            passed = count[v : v + 1]
            if side == 1:
                passed = passed[:, BLOCK - 1 : BLOCK] - passed + hot[v : v + 1]
            power = power + coef[part, v : v + 1] * passed
            size = size + coef[part, 8 + v : 9 + v] * hot[v : v + 1]
        sc["run"][part, :] = power
        sc["from"][part, :] = power - size
        for v in range(8):
            at = v if v < 4 else v + 4
            sc["spread"][side, v] = jnp.broadcast_to(coef[part, at : at + 1], (32, 128))
    sc["run_t"][...] = sc["run"][...].T
    letter = jnp.broadcast_to(mine.astype(F32), (128, BLOCK)).T.astype(jnp.int32)[:, 0:32]
    for strand in range(2):
        hit = jnp.where(iota((BLOCK, 32), 1) % 16 == letter + 8 * strand, 1.0, 0.0).astype(BF16)
        sc["gate"][strand] = dot(hit, sc["gate_parts"][...])
    for d in range(2):
        sc["b_columns"][d, :, 0:GRAMS] = sc["table"][d, 0:GRAMS, E:CH].astype(F32).T.astype(BF16)


def local_decays(sd, sc):
    left = iota((BLOCK, 128), 1) < 64
    half = BLOCK // 2
    rising = RISING[sd]
    t_at, s_at = iota((half, half), 0), iota((half, half), 1)
    reach = s_at <= t_at if rising else s_at >= t_at
    for pair in range(8):
        reached = []
        for sub in range(2):
            h = 16 * sd + 2 * pair + sub
            to = jnp.broadcast_to(sc["run_t"][:, h : h + 1], (BLOCK, 128))
            reached.append(to)
            source = sc["from"][h : h + 1, :]
            for top in (0, 1):
                for side in (0, 1):
                    ts, ss = slice(half * top, half * top + half), slice(half * side, half * side + half)
                    if top == side:
                        decay = jnp.where(reach, jnp.exp2(to[ts] - source[:, ss]), 0.0)
                    elif (side < top) == rising:
                        decay = jnp.exp2(to[ts] - source[:, ss])
                    else:
                        continue
                    sc["decay"][h, ts, ss] = decay.astype(BF16)
        sc["grow"][sd, :, 128 * pair : 128 * pair + 128] = jnp.exp2(jnp.where(left, reached[0], reached[1]))


def mixer(here, comp, tokens, cw_ref, cb_ref, ng_ref, sc, after_history, between_scans):
    blocks = tokens.shape[0]
    others = jnp.zeros_like(tokens)
    for v in range(4):
        others = jnp.where(tokens == v, comp[v], others)

    block_at, lane_at = iota(tokens.shape, 0), iota(tokens.shape, 1)
    low_edge = (block_at == 0) & (lane_at < 3)
    high_edge = (block_at == blocks - 1) & (lane_at >= BLOCK - 3)
    for strand, letters in ((0, tokens), (1, others)):
        rise = 64 * shifted(letters, 3) + 16 * shifted(letters, 2) + 4 * shifted(letters, 1) + letters
        fall = 64 * shifted(letters, -3) + 16 * shifted(letters, -2) + 4 * shifted(letters, -1) + letters
        sc["words"][strand] = jnp.where(low_edge, GRAMS + 4 * strand + lane_at, rise)
        sc["words"][2 + strand] = jnp.where(high_edge, GRAMS + 4 * strand + BLOCK - 1 - lane_at, fall)

    edge_letters = []
    row = iota((16, 1), 0)

    def letter_of(source, block, lane):
        line = source[block : block + 1, :]
        return jnp.sum(jnp.where(iota(line.shape, 1) == lane, line, 0), axis=1, keepdims=True)

    low = [[letter_of(s, 0, j) for j in range(3)] for s in (tokens, others)]
    high = [[letter_of(s, blocks - 1, BLOCK - 1 - j) for j in range(3)] for s in (tokens, others)]
    for d in range(2):
        first, second = (low[0], high[1]) if d == 0 else (high[0], low[1])
        columns = {}
        for k in (1, 2, 3):
            column = jnp.full((16, 1), 4, jnp.int32)
            for strand, letters in ((0, first), (1, second)):
                for j in range(3):
                    at = j - (3 - k)
                    if at >= 0:
                        column = jnp.where(row == 4 * strand + j, letters[at], column)
            columns[k] = column
        edge_letters.append(columns)
    edge_tables(edge_letters, sc["conv_in"], cw_ref, cb_ref, sc["table"])

    for v in range(4):
        sc["one_hot"][v * blocks : (v + 1) * blocks, :] = jnp.where(tokens == v, 1.0, 0.0)
    one_hot = sc["one_hot"][...]
    upper = jnp.where(iota((BLOCK, BLOCK), 0) <= iota((BLOCK, BLOCK), 1), 1.0, 0.0)
    inside = dot(one_hot.astype(BF16), upper.astype(BF16))
    sc["inside"][...] = inside
    total = inside[:, BLOCK - 1 : BLOCK]
    rows = 4 * blocks
    a, b = iota((rows, rows), 0), iota((rows, rows), 1)
    aj, bj = a % blocks, b % blocks
    between = (a // blocks == b // blocks) & (((aj < bj) & (bj < here)) | ((here < bj) & (bj < aj)))
    passed = dot(jnp.where(between, 1.0, 0.0).astype(BF16), jnp.broadcast_to(total, inside.shape).astype(BF16))
    before = iota((rows, 1), 0) % blocks < here
    sc["away"][...] = passed + jnp.where(before, total - inside, inside - one_hot)

    def entry_weights(j, side):
        counts = [sc["away"][pl.ds(v * blocks + j, 1), :] for v in range(4)]
        letter = [sc["one_hot"][pl.ds(v * blocks + j, 1), :] for v in range(4)]
        halves = []
        for lanes in (slice(0, 128), slice(128, 256)):
            power = jnp.zeros((32, 128), F32)
            for v in range(4):
                power = power + sc["spread"][side, v] * counts[v][:, lanes]
                power = power + sc["spread"][side, 4 + v] * letter[v][:, lanes]
            halves.append(jnp.exp2(power))
        return jnp.concatenate(halves, axis=1)

    word_of_row = iota((GRAMS, BLOCK), 0).astype(F32).astype(BF16)
    group = 8

    def entering(step, acc):
        hits, powers = [], []
        for i in range(group):
            j = step * group + i
            side = jnp.where(j < here, 0, 1)
            words = sc["words"][2 * side, pl.ds(j, 1), :].astype(F32).astype(BF16)
            hits.append(jnp.where(word_of_row == words, jnp.ones((), BF16), jnp.zeros((), BF16)))
            power = entry_weights(j, side)
            both = [jnp.where(j < here, power, 0.0), jnp.where(j > here, power, 0.0)]
            powers.append(jnp.concatenate(both, axis=0).astype(BF16))
        return acc + dot_t(jnp.concatenate(hits, axis=1), jnp.concatenate(powers, axis=1))

    other_word = jnp.zeros((1, GRAMS), jnp.int32)
    for place in (64, 16, 4, 1):
        digit = (iota((1, GRAMS), 1) // place) % 4
        for v in range(4):
            other_word = other_word + jnp.where(digit == v, comp[v] * place, 0)
    swap = jnp.where(iota((GRAMS, GRAMS), 0) == other_word, 1.0, 0.0).astype(BF16)
    acc = lax.fori_loop(0, blocks // group, entering, jnp.zeros((GRAMS, 64), F32)).astype(BF16)
    swapped = dot(swap, acc)
    lane64 = iota((GRAMS, 64), 1)
    sc["weigh"][0:GRAMS, :] = jnp.where(lane64 % 32 < 16, acc.astype(F32), swapped).astype(BF16)
    edges = []
    for side in (0, 1):
        present = here > 0 if side == 0 else here < blocks - 1
        edge = entry_weights(0 if side == 0 else blocks - 1, side)
        edges.append(jnp.where(present, edge, 0.0).astype(BF16))
    own = (iota((16, 32), 0) < 4) == (iota((16, 32), 1) < 16)
    for side in (0, 1):
        r16, l16 = iota((16, BLOCK), 0), iota((16, BLOCK), 1)
        pos = l16 if side == 0 else BLOCK - 1 - l16
        pick = jnp.where((pos < 3) & ((r16 == pos) | (r16 == 4 + pos)), 1.0, 0.0).astype(BF16)
        picked = jnp.where(own, dot_t(pick, edges[side]), 0.0)
        sc["edge"][:, 32 * side : 32 * side + 32] = picked
    sc["weigh"][GRAMS:ROWS, :] = sc["edge"][...].astype(BF16)

    for i in range(4):
        sc["local"][i : i + 1, :] = sc["words"][i, pl.ds(here, 1), :].astype(F32)
    sc["local"][4:128, :] = jnp.zeros((124, BLOCK), F32)
    local = sc["local"][...].T.astype(jnp.int32)
    for d in range(2):
        tail = sc["table"][d, GRAMS:ROWS, E:CH].astype(F32)
        tail = jnp.concatenate([tail, jnp.zeros((112, CH - E), F32)], axis=0).T
        sc["b_columns"][d, :, GRAMS:ROWS] = tail[:, 0 : ROWS - GRAMS].astype(BF16)

    after_history()
    left = iota((BLOCK, 128), 1) < 64
    half = BLOCK // 2
    for sd in range(4):
        d, rising = SET[sd], RISING[sd]
        hit = jnp.where(iota((BLOCK, ROWS), 1) == local[:, sd : sd + 1], 1.0, 0.0).astype(BF16)
        conved = dot(hit, sc["table"][d])
        sc["conved"][...] = conved.astype(BF16)
        tail = conved[:, E:]
        b_rows = tail[:, :64].astype(BF16)
        c_rows = pltpu.roll(tail, 64, axis=1)[:, :64].astype(BF16)
        sc["scores"][...] = dot_t(c_rows, b_rows).astype(BF16)

        place = jnp.where(iota((64, E), 0) == 16 * sd + iota((64, E), 1) // 64, 1.0, 0.0).astype(BF16)
        weights = dot(sc["weigh"][...], place)
        weighted = weights.astype(BF16) * sc["table"][d, :, 0:E]
        state = dot(sc["b_columns"][d, 0:64, :], weighted).astype(BF16)
        sc["carried"][...] = dot(c_rows, state)

        square = jnp.zeros((BLOCK, 128), F32)
        for pair in range(8):
            cols = slice(128 * pair, 128 * pair + 128)
            values = sc["conved"][:, cols]
            parts = []
            for sub in range(2):
                h = 16 * sd + 2 * pair + sub
                rows_of = []
                for top in (True, False):
                    ts = slice(0, half) if top else slice(half, BLOCK)
                    ss = slice(0, BLOCK) if top != rising else ts
                    rows_of.append(dot(sc["decay"][h, ts, ss] * sc["scores"][ts, ss], values[ss]))
                parts.append(jnp.concatenate(rows_of, axis=0))
            both = jnp.where(left, parts[0], parts[1])
            both = both + sc["carried"][:, cols] * sc["grow"][sd, :, cols]
            both = both + sc["skip_rows"][4 + d : 5 + d, cols] * values.astype(F32)
            gated = both * sc["gate"][STRAND[sd], :, cols]
            square = square + gated * gated
            sc["gated"][:, cols] = gated
        mean = jnp.sum(square, axis=1, keepdims=True) * (1.0 / E)
        normed = sc["gated"][...] * lax.rsqrt(mean + EPS) * ng_ref[d : d + 1, :]
        if sd == 0:
            sc["mixed"][...] = normed
        else:
            sc["mixed"][...] += normed
        between_scans(sd)
    return sc["mixed"][...].astype(BF16)


def scratch(blocks):
    return {
        "gate_parts": pltpu.VMEM((32, E), BF16),
        "conv_in": pltpu.VMEM((16, CH), F32),
        "coef": pltpu.VMEM((128, 128), F32),
        "skip_rows": pltpu.VMEM((8, E), F32),
        "words": pltpu.VMEM((4, blocks, BLOCK), jnp.int32),
        "s01": pltpu.VMEM((16, CH), F32),
        "s23": pltpu.VMEM((16, CH), F32),
        "table": pltpu.VMEM((2, ROWS, CH), BF16),
        "one_hot": pltpu.VMEM((4 * blocks, BLOCK), F32),
        "inside": pltpu.VMEM((4 * blocks, BLOCK), F32),
        "away": pltpu.VMEM((4 * blocks, BLOCK), F32),
        "weigh": pltpu.VMEM((ROWS, 64), BF16),
        "edge": pltpu.VMEM((16, 64), F32),
        "spread": pltpu.VMEM((2, 8, 32, 128), F32),
        "tokens": pltpu.VMEM((blocks, BLOCK), jnp.int32),
        "run": pltpu.VMEM((128, BLOCK), F32),
        "from": pltpu.VMEM((64, BLOCK), F32),
        "local": pltpu.VMEM((128, BLOCK), F32),
        "gate": pltpu.VMEM((2, BLOCK, E), F32),
        "conved": pltpu.VMEM((BLOCK, CH), BF16),
        "scores": pltpu.VMEM((BLOCK, BLOCK), BF16),
        "run_t": pltpu.VMEM((BLOCK, 128), F32),
        "b_columns": pltpu.VMEM((2, 128, ROWS), BF16),
        "decay": pltpu.VMEM((64, BLOCK, BLOCK), BF16),
        "grow": pltpu.VMEM((4, BLOCK, E), F32),
        "carried": pltpu.VMEM((BLOCK, E), F32),
        "gated": pltpu.VMEM((BLOCK, E), F32),
        "mixed": pltpu.VMEM((BLOCK, E), F32),
    }


MESH = pl.DeviceIdType.MESH
PARAMS = 10


def kernel(names, *refs):
    params, shard = refs[:PARAMS], refs[PARAMS]
    tok, out = refs[PARAMS + 1], refs[PARAMS + 2]
    sc = dict(zip(names, refs[PARAMS + 3 :]))
    batch, here = lax.axis_index("batch"), lax.axis_index("seq")
    z_low, core = lax.div(batch, 2), lax.rem(batch, 2)
    y, z_high, x = lax.div(here, 8), lax.rem(lax.div(here, 4), 2), lax.rem(here, 4)
    z = z_high * 4 + z_low
    received, wall = sc["received"], sc["wall"]
    partner = (z_low * 2 + 1 - core, here)
    barrier = pltpu.get_barrier_semaphore()

    def greet(device):
        pl.semaphore_signal(barrier, inc=1, device_id=device, device_id_type=MESH)

    def at(xx, yy, zz):
        return (lax.rem(zz, 4) * 2 + core, yy * 8 + lax.div(zz, 4) * 4 + xx)

    def loop(first, last, act):
        def go(k, carry):
            act(k)
            return carry

        lax.fori_loop(first, last, go, 0)

    def greet_z(k):
        greet((lax.rem(z_low + k, 4) * 2 + core, y * 8 + x))
        greet((lax.rem(z_low + k, 4) * 2 + core, y * 8 + 4 + x))

    loop(1, 32, lambda k: greet((batch, lax.rem(here + k, 32))))
    loop(1, 4, greet_z)
    greet(partner)

    def copy_of(piece, send, recv, device):
        return pltpu.make_async_remote_copy(piece, piece, send, recv, device, MESH)

    def seq_peer(k):
        return lax.rem(here + k, 32)

    def token_copy(k, owner):
        return copy_of(received.at[owner], sc["token_send"].at[k], sc["token_recv"].at[owner], (batch, seq_peer(k)))

    mine, inner, outer = [y * 4 + x, x * 4 + y], [x, y], [y, x]

    def z_copy(c, k, owner):
        piece = wall.at[core, c, mine[c], owner]
        return copy_of(piece, sc["z_send"].at[c, k], sc["z_recv"].at[c, owner], at(x, y, lax.rem(z + k, 8)))

    def along(c, k, first):
        step_x, step_y = at(lax.rem(x + k, 4), y, z), at(x, lax.rem(y + k, 4), z)
        return step_x if (c == 0) == first else step_y

    def second_copy(c, k, owner):
        piece = wall.at[core, c, 4 * outer[c] + owner]
        return copy_of(piece, sc["second_send"].at[c, k], sc["second_recv"].at[c, owner], along(c, k, True))

    def third_copy(c, k, owner):
        piece = wall.at[core, c, pl.ds(4 * owner, 4)]
        return copy_of(piece, sc["third_send"].at[c, k], sc["third_recv"].at[c, owner], along(c, k, False))

    def core_copy(side, c, owner):
        piece = wall.at[side, c, pl.ds(4 * owner, 4)]
        return copy_of(piece, sc["core_send"].at[c, owner], sc["core_recv"].at[c, owner], partner)

    first = [pltpu.make_async_copy(tok, received.at[here], sc["own_sem"].at[0])]
    for c in range(2):
        half = shard.at[16 * c : 16 * c + 16]
        first.append(pltpu.make_async_copy(half, wall.at[core, c, mine[c], z], sc["own_sem"].at[1 + c]))
    fetch, held = [], []
    for i, ref in enumerate(params):
        held.append(sc[f"held{i}"])
        fetch.append(pltpu.make_async_copy(ref, held[i], sc["own_sem"].at[3 + i]))
    for copy in first + fetch:
        copy.start()
    for copy in first:
        copy.wait()

    def send():
        pl.semaphore_wait(barrier, 38)
        for c in range(2):
            loop(1, 8, lambda k: z_copy(c, k, z).start())
        loop(1, 32, lambda k: token_copy(k, here).start())

    def pass_on_z():
        for c in range(2):
            loop(1, 8, lambda k: z_copy(c, k, lax.rem(z + k, 8)).wait_recv())
            loop(1, 4, lambda k: second_copy(c, k, inner[c]).start())

    distance = z + lax.min(y, 4 - y) + lax.min(x, 4 - x)
    soon = (z_high == 0) & (distance < 4)
    later = (z_high == 0) & (distance >= 4)
    last = z_high == 1

    pl.when(last)(send)
    for copy in fetch:
        copy.wait()
    comp_ref, emb, inw, stw, cw, cb, sb, dr, sg, ng = held
    comp = [comp_ref[v] for v in range(4)]
    letter_tables(
        comp, emb, inw, stw, (sb, dr, sg), sc["gate_parts"], sc["conv_in"], sc["coef"], sc["skip_rows"]
    )
    gram_tables(sc["conv_in"], cw, cb, sc["s01"], sc["s23"], sc["table"])
    pl.when(later)(send)
    local_counts(received[here], sc)
    pl.when(last)(pass_on_z)
    local_decays(0, sc)
    local_decays(1, sc)
    pl.when(later)(pass_on_z)
    local_decays(2, sc)
    local_decays(3, sc)

    @pl.when(soon)
    def _():
        send()
        pass_on_z()

    loop(1, 32, lambda k: token_copy(k, seq_peer(k)).wait_recv())
    for j in range(32):
        sc["tokens"][j : j + 1, :] = received[j]

    def pass_on_second():
        for c in range(2):
            loop(1, 4, lambda k: second_copy(c, k, lax.rem(inner[c] + k, 4)).wait_recv())
            loop(1, 4, lambda k: third_copy(c, k, outer[c]).start())
            core_copy(core, c, outer[c]).start()

    def pass_on_third(sd):
        if sd in (1, 2):
            for k in (1, 3) if sd == 1 else (2,):
                for c in range(2):
                    owner = lax.rem(outer[c] + k, 4)
                    third_copy(c, k, owner).wait_recv()
                    core_copy(core, c, owner).start()

    mixed = mixer(here, comp, sc["tokens"][...], cw, cb, ng, sc, pass_on_second, pass_on_third)
    for c in range(2):
        loop(0, 4, lambda q: core_copy(1 - core, c, q).wait_recv())
    order = []
    for s in range(32):
        yy, zz, xx = s // 8, 4 * ((s // 4) % 2), s % 4
        order += [(0, 4 * yy + xx, zz), (1, 4 * xx + yy, zz)]
    for low in range(4):
        sides = [jnp.concatenate([wall[k, c, p, zz + low] for c, p, zz in order], axis=0) for k in range(2)]
        out[:, 256 * low : 256 * low + 256] = dot(mixed, jnp.concatenate(sides, axis=1)).astype(BF16)

    for c in range(2):
        loop(1, 8, lambda k: z_copy(c, k, z).wait_send())
        loop(1, 4, lambda k: second_copy(c, k, inner[c]).wait_send())
        loop(1, 4, lambda k: third_copy(c, k, outer[c]).wait_send())
        loop(0, 4, lambda q: core_copy(core, c, q).wait_send())
    loop(1, 32, lambda k: token_copy(k, here).wait_send())


def on_device(tok, comp, emb, inw, stw, cw, cb, sb, dr, sg, ng, wout):
    params = [comp, emb, inw, stw.T, cw, cb, sb, dr, sg, ng]
    shapes = scratch(32)
    shapes["received"] = pltpu.VMEM((32, 1, BLOCK), jnp.int32)
    shapes["wall"] = pltpu.VMEM((2, 2, 16, 8, 16, 128), BF16)
    shapes["own_sem"] = pltpu.SemaphoreType.DMA((3 + PARAMS,))
    for name, count in (("token", (32,)), ("z", (2, 8)), ("second", (2, 4)), ("third", (2, 4)), ("core", (2, 4))):
        shapes[name + "_send"] = pltpu.SemaphoreType.DMA(count)
        shapes[name + "_recv"] = pltpu.SemaphoreType.DMA(count)
    for i, value in enumerate(params):
        space = pltpu.SMEM if value.ndim == 1 else pltpu.VMEM
        shapes[f"held{i}"] = space(value.shape, value.dtype)
    anywhere = pl.BlockSpec(memory_space=pl.ANY)
    out = pl.pallas_call(
        partial(kernel, tuple(shapes)),
        out_shape=jax.ShapeDtypeStruct((BLOCK, D), BF16),
        in_specs=[anywhere] * (PARAMS + 2),
        out_specs=pl.BlockSpec(memory_space=pltpu.VMEM),
        scratch_shapes=list(shapes.values()),
        compiler_params=pltpu.CompilerParams(
            collective_id=0, has_side_effects=True, vmem_limit_bytes=60 << 20
        ),
    )(*params, wout, tok)
    return out[None]


def solution(mesh):
    placed = (P("batch", "seq"),) + (P(),) * 10 + (P("seq", "batch"),)
    return jax.shard_map(
        on_device, mesh=mesh, in_specs=placed, out_specs=P("batch", "seq", None), check_vma=False
    )
```

```python
from functools import partial

import jax
import jax.numpy as jnp
from jax import lax
from jax.experimental import pallas as pl
from jax.experimental.pallas import tpu as pltpu
from jax.sharding import PartitionSpec as P

D = 1024
E = 1024
H = 16
N = 64
CH = 1152
BLOCK = 256
GRAMS = 256
ROWS = 272
LOG2E = 1.4426950408889634
EPS = 1e-05
F32 = jnp.float32
BF16 = jnp.bfloat16
HIGH = lax.Precision.HIGHEST
STRAND = (0, 1, 0, 1)
SET = (0, 1, 1, 0)
RISING = (True, True, False, False)


def iota(shape, dim):
    return lax.broadcasted_iota(jnp.int32, shape, dim)


def silu(x):
    return x * jax.nn.sigmoid(x)


def dot(a, b, **kw):
    return jnp.dot(a, b, preferred_element_type=F32, **kw)


def dot_t(a, b):
    return lax.dot_general(a, b, (((1,), (1,)), ((), ())), preferred_element_type=F32)


def letter_tables(comp, emb_ref, inw_ref, stw_ref, small_refs, gate_parts, conv_in, coef, skip_rows):
    row = iota((16, 1), 0)
    letter = jnp.where(row < 4, row, 4)
    for v in range(4):
        letter = jnp.where(row == 8 + v, comp[v], letter)
    emb = emb_ref[...].astype(F32)
    rows = jnp.zeros((16, D), F32)
    for x in range(4):
        rows = jnp.where(letter == x, emb[x : x + 1], rows)
    rows = rows.astype(BF16)
    projected = dot(rows, inw_ref[...]).astype(BF16).astype(F32)
    gate = silu(projected[:, :E])
    hi = gate.astype(BF16)
    gate_parts[0:16, :] = hi
    gate_parts[16:32, :] = (gate - hi.astype(F32)).astype(BF16)
    conv_in[...] = projected[:, E:]

    step_raw = dot_t(rows, stw_ref[...])
    lane = iota((16, 128), 1)
    spread = jnp.where((lane % 16 == iota((16, 128), 0)) & (lane < 64), 1.0, 0.0)
    step_raw = dot(step_raw, spread, precision=HIGH)
    bias_ref, rate_ref, gain_ref = small_refs
    row8 = iota((8, H), 0)
    packed = jnp.zeros((8, H), F32)
    for at, ref in ((0, bias_ref), (2, rate_ref), (4, gain_ref)):
        for d in range(2):
            packed = jnp.where(row8 == at + d, ref[d : d + 1, :], packed)
    spread_small = dot(packed, spread, precision=HIGH)
    sd = iota((1, 128), 1) // 16
    second_set = (sd == 1) | (sd == 2)
    other = sd % 2 == 1
    bias = jnp.where(second_set, spread_small[1:2], spread_small[0:1])
    rate = jnp.where(second_set, spread_small[3:4], spread_small[2:3])
    x = jnp.where(other, step_raw[8:16], step_raw[0:8]) + bias
    step = jnp.maximum(x, 0.0) + jnp.log1p(jnp.exp(-jnp.abs(x)))
    coef[...] = jnp.zeros_like(coef)
    coef[0:8, :] = -rate * step * LOG2E
    coef[8:16, :] = jnp.maximum(jnp.log(step) * LOG2E, -1e30)
    wide = jnp.where(iota((H, E), 1) // 64 == iota((H, E), 0), 1.0, 0.0)
    skip_rows[...] = dot(packed, wide, precision=HIGH)


def gram_tables(conv_in, cw_ref, cb_ref, s01, s23, table):
    letters = conv_in[0:8, :]
    for d in range(2):
        taps = [cw_ref[d, k : k + 1, :] * letters for k in range(4)]
        bias = cb_ref[d : d + 1, :]
        for x in range(4):
            s01[4 * x : 4 * x + 4, :] = bias + taps[0][x : x + 1] + taps[1][0:4]
            s23[4 * x : 4 * x + 4, :] = taps[2][x : x + 1] + taps[3][0:4]
        low = s23[...]
        for i in range(16):
            table[d, 16 * i : 16 * i + 16, :] = silu(s01[i : i + 1, :] + low).astype(BF16)


def edge_tables(edge_letters, conv_in, cw_ref, cb_ref, table):
    letters = conv_in[0:8, :]
    for d in range(2):
        taps = [cw_ref[d, k : k + 1, :] * letters for k in range(4)]
        bias = cb_ref[d : d + 1, :]
        total = jnp.broadcast_to(bias, (16, CH))
        for k in (1, 2, 3):
            for x in range(4):
                total = total + jnp.where(edge_letters[d][k] == x, taps[k][x : x + 1], 0.0)
        total = jnp.where(iota((16, 1), 0) < 8, silu(total), 0.0)
        table[d, GRAMS:ROWS, :] = total.astype(BF16)


def shifted(tokens, amount):
    lane = iota(tokens.shape, 1)
    moved = pltpu.roll(tokens, amount % BLOCK, axis=1)
    if amount > 0:
        return jnp.where(lane < amount, pltpu.roll(moved, 1, axis=0), moved)
    return jnp.where(lane >= BLOCK + amount, pltpu.roll(moved, tokens.shape[0] - 1, axis=0), moved)


def local_counts(mine, sc):
    hot = jnp.concatenate([jnp.where(mine == v, 1.0, 0.0) for v in range(4)] + [jnp.zeros((4, BLOCK), F32)], axis=0)
    upper = jnp.where(iota((BLOCK, BLOCK), 0) <= iota((BLOCK, BLOCK), 1), 1.0, 0.0)
    count = dot(hot.astype(BF16), upper.astype(BF16))
    coef = sc["coef"][...].T
    sc["run"][...] = jnp.zeros_like(sc["run"])
    for side in (0, 1):
        part = slice(32 * side, 32 * side + 32)
        power = jnp.zeros((32, BLOCK), F32)
        size = jnp.zeros((32, BLOCK), F32)
        for v in range(4):
            passed = count[v : v + 1]
            if side == 1:
                passed = passed[:, BLOCK - 1 : BLOCK] - passed + hot[v : v + 1]
            power = power + coef[part, v : v + 1] * passed
            size = size + coef[part, 8 + v : 9 + v] * hot[v : v + 1]
        sc["run"][part, :] = power
        sc["from"][part, :] = power - size
        k = iota((32, 48), 1)
        factor = jnp.zeros((32, 48), F32)
        for v in range(4):
            decay, size = coef[part, v : v + 1], coef[part, 8 + v : 9 + v]
            value = jnp.where(k < 16, 64.0 * decay, jnp.where(k < 32, decay, size))
            factor = jnp.where(k % 4 == v, value, factor)
        pieces = []
        for _ in range(3):
            pieces.append(factor.astype(BF16).astype(F32))
            factor = factor - pieces[-1]
        pieces = jnp.concatenate(pieces, axis=0)
        block = (iota((96, 48), 1) // 4) % 4
        for at in range(4):
            sc["factor"][side, at] = jnp.where(block == at, pieces, 0.0).astype(BF16)
    sc["run_t"][...] = sc["run"][...].T
    letter = jnp.broadcast_to(mine.astype(F32), (128, BLOCK)).T.astype(jnp.int32)[:, 0:32]
    for strand in range(2):
        hit = jnp.where(iota((BLOCK, 32), 1) % 16 == letter + 8 * strand, 1.0, 0.0).astype(BF16)
        sc["gate"][strand] = dot(hit, sc["gate_parts"][...])
    eye = iota((128, 128), 0) == iota((128, 128), 1)
    for d in range(2):
        for h in range(H):
            gain = sc["skip_rows"][4 + d : 5 + d, 64 * h : 64 * h + 1]
            sc["skip_eye"][16 * d + h] = jnp.where(eye, gain, 0.0).astype(BF16)
        sc["b_columns"][d, :, 0:GRAMS] = sc["table"][d, 0:GRAMS, E:CH].astype(F32).T.astype(BF16)


def local_conv(mine, comp, sc):
    others = jnp.zeros_like(mine)
    for v in range(4):
        others = jnp.where(mine == v, comp[v], others)
    lane = iota(mine.shape, 1)
    words = []
    for sd in range(4):
        letters = others if STRAND[sd] else mine
        word = letters
        for k in (1, 2, 3):
            word = word + 4**k * pltpu.roll(letters, k if RISING[sd] else BLOCK - k, axis=1)
        inside = lane >= 3 if RISING[sd] else lane < BLOCK - 3
        words.append(jnp.where(inside, word, -1).astype(F32))
    words = jnp.concatenate(words + [jnp.zeros((124, BLOCK), F32)], axis=0).T.astype(jnp.int32)
    for sd in range(4):
        hit = jnp.where(iota((BLOCK, GRAMS), 1) == words[:, sd : sd + 1], 1.0, 0.0).astype(BF16)
        sc["conved"][sd] = dot(hit, sc["table"][SET[sd], 0:GRAMS]).astype(BF16)
    other_word = jnp.zeros((1, GRAMS), jnp.int32)
    for place in (64, 16, 4, 1):
        digit = (iota((1, GRAMS), 1) // place) % 4
        for v in range(4):
            other_word = other_word + jnp.where(digit == v, comp[v] * place, 0)
    sc["swap"][...] = jnp.where(iota((GRAMS, GRAMS), 0) == other_word, 1.0, 0.0).astype(BF16)


def local_decays(sd, sc):
    left = iota((BLOCK, 128), 1) < 64
    half = BLOCK // 2
    rising = RISING[sd]
    t_at, s_at = iota((half, half), 0), iota((half, half), 1)
    reach = s_at <= t_at if rising else s_at >= t_at
    for pair in range(8):
        reached = []
        for sub in range(2):
            h = 16 * sd + 2 * pair + sub
            to = jnp.broadcast_to(sc["run_t"][:, h : h + 1], (BLOCK, 128))
            reached.append(to)
            source = sc["from"][h : h + 1, :]
            for top in (0, 1):
                for side in (0, 1):
                    ts, ss = slice(half * top, half * top + half), slice(half * side, half * side + half)
                    if top == side:
                        decay = jnp.where(reach, jnp.exp2(to[ts] - source[:, ss]), 0.0)
                    elif (side < top) == rising:
                        decay = jnp.exp2(to[ts] - source[:, ss])
                    else:
                        continue
                    sc["decay"][h, ts, ss] = decay.astype(BF16)
        sc["grow"][sd, :, 128 * pair : 128 * pair + 128] = jnp.exp2(jnp.where(left, reached[0], reached[1]))


def mixer(here, comp, tokens, cw_ref, cb_ref, ng_ref, sc, between_scans):
    blocks = tokens.shape[0]
    others = jnp.zeros_like(tokens)
    for v in range(4):
        others = jnp.where(tokens == v, comp[v], others)

    block_at, lane_at = iota(tokens.shape, 0), iota(tokens.shape, 1)
    low_edge = (block_at == 0) & (lane_at < 3)
    high_edge = (block_at == blocks - 1) & (lane_at >= BLOCK - 3)
    for strand, letters in ((0, tokens), (1, others)):
        rise = 64 * shifted(letters, 3) + 16 * shifted(letters, 2) + 4 * shifted(letters, 1) + letters
        fall = 64 * shifted(letters, -3) + 16 * shifted(letters, -2) + 4 * shifted(letters, -1) + letters
        sc["words"][strand] = jnp.where(low_edge, GRAMS + 4 * strand + lane_at, rise)
        sc["words"][2 + strand] = jnp.where(high_edge, GRAMS + 4 * strand + BLOCK - 1 - lane_at, fall)

    edge_letters = []
    row = iota((16, 1), 0)

    def letter_of(source, block, lane):
        line = source[block : block + 1, :]
        return jnp.sum(jnp.where(iota(line.shape, 1) == lane, line, 0), axis=1, keepdims=True)

    low = [[letter_of(s, 0, j) for j in range(3)] for s in (tokens, others)]
    high = [[letter_of(s, blocks - 1, BLOCK - 1 - j) for j in range(3)] for s in (tokens, others)]
    for d in range(2):
        first, second = (low[0], high[1]) if d == 0 else (high[0], low[1])
        columns = {}
        for k in (1, 2, 3):
            column = jnp.full((16, 1), 4, jnp.int32)
            for strand, letters in ((0, first), (1, second)):
                for j in range(3):
                    at = j - (3 - k)
                    if at >= 0:
                        column = jnp.where(row == 4 * strand + j, letters[at], column)
            columns[k] = column
        edge_letters.append(columns)
    edge_tables(edge_letters, sc["conv_in"], cw_ref, cb_ref, sc["table"])

    rows = 4 * blocks
    one_hot = jnp.where(sc["fourfold"][...] == iota((rows, BLOCK), 0) % 4, 1.0, 0.0)
    upper = jnp.where(iota((BLOCK, BLOCK), 0) <= iota((BLOCK, BLOCK), 1), 1.0, 0.0)
    inside = dot(one_hot.astype(BF16), upper.astype(BF16))
    total = inside[:, BLOCK - 1 : BLOCK]
    a, b = iota((rows, rows), 0), iota((rows, rows), 1)
    aj, bj = a // 4, b // 4
    between = (a % 4 == b % 4) & (((aj < bj) & (bj < here)) | ((here < bj) & (bj < aj)))
    passed = dot(jnp.where(between, 1.0, 0.0).astype(BF16), jnp.broadcast_to(total, inside.shape).astype(BF16))
    before = iota((rows, 1), 0) // 4 < here
    away = passed + jnp.where(before, total - inside, inside - one_hot)
    high = jnp.floor(away * (1.0 / 64.0))
    sc["counts"][0] = high.astype(BF16)
    sc["counts"][1] = (away - 64.0 * high).astype(BF16)
    sc["counts"][2] = one_hot.astype(BF16)

    def entry_weights(four, at, side):
        start = 16 * four if isinstance(four, int) else pl.multiple_of(16 * four, 16)
        counts = jnp.concatenate([sc["counts"][i, pl.ds(start, 16), :] for i in range(3)], axis=0)
        power = dot(sc["factor"][side, at], counts)
        return jnp.exp2(power[0:32] + power[32:64] + power[64:96])

    word_of_row = iota((GRAMS, BLOCK), 0).astype(F32).astype(BF16)
    group = 8

    def entering(step, acc):
        hits, powers = [], []
        for i in range(group):
            j = step * group + i
            side = jnp.where(j < here, 0, 1)
            words = sc["words"][2 * side, pl.ds(j, 1), :].astype(F32).astype(BF16)
            hits.append(jnp.where(word_of_row == words, jnp.ones((), BF16), jnp.zeros((), BF16)))
            power = entry_weights(step * (group // 4) + i // 4, i % 4, side)
            both = [jnp.where(j < here, power, 0.0), jnp.where(j > here, power, 0.0)]
            powers.append(jnp.concatenate(both, axis=0).astype(BF16))
        return acc + dot_t(jnp.concatenate(hits, axis=1), jnp.concatenate(powers, axis=1))

    acc = lax.fori_loop(0, blocks // group, entering, jnp.zeros((GRAMS, 64), F32)).astype(BF16)
    swapped = dot(sc["swap"][...], acc)
    lane64 = iota((GRAMS, 64), 1)
    sc["weigh"][0:GRAMS, :] = jnp.where(lane64 % 32 < 16, acc.astype(F32), swapped).astype(BF16)
    edges = []
    for side in (0, 1):
        present = here > 0 if side == 0 else here < blocks - 1
        edge = entry_weights(0, 0, 0) if side == 0 else entry_weights(blocks // 4 - 1, 3, 1)
        edges.append(jnp.where(present, edge, 0.0).astype(BF16))
    own = (iota((16, 32), 0) < 4) == (iota((16, 32), 1) < 16)
    for side in (0, 1):
        r16, l16 = iota((16, BLOCK), 0), iota((16, BLOCK), 1)
        pos = l16 if side == 0 else BLOCK - 1 - l16
        pick = jnp.where((pos < 3) & ((r16 == pos) | (r16 == 4 + pos)), 1.0, 0.0).astype(BF16)
        picked = jnp.where(own, dot_t(pick, edges[side]), 0.0)
        sc["edge"][:, 32 * side : 32 * side + 32] = picked
    sc["weigh"][GRAMS:ROWS, :] = sc["edge"][...].astype(BF16)

    for i in range(4):
        sc["local"][i : i + 1, :] = sc["words"][i, pl.ds(here, 1), :].astype(F32)
    sc["local"][4:128, :] = jnp.zeros((124, BLOCK), F32)
    local = sc["local"][...].T.astype(jnp.int32)
    for d in range(2):
        tail = sc["table"][d, GRAMS:ROWS, E:CH].astype(F32)
        tail = jnp.concatenate([tail, jnp.zeros((112, CH - E), F32)], axis=0).T
        sc["b_columns"][d, :, GRAMS:ROWS] = tail[:, 0 : ROWS - GRAMS].astype(BF16)

    for d in range(2):
        scans = [sd for sd in range(4) if SET[sd] == d]
        hits = []
        for sd in scans:
            part = slice(0, 16) if RISING[sd] else slice(BLOCK - 16, BLOCK)
            hits.append(jnp.where(iota((16, ROWS), 1) == local[part, sd : sd + 1], 1.0, 0.0))
        rows = dot(jnp.concatenate(hits, axis=0).astype(BF16), sc["table"][d]).astype(BF16)
        for i, sd in enumerate(scans):
            part = slice(0, 16) if RISING[sd] else slice(BLOCK - 16, BLOCK)
            sc["conved"][sd, part, :] = rows[16 * i : 16 * i + 16]

    for sd in range(4):
        d = SET[sd]
        tail = sc["conved"][sd, :, E:CH]
        b_rows = tail[:, :64]
        c_rows = pltpu.roll(tail.astype(F32), 64, axis=1)[:, :64].astype(BF16)
        sc["scores"][sd] = dot_t(c_rows, b_rows).astype(BF16)
        place = jnp.where(iota((64, E), 0) == 16 * sd + iota((64, E), 1) // 64, 1.0, 0.0).astype(BF16)
        weights = dot(sc["weigh"][...], place)
        weighted = weights.astype(BF16) * sc["table"][d, :, 0:E]
        state = dot(sc["b_columns"][d, 0:64, :], weighted).astype(BF16)
        sc["carried"][sd] = dot(c_rows, state)

    left = iota((BLOCK, 128), 1) < 64
    half = BLOCK // 2
    scales = []
    for sd in range(4):
        d, rising = SET[sd], RISING[sd]
        square = jnp.zeros((BLOCK, 128), F32)
        for pair in range(8):
            cols = slice(128 * pair, 128 * pair + 128)
            values = sc["conved"][sd, :, cols]
            parts = []
            for sub in range(2):
                h = 16 * sd + 2 * pair + sub
                skip = sc["skip_eye"][16 * d + 2 * pair + sub]
                rows_of = []
                for top in (True, False):
                    ts = slice(0, half) if top else slice(half, BLOCK)
                    mixing = sc["decay"][h, ts, ts] * sc["scores"][sd, ts, ts] + skip
                    if top == rising:
                        rows_of.append(dot(mixing, values[ts]))
                    else:
                        ss = slice(half, BLOCK) if top else slice(0, half)
                        far = sc["decay"][h, ts, ss] * sc["scores"][sd, ts, ss]
                        whole = [mixing, far] if top else [far, mixing]
                        rows_of.append(dot(jnp.concatenate(whole, axis=1), values))
                parts.append(jnp.concatenate(rows_of, axis=0))
            both = jnp.where(left, parts[0], parts[1]) + sc["carried"][sd, :, cols] * sc["grow"][sd, :, cols]
            gated = both * sc["gate"][STRAND[sd], :, cols]
            square = square + gated * gated
            sc["gated"][sd, :, cols] = gated
        mean = jnp.sum(square, axis=1, keepdims=True) * (1.0 / E)
        scales.append(lax.rsqrt(mean + EPS))
        between_scans(sd)
    for pair in range(8):
        cols = slice(128 * pair, 128 * pair + 128)
        ones, twos = [sc["gated"][0, :, cols] * scales[0], sc["gated"][3, :, cols] * scales[3]], [
            sc["gated"][1, :, cols] * scales[1],
            sc["gated"][2, :, cols] * scales[2],
        ]
        mixed = (ones[0] + ones[1]) * ng_ref[0:1, cols] + (twos[0] + twos[1]) * ng_ref[1:2, cols]
        sc["mixed"][:, cols] = mixed.astype(BF16)
    return sc["mixed"][...]


def scratch(blocks):
    return {
        "gate_parts": pltpu.VMEM((32, E), BF16),
        "conv_in": pltpu.VMEM((16, CH), F32),
        "coef": pltpu.VMEM((128, 128), F32),
        "skip_rows": pltpu.VMEM((8, E), F32),
        "words": pltpu.VMEM((4, blocks, BLOCK), jnp.int32),
        "s01": pltpu.VMEM((16, CH), F32),
        "s23": pltpu.VMEM((16, CH), F32),
        "table": pltpu.VMEM((2, ROWS, CH), BF16),
        "weigh": pltpu.VMEM((ROWS, 64), BF16),
        "edge": pltpu.VMEM((16, 64), F32),
        "tokens": pltpu.VMEM((blocks, BLOCK), jnp.int32),
        "run": pltpu.VMEM((128, BLOCK), F32),
        "from": pltpu.VMEM((64, BLOCK), F32),
        "local": pltpu.VMEM((128, BLOCK), F32),
        "gate": pltpu.VMEM((2, BLOCK, E), F32),
        "conved": pltpu.VMEM((4, BLOCK, CH), BF16),
        "scores": pltpu.VMEM((4, BLOCK, BLOCK), BF16),
        "swap": pltpu.VMEM((GRAMS, GRAMS), BF16),
        "skip_eye": pltpu.VMEM((32, 128, 128), BF16),
        "factor": pltpu.VMEM((2, 4, 96, 48), BF16),
        "counts": pltpu.VMEM((3, 4 * blocks, BLOCK), BF16),
        "fourfold": pltpu.VMEM((4 * blocks, BLOCK), jnp.int32),
        "run_t": pltpu.VMEM((BLOCK, 128), F32),
        "b_columns": pltpu.VMEM((2, 128, ROWS), BF16),
        "decay": pltpu.VMEM((64, BLOCK, BLOCK), BF16),
        "grow": pltpu.VMEM((4, BLOCK, E), F32),
        "carried": pltpu.VMEM((4, BLOCK, E), F32),
        "gated": pltpu.VMEM((4, BLOCK, E), F32),
        "mixed": pltpu.VMEM((BLOCK, E), BF16),
    }


MESH = pl.DeviceIdType.MESH
PARAMS = 10


def kernel(names, *refs):
    params, shard = refs[:PARAMS], refs[PARAMS]
    tok, out = refs[PARAMS + 1], refs[PARAMS + 2]
    sc = dict(zip(names, refs[PARAMS + 3 :]))
    batch, here = lax.axis_index("batch"), lax.axis_index("seq")
    z_low, core = lax.div(batch, 2), lax.rem(batch, 2)
    y, z_high, x = lax.div(here, 8), lax.rem(lax.div(here, 4), 2), lax.rem(here, 4)
    z = z_high * 4 + z_low
    received, wall = sc["received"], sc["wall"]
    partner = (z_low * 2 + 1 - core, here)
    barrier = pltpu.get_barrier_semaphore()

    def greet(device):
        pl.semaphore_signal(barrier, inc=1, device_id=device, device_id_type=MESH)

    def at(xx, yy, zz):
        return (lax.rem(zz, 4) * 2 + core, yy * 8 + lax.div(zz, 4) * 4 + xx)

    def loop(first, last, act):
        def go(k, carry):
            act(k)
            return carry

        lax.fori_loop(first, last, go, 0)

    loop(1, 8, lambda k: greet(at(x, y, lax.rem(z + k, 8))))
    loop(1, 16, lambda k: greet((batch, lax.div(lax.rem(4 * y + x + k, 16), 4) * 8 + 4 * z_high + lax.rem(x + k, 4))))
    greet(partner)

    def copy_of(piece, send, recv, device):
        return pltpu.make_async_remote_copy(piece, piece, send, recv, device, MESH)

    def token_z(owner):
        piece = received.at[y, x, owner]
        return copy_of(piece, sc["token_send"].at[0], sc["token_recv"].at[16], at(x, y, lax.rem(z + 4, 8)))

    def plane_peer(k):
        return lax.rem(4 * y + x + k, 16)

    def token_plane(k, owner):
        device = at(lax.rem(plane_peer(k), 4), lax.div(plane_peer(k), 4), z)
        piece = received.at[lax.div(owner, 4), lax.rem(owner, 4)]
        return copy_of(piece, sc["token_send"].at[k], sc["token_recv"].at[owner], device)

    mine, inner, outer = [y * 4 + x, x * 4 + y], [x, y], [y, x]

    def z_copy(c, k, owner):
        piece = wall.at[core, c, mine[c], owner]
        return copy_of(piece, sc["z_send"].at[c, k], sc["z_recv"].at[c, owner], at(x, y, lax.rem(z + k, 8)))

    def along(c, k, first):
        step_x, step_y = at(lax.rem(x + k, 4), y, z), at(x, lax.rem(y + k, 4), z)
        return step_x if (c == 0) == first else step_y

    def second_copy(c, k, owner):
        piece = wall.at[core, c, 4 * outer[c] + owner]
        return copy_of(piece, sc["second_send"].at[c, k], sc["second_recv"].at[c, owner], along(c, k, True))

    def third_copy(c, k, owner):
        piece = wall.at[core, c, pl.ds(4 * owner, 4)]
        return copy_of(piece, sc["third_send"].at[c, k], sc["third_recv"].at[c, owner], along(c, k, False))

    def core_copy(side, c, owner):
        piece = wall.at[side, c, pl.ds(4 * owner, 4)]
        return copy_of(piece, sc["core_send"].at[c, owner], sc["core_recv"].at[c, owner], partner)

    first = [pltpu.make_async_copy(tok, received.at[y, x, z_high], sc["own_sem"].at[0])]
    for c in range(2):
        half = shard.at[16 * c : 16 * c + 16]
        first.append(pltpu.make_async_copy(half, wall.at[core, c, mine[c], z], sc["own_sem"].at[1 + c]))
    fetch, held = [], []
    for i, ref in enumerate(params):
        held.append(sc[f"held{i}"])
        fetch.append(pltpu.make_async_copy(ref, held[i], sc["own_sem"].at[3 + i]))
    for copy in first + fetch:
        copy.start()
    for copy in first:
        copy.wait()

    def send():
        pl.semaphore_wait(barrier, 23)
        token_z(z_high).start()
        for c in range(2):
            loop(1, 8, lambda k: z_copy(c, k, z).start())

    last = z_high == 1

    pl.when(last)(send)
    for copy in fetch:
        copy.wait()
    comp_ref, emb, inw, stw, cw, cb, sb, dr, sg, ng = held
    comp = [comp_ref[v] for v in range(4)]
    letter_tables(
        comp, emb, inw, stw, (sb, dr, sg), sc["gate_parts"], sc["conv_in"], sc["coef"], sc["skip_rows"]
    )
    gram_tables(sc["conv_in"], cw, cb, sc["s01"], sc["s23"], sc["table"])
    pl.when(z_high == 0)(send)
    local_counts(received[y, x, z_high], sc)
    local_conv(received[y, x, z_high], comp, sc)
    for sd in range(4):
        local_decays(sd, sc)

    token_z(1 - z_high).wait_recv()
    loop(1, 16, lambda k: token_plane(k, 4 * y + x).start())
    for c in range(2):
        loop(1, 8, lambda k: z_copy(c, k, lax.rem(z + k, 8)).wait_recv())
        loop(1, 4, lambda k: second_copy(c, k, inner[c]).start())
    for c in range(2):
        loop(1, 4, lambda k: second_copy(c, k, lax.rem(inner[c] + k, 4)).wait_recv())
        loop(1, 4, lambda k: third_copy(c, k, outer[c]).start())
        core_copy(core, c, outer[c]).start()
    loop(1, 16, lambda k: token_plane(k, plane_peer(k)).wait_recv())
    for j in range(32):
        line = received[j // 8, j % 4, (j // 4) % 2]
        sc["tokens"][j : j + 1, :] = line
        sc["fourfold"][4 * j : 4 * j + 4, :] = jnp.broadcast_to(line, (4, BLOCK))

    def pass_on_third(sd):
        if sd < 2:
            for k in (1, 3) if sd == 0 else (2,):
                for c in range(2):
                    owner = lax.rem(outer[c] + k, 4)
                    third_copy(c, k, owner).wait_recv()
                    core_copy(core, c, owner).start()

    mixed = mixer(here, comp, sc["tokens"][...], cw, cb, ng, sc, pass_on_third)
    for c in range(2):
        loop(0, 4, lambda q: core_copy(1 - core, c, q).wait_recv())
    order = []
    for s in range(32):
        yy, zz, xx = s // 8, 4 * ((s // 4) % 2), s % 4
        order += [(0, 4 * yy + xx, zz), (1, 4 * xx + yy, zz)]
    for low in range(4):
        sides = [jnp.concatenate([wall[k, c, p, zz + low] for c, p, zz in order], axis=0) for k in range(2)]
        out[:, 256 * low : 256 * low + 256] = dot(mixed, jnp.concatenate(sides, axis=1)).astype(BF16)

    for c in range(2):
        loop(1, 8, lambda k: z_copy(c, k, z).wait_send())
        loop(1, 4, lambda k: second_copy(c, k, inner[c]).wait_send())
        loop(1, 4, lambda k: third_copy(c, k, outer[c]).wait_send())
        loop(0, 4, lambda q: core_copy(core, c, q).wait_send())
    token_z(z_high).wait_send()
    loop(1, 16, lambda k: token_plane(k, 4 * y + x).wait_send())


def on_device(tok, comp, emb, inw, stw, cw, cb, sb, dr, sg, ng, wout):
    params = [comp, emb, inw, stw.T, cw, cb, sb, dr, sg, ng]
    shapes = scratch(32)
    shapes["received"] = pltpu.VMEM((4, 4, 2, 1, BLOCK), jnp.int32)
    shapes["wall"] = pltpu.VMEM((2, 2, 16, 8, 16, 128), BF16)
    shapes["own_sem"] = pltpu.SemaphoreType.DMA((3 + PARAMS,))
    for name, count in (("token", (17,)), ("z", (2, 8)), ("second", (2, 4)), ("third", (2, 4)), ("core", (2, 4))):
        shapes[name + "_send"] = pltpu.SemaphoreType.DMA(count)
        shapes[name + "_recv"] = pltpu.SemaphoreType.DMA(count)
    for i, value in enumerate(params):
        space = pltpu.SMEM if value.ndim == 1 else pltpu.VMEM
        shapes[f"held{i}"] = space(value.shape, value.dtype)
    anywhere = pl.BlockSpec(memory_space=pl.ANY)
    out = pl.pallas_call(
        partial(kernel, tuple(shapes)),
        out_shape=jax.ShapeDtypeStruct((BLOCK, D), BF16),
        in_specs=[anywhere] * (PARAMS + 2),
        out_specs=pl.BlockSpec(memory_space=pltpu.VMEM),
        scratch_shapes=list(shapes.values()),
        compiler_params=pltpu.CompilerParams(
            collective_id=0, has_side_effects=True, vmem_limit_bytes=60 << 20
        ),
    )(*params, wout, tok)
    return out[None]


def solution(mesh):
    placed = (P("batch", "seq"),) + (P(),) * 10 + (P("seq", "batch"),)
    return jax.shard_map(
        on_device, mesh=mesh, in_specs=placed, out_specs=P("batch", "seq", None), check_vma=False
    )
```

```python
from functools import partial

import jax
import jax.numpy as jnp
from jax import lax
from jax.experimental import pallas as pl
from jax.experimental.pallas import tpu as pltpu
from jax.sharding import PartitionSpec as P

D = 1024
E = 1024
H = 16
N = 64
CH = 1152
BLOCK = 256
GRAMS = 256
ROWS = 272
LOG2E = 1.4426950408889634
EPS = 1e-05
F32 = jnp.float32
BF16 = jnp.bfloat16
HIGH = lax.Precision.HIGHEST
STRAND = (0, 1, 0, 1)
SET = (0, 1, 1, 0)
RISING = (True, True, False, False)


def iota(shape, dim):
    return lax.broadcasted_iota(jnp.int32, shape, dim)


def silu(x):
    return x * jax.nn.sigmoid(x)


def dot(a, b, **kw):
    return jnp.dot(a, b, preferred_element_type=F32, **kw)


def dot_t(a, b):
    return lax.dot_general(a, b, (((1,), (1,)), ((), ())), preferred_element_type=F32)


def letter_tables(comp, emb_ref, inw_ref, stw_ref, small_refs, gate_parts, conv_in, coef, skip_rows):
    row = iota((16, 1), 0)
    letter = jnp.where(row < 4, row, 4)
    for v in range(4):
        letter = jnp.where(row == 8 + v, comp[v], letter)
    emb = emb_ref[...].astype(F32)
    rows = jnp.zeros((16, D), F32)
    for x in range(4):
        rows = jnp.where(letter == x, emb[x : x + 1], rows)
    rows = rows.astype(BF16)
    projected = dot(rows, inw_ref[...]).astype(BF16).astype(F32)
    gate = silu(projected[:, :E])
    hi = gate.astype(BF16)
    gate_parts[0:16, :] = hi
    gate_parts[16:32, :] = (gate - hi.astype(F32)).astype(BF16)
    conv_in[...] = projected[:, E:]

    step_raw = dot_t(rows, stw_ref[...])
    lane = iota((16, 128), 1)
    spread = jnp.where((lane % 16 == iota((16, 128), 0)) & (lane < 64), 1.0, 0.0)
    step_raw = dot(step_raw, spread, precision=HIGH)
    bias_ref, rate_ref, gain_ref = small_refs
    row8 = iota((8, H), 0)
    packed = jnp.zeros((8, H), F32)
    for at, ref in ((0, bias_ref), (2, rate_ref), (4, gain_ref)):
        for d in range(2):
            packed = jnp.where(row8 == at + d, ref[d : d + 1, :], packed)
    spread_small = dot(packed, spread, precision=HIGH)
    sd = iota((1, 128), 1) // 16
    second_set = (sd == 1) | (sd == 2)
    other = sd % 2 == 1
    bias = jnp.where(second_set, spread_small[1:2], spread_small[0:1])
    rate = jnp.where(second_set, spread_small[3:4], spread_small[2:3])
    x = jnp.where(other, step_raw[8:16], step_raw[0:8]) + bias
    step = jnp.maximum(x, 0.0) + jnp.log1p(jnp.exp(-jnp.abs(x)))
    coef[...] = jnp.zeros_like(coef)
    coef[0:8, :] = -rate * step * LOG2E
    coef[8:16, :] = jnp.maximum(jnp.log(step) * LOG2E, -1e30)
    wide = jnp.where(iota((H, E), 1) // 64 == iota((H, E), 0), 1.0, 0.0)
    skip_rows[...] = dot(packed, wide, precision=HIGH)


def gram_tables(conv_in, cw_ref, cb_ref, s01, s23, table):
    letters = conv_in[0:8, :]
    for d in range(2):
        taps = [cw_ref[d, k : k + 1, :] * letters for k in range(4)]
        bias = cb_ref[d : d + 1, :]
        for x in range(4):
            s01[4 * x : 4 * x + 4, :] = bias + taps[0][x : x + 1] + taps[1][0:4]
            s23[4 * x : 4 * x + 4, :] = taps[2][x : x + 1] + taps[3][0:4]
        low = s23[...]
        for i in range(16):
            table[d, 16 * i : 16 * i + 16, :] = silu(s01[i : i + 1, :] + low).astype(BF16)


def edge_tables(edge_letters, conv_in, cw_ref, cb_ref, table):
    letters = conv_in[0:8, :]
    for d in range(2):
        taps = [cw_ref[d, k : k + 1, :] * letters for k in range(4)]
        bias = cb_ref[d : d + 1, :]
        total = jnp.broadcast_to(bias, (16, CH))
        for k in (1, 2, 3):
            for x in range(4):
                total = total + jnp.where(edge_letters[d][k] == x, taps[k][x : x + 1], 0.0)
        total = jnp.where(iota((16, 1), 0) < 8, silu(total), 0.0)
        table[d, GRAMS:ROWS, :] = total.astype(BF16)


def shifted(tokens, amount):
    lane = iota(tokens.shape, 1)
    moved = pltpu.roll(tokens, amount % BLOCK, axis=1)
    if amount > 0:
        return jnp.where(lane < amount, pltpu.roll(moved, 1, axis=0), moved)
    return jnp.where(lane >= BLOCK + amount, pltpu.roll(moved, tokens.shape[0] - 1, axis=0), moved)


def local_counts(mine, sc):
    hot = jnp.concatenate([jnp.where(mine == v, 1.0, 0.0) for v in range(4)] + [jnp.zeros((4, BLOCK), F32)], axis=0)
    upper = jnp.where(iota((BLOCK, BLOCK), 0) <= iota((BLOCK, BLOCK), 1), 1.0, 0.0)
    count = dot(hot.astype(BF16), upper.astype(BF16))
    coef = sc["coef"][...].T
    sc["run"][...] = jnp.zeros_like(sc["run"])
    for side in (0, 1):
        part = slice(32 * side, 32 * side + 32)
        power = jnp.zeros((32, BLOCK), F32)
        size = jnp.zeros((32, BLOCK), F32)
        for v in range(4):
            passed = count[v : v + 1]
            if side == 1:
                passed = passed[:, BLOCK - 1 : BLOCK] - passed + hot[v : v + 1]
            power = power + coef[part, v : v + 1] * passed
            size = size + coef[part, 8 + v : 9 + v] * hot[v : v + 1]
        sc["run"][part, :] = power
        sc["from"][part, :] = power - size
        k = iota((32, 48), 1)
        factor = jnp.zeros((32, 48), F32)
        for v in range(4):
            decay, size = coef[part, v : v + 1], coef[part, 8 + v : 9 + v]
            value = jnp.where(k < 16, 64.0 * decay, jnp.where(k < 32, decay, size))
            factor = jnp.where(k % 4 == v, value, factor)
        pieces = []
        for _ in range(3):
            pieces.append(factor.astype(BF16).astype(F32))
            factor = factor - pieces[-1]
        pieces = jnp.concatenate(pieces, axis=0)
        block = (iota((96, 48), 1) // 4) % 4
        for at in range(4):
            sc["factor"][side, at] = jnp.where(block == at, pieces, 0.0).astype(BF16)
    sc["run_t"][...] = sc["run"][...].T
    letter = jnp.broadcast_to(mine.astype(F32), (128, BLOCK)).T.astype(jnp.int32)[:, 0:32]
    for strand in range(2):
        hit = jnp.where(iota((BLOCK, 32), 1) % 16 == letter + 8 * strand, 1.0, 0.0).astype(BF16)
        sc["gate"][strand] = dot(hit, sc["gate_parts"][...])
    eye = iota((128, 128), 0) == iota((128, 128), 1)
    for d in range(2):
        for h in range(H):
            gain = sc["skip_rows"][4 + d : 5 + d, 64 * h : 64 * h + 1]
            sc["skip_eye"][16 * d + h] = jnp.where(eye, gain, 0.0).astype(BF16)
        sc["b_columns"][d, :, 0:GRAMS] = sc["table"][d, 0:GRAMS, E:CH].astype(F32).T.astype(BF16)


def local_conv(mine, comp, sc):
    others = jnp.zeros_like(mine)
    for v in range(4):
        others = jnp.where(mine == v, comp[v], others)
    lane = iota(mine.shape, 1)
    words = []
    for sd in range(4):
        letters = others if STRAND[sd] else mine
        word = letters
        for k in (1, 2, 3):
            word = word + 4**k * pltpu.roll(letters, k if RISING[sd] else BLOCK - k, axis=1)
        inside = lane >= 3 if RISING[sd] else lane < BLOCK - 3
        words.append(jnp.where(inside, word, -1).astype(F32))
    words = jnp.concatenate(words + [jnp.zeros((124, BLOCK), F32)], axis=0).T.astype(jnp.int32)
    for sd in range(4):
        hit = jnp.where(iota((BLOCK, GRAMS), 1) == words[:, sd : sd + 1], 1.0, 0.0).astype(BF16)
        sc["conved"][sd] = dot(hit, sc["table"][SET[sd], 0:GRAMS]).astype(BF16)
    other_word = jnp.zeros((1, GRAMS), jnp.int32)
    for place in (64, 16, 4, 1):
        digit = (iota((1, GRAMS), 1) // place) % 4
        for v in range(4):
            other_word = other_word + jnp.where(digit == v, comp[v] * place, 0)
    sc["swap"][...] = jnp.where(iota((GRAMS, GRAMS), 0) == other_word, 1.0, 0.0).astype(BF16)


def local_decays(sd, sc):
    left = iota((BLOCK, 128), 1) < 64
    half = BLOCK // 2
    rising = RISING[sd]
    t_at, s_at = iota((half, half), 0), iota((half, half), 1)
    reach = s_at <= t_at if rising else s_at >= t_at
    for pair in range(8):
        reached = []
        for sub in range(2):
            h = 16 * sd + 2 * pair + sub
            to = jnp.broadcast_to(sc["run_t"][:, h : h + 1], (BLOCK, 128))
            reached.append(to)
            source = sc["from"][h : h + 1, :]
            for top in (0, 1):
                for side in (0, 1):
                    ts, ss = slice(half * top, half * top + half), slice(half * side, half * side + half)
                    if top == side:
                        decay = jnp.where(reach, jnp.exp2(to[ts] - source[:, ss]), 0.0)
                    elif (side < top) == rising:
                        decay = jnp.exp2(to[ts] - source[:, ss])
                    else:
                        continue
                    sc["decay"][h, ts, ss] = decay.astype(BF16)
        sc["grow"][sd, :, 128 * pair : 128 * pair + 128] = jnp.exp2(jnp.where(left, reached[0], reached[1]))


def mixer(here, comp, tokens, cw_ref, cb_ref, ng_ref, sc, between_scans):
    blocks = tokens.shape[0]
    others = jnp.zeros_like(tokens)
    for v in range(4):
        others = jnp.where(tokens == v, comp[v], others)

    block_at, lane_at = iota(tokens.shape, 0), iota(tokens.shape, 1)
    low_edge = (block_at == 0) & (lane_at < 3)
    high_edge = (block_at == blocks - 1) & (lane_at >= BLOCK - 3)
    for strand, letters in ((0, tokens), (1, others)):
        rise = 64 * shifted(letters, 3) + 16 * shifted(letters, 2) + 4 * shifted(letters, 1) + letters
        fall = 64 * shifted(letters, -3) + 16 * shifted(letters, -2) + 4 * shifted(letters, -1) + letters
        sc["words"][strand] = jnp.where(low_edge, GRAMS + 4 * strand + lane_at, rise)
        sc["words"][2 + strand] = jnp.where(high_edge, GRAMS + 4 * strand + BLOCK - 1 - lane_at, fall)

    edge_letters = []
    row = iota((16, 1), 0)

    def letter_of(source, block, lane):
        line = source[block : block + 1, :]
        return jnp.sum(jnp.where(iota(line.shape, 1) == lane, line, 0), axis=1, keepdims=True)

    low = [[letter_of(s, 0, j) for j in range(3)] for s in (tokens, others)]
    high = [[letter_of(s, blocks - 1, BLOCK - 1 - j) for j in range(3)] for s in (tokens, others)]
    for d in range(2):
        first, second = (low[0], high[1]) if d == 0 else (high[0], low[1])
        columns = {}
        for k in (1, 2, 3):
            column = jnp.full((16, 1), 4, jnp.int32)
            for strand, letters in ((0, first), (1, second)):
                for j in range(3):
                    at = j - (3 - k)
                    if at >= 0:
                        column = jnp.where(row == 4 * strand + j, letters[at], column)
            columns[k] = column
        edge_letters.append(columns)
    edge_tables(edge_letters, sc["conv_in"], cw_ref, cb_ref, sc["table"])

    rows = 4 * blocks
    one_hot = jnp.where(sc["fourfold"][...] == iota((rows, BLOCK), 0) % 4, 1.0, 0.0)
    upper = jnp.where(iota((BLOCK, BLOCK), 0) <= iota((BLOCK, BLOCK), 1), 1.0, 0.0)
    inside = dot(one_hot.astype(BF16), upper.astype(BF16))
    total = inside[:, BLOCK - 1 : BLOCK]
    a, b = iota((rows, rows), 0), iota((rows, rows), 1)
    aj, bj = a // 4, b // 4
    between = (a % 4 == b % 4) & (((aj < bj) & (bj < here)) | ((here < bj) & (bj < aj)))
    passed = dot(jnp.where(between, 1.0, 0.0).astype(BF16), jnp.broadcast_to(total, inside.shape).astype(BF16))
    before = iota((rows, 1), 0) // 4 < here
    away = passed + jnp.where(before, total - inside, inside - one_hot)
    high = jnp.floor(away * (1.0 / 64.0))
    sc["counts"][0] = high.astype(BF16)
    sc["counts"][1] = (away - 64.0 * high).astype(BF16)
    sc["counts"][2] = one_hot.astype(BF16)

    def entry_weights(four, at, side):
        start = 16 * four if isinstance(four, int) else pl.multiple_of(16 * four, 16)
        counts = jnp.concatenate([sc["counts"][i, pl.ds(start, 16), :] for i in range(3)], axis=0)
        power = dot(sc["factor"][side, at], counts)
        return jnp.exp2(power[0:32] + power[32:64] + power[64:96])

    word_of_row = iota((GRAMS, BLOCK), 0).astype(F32).astype(BF16)
    group = 8

    def entering(step, acc):
        hits, powers = [], []
        for i in range(group):
            j = step * group + i
            side = jnp.where(j < here, 0, 1)
            words = sc["words"][2 * side, pl.ds(j, 1), :].astype(F32).astype(BF16)
            hits.append(jnp.where(word_of_row == words, jnp.ones((), BF16), jnp.zeros((), BF16)))
            power = entry_weights(step * (group // 4) + i // 4, i % 4, side)
            both = [jnp.where(j < here, power, 0.0), jnp.where(j > here, power, 0.0)]
            powers.append(jnp.concatenate(both, axis=0).astype(BF16))
        return acc + dot_t(jnp.concatenate(hits, axis=1), jnp.concatenate(powers, axis=1))

    acc = lax.fori_loop(0, blocks // group, entering, jnp.zeros((GRAMS, 64), F32)).astype(BF16)
    swapped = dot(sc["swap"][...], acc)
    lane64 = iota((GRAMS, 64), 1)
    sc["weigh"][0:GRAMS, :] = jnp.where(lane64 % 32 < 16, acc.astype(F32), swapped).astype(BF16)
    edges = []
    for side in (0, 1):
        present = here > 0 if side == 0 else here < blocks - 1
        edge = entry_weights(0, 0, 0) if side == 0 else entry_weights(blocks // 4 - 1, 3, 1)
        edges.append(jnp.where(present, edge, 0.0).astype(BF16))
    own = (iota((16, 32), 0) < 4) == (iota((16, 32), 1) < 16)
    for side in (0, 1):
        r16, l16 = iota((16, BLOCK), 0), iota((16, BLOCK), 1)
        pos = l16 if side == 0 else BLOCK - 1 - l16
        pick = jnp.where((pos < 3) & ((r16 == pos) | (r16 == 4 + pos)), 1.0, 0.0).astype(BF16)
        picked = jnp.where(own, dot_t(pick, edges[side]), 0.0)
        sc["edge"][:, 32 * side : 32 * side + 32] = picked
    sc["weigh"][GRAMS:ROWS, :] = sc["edge"][...].astype(BF16)

    for i in range(4):
        sc["local"][i : i + 1, :] = sc["words"][i, pl.ds(here, 1), :].astype(F32)
    sc["local"][4:128, :] = jnp.zeros((124, BLOCK), F32)
    local = sc["local"][...].T.astype(jnp.int32)
    for d in range(2):
        tail = sc["table"][d, GRAMS:ROWS, E:CH].astype(F32)
        tail = jnp.concatenate([tail, jnp.zeros((112, CH - E), F32)], axis=0).T
        sc["b_columns"][d, :, GRAMS:ROWS] = tail[:, 0 : ROWS - GRAMS].astype(BF16)

    for d in range(2):
        scans = [sd for sd in range(4) if SET[sd] == d]
        hits = []
        for sd in scans:
            part = slice(0, 16) if RISING[sd] else slice(BLOCK - 16, BLOCK)
            hits.append(jnp.where(iota((16, ROWS), 1) == local[part, sd : sd + 1], 1.0, 0.0))
        rows = dot(jnp.concatenate(hits, axis=0).astype(BF16), sc["table"][d]).astype(BF16)
        for i, sd in enumerate(scans):
            part = slice(0, 16) if RISING[sd] else slice(BLOCK - 16, BLOCK)
            sc["conved"][sd, part, :] = rows[16 * i : 16 * i + 16]

    for sd in range(4):
        d = SET[sd]
        tail = sc["conved"][sd, :, E:CH]
        b_rows = tail[:, :64]
        c_rows = pltpu.roll(tail.astype(F32), 64, axis=1)[:, :64].astype(BF16)
        sc["scores"][sd] = dot_t(c_rows, b_rows).astype(BF16)
        place = jnp.where(iota((64, E), 0) == 16 * sd + iota((64, E), 1) // 64, 1.0, 0.0).astype(BF16)
        weights = dot(sc["weigh"][...], place)
        weighted = weights.astype(BF16) * sc["table"][d, :, 0:E]
        state = dot(sc["b_columns"][d, 0:64, :], weighted).astype(BF16)
        sc["carried"][sd] = dot(c_rows, state)

    left = iota((BLOCK, 128), 1) < 64
    half = BLOCK // 2
    scales = []
    for sd in range(4):
        d, rising = SET[sd], RISING[sd]
        square = jnp.zeros((BLOCK, 128), F32)
        for pair in range(8):
            cols = slice(128 * pair, 128 * pair + 128)
            values = sc["conved"][sd, :, cols]
            parts = []
            for sub in range(2):
                h = 16 * sd + 2 * pair + sub
                skip = sc["skip_eye"][16 * d + 2 * pair + sub]
                rows_of = []
                for top in (True, False):
                    ts = slice(0, half) if top else slice(half, BLOCK)
                    mixing = sc["decay"][h, ts, ts] * sc["scores"][sd, ts, ts] + skip
                    if top == rising:
                        rows_of.append(dot(mixing, values[ts]))
                    else:
                        ss = slice(half, BLOCK) if top else slice(0, half)
                        far = sc["decay"][h, ts, ss] * sc["scores"][sd, ts, ss]
                        whole = [mixing, far] if top else [far, mixing]
                        rows_of.append(dot(jnp.concatenate(whole, axis=1), values))
                parts.append(jnp.concatenate(rows_of, axis=0))
            both = jnp.where(left, parts[0], parts[1]) + sc["carried"][sd, :, cols] * sc["grow"][sd, :, cols]
            gated = both * sc["gate"][STRAND[sd], :, cols]
            square = square + gated * gated
            sc["gated"][sd, :, cols] = gated
        mean = jnp.sum(square, axis=1, keepdims=True) * (1.0 / E)
        scales.append(lax.rsqrt(mean + EPS))
        between_scans(sd)
    for pair in range(8):
        cols = slice(128 * pair, 128 * pair + 128)
        ones, twos = [sc["gated"][0, :, cols] * scales[0], sc["gated"][3, :, cols] * scales[3]], [
            sc["gated"][1, :, cols] * scales[1],
            sc["gated"][2, :, cols] * scales[2],
        ]
        mixed = (ones[0] + ones[1]) * ng_ref[0:1, cols] + (twos[0] + twos[1]) * ng_ref[1:2, cols]
        sc["mixed"][:, cols] = mixed.astype(BF16)
    return sc["mixed"][...]


def scratch(blocks):
    return {
        "gate_parts": pltpu.VMEM((32, E), BF16),
        "conv_in": pltpu.VMEM((16, CH), F32),
        "coef": pltpu.VMEM((128, 128), F32),
        "skip_rows": pltpu.VMEM((8, E), F32),
        "words": pltpu.VMEM((4, blocks, BLOCK), jnp.int32),
        "s01": pltpu.VMEM((16, CH), F32),
        "s23": pltpu.VMEM((16, CH), F32),
        "table": pltpu.VMEM((2, ROWS, CH), BF16),
        "weigh": pltpu.VMEM((ROWS, 64), BF16),
        "edge": pltpu.VMEM((16, 64), F32),
        "tokens": pltpu.VMEM((blocks, BLOCK), jnp.int32),
        "run": pltpu.VMEM((128, BLOCK), F32),
        "from": pltpu.VMEM((64, BLOCK), F32),
        "local": pltpu.VMEM((128, BLOCK), F32),
        "gate": pltpu.VMEM((2, BLOCK, E), F32),
        "conved": pltpu.VMEM((4, BLOCK, CH), BF16),
        "scores": pltpu.VMEM((4, BLOCK, BLOCK), BF16),
        "swap": pltpu.VMEM((GRAMS, GRAMS), BF16),
        "skip_eye": pltpu.VMEM((32, 128, 128), BF16),
        "factor": pltpu.VMEM((2, 4, 96, 48), BF16),
        "counts": pltpu.VMEM((3, 4 * blocks, BLOCK), BF16),
        "fourfold": pltpu.VMEM((4 * blocks, BLOCK), jnp.int32),
        "run_t": pltpu.VMEM((BLOCK, 128), F32),
        "b_columns": pltpu.VMEM((2, 128, ROWS), BF16),
        "decay": pltpu.VMEM((64, BLOCK, BLOCK), BF16),
        "grow": pltpu.VMEM((4, BLOCK, E), F32),
        "carried": pltpu.VMEM((4, BLOCK, E), F32),
        "gated": pltpu.VMEM((4, BLOCK, E), F32),
        "mixed": pltpu.VMEM((BLOCK, E), BF16),
    }


MESH = pl.DeviceIdType.MESH
PARAMS = 10


def kernel(names, *refs):
    params, shard = refs[:PARAMS], refs[PARAMS]
    tok, out = refs[PARAMS + 1], refs[PARAMS + 2]
    sc = dict(zip(names, refs[PARAMS + 3 :]))
    batch, here = lax.axis_index("batch"), lax.axis_index("seq")
    z_low, core = lax.div(batch, 2), lax.rem(batch, 2)
    y, z_high, x = lax.div(here, 8), lax.rem(lax.div(here, 4), 2), lax.rem(here, 4)
    z = z_high * 4 + z_low
    received, wall = sc["received"], sc["wall"]
    partner = (z_low * 2 + 1 - core, here)
    barrier = pltpu.get_barrier_semaphore()

    def greet(device):
        pl.semaphore_signal(barrier, inc=1, device_id=device, device_id_type=MESH)

    def at(xx, yy, zz):
        return (lax.rem(zz, 4) * 2 + core, yy * 8 + lax.div(zz, 4) * 4 + xx)

    def loop(first, last, act):
        def go(k, carry):
            act(k)
            return carry

        lax.fori_loop(first, last, go, 0)

    loop(1, 8, lambda k: greet(at(x, y, lax.rem(z + k, 8))))
    loop(1, 16, lambda k: greet((batch, lax.div(lax.rem(4 * y + x + k, 16), 4) * 8 + 4 * z_high + lax.rem(x + k, 4))))
    greet(partner)

    def copy_of(piece, send, recv, device):
        return pltpu.make_async_remote_copy(piece, piece, send, recv, device, MESH)

    def token_z(owner):
        piece = received.at[y, x, owner]
        return copy_of(piece, sc["token_send"].at[0], sc["token_recv"].at[16], at(x, y, lax.rem(z + 4, 8)))

    def plane_peer(k):
        return lax.rem(4 * y + x + k, 16)

    def token_plane(k, owner):
        device = at(lax.rem(plane_peer(k), 4), lax.div(plane_peer(k), 4), z)
        piece = received.at[lax.div(owner, 4), lax.rem(owner, 4)]
        return copy_of(piece, sc["token_send"].at[k], sc["token_recv"].at[owner], device)

    mine, inner, outer = [y * 4 + x, x * 4 + y], [x, y], [y, x]

    def z_copy(c, k, owner):
        piece = wall.at[core, c, mine[c], owner]
        return copy_of(piece, sc["z_send"].at[c, k], sc["z_recv"].at[c, owner], at(x, y, lax.rem(z + k, 8)))

    def along(c, k, first):
        step_x, step_y = at(lax.rem(x + k, 4), y, z), at(x, lax.rem(y + k, 4), z)
        return step_x if (c == 0) == first else step_y

    def second_copy(c, k, owner):
        piece = wall.at[core, c, 4 * outer[c] + owner]
        return copy_of(piece, sc["second_send"].at[c, k], sc["second_recv"].at[c, owner], along(c, k, True))

    def third_copy(c, k, owner):
        piece = wall.at[core, c, pl.ds(4 * owner, 4)]
        return copy_of(piece, sc["third_send"].at[c, k], sc["third_recv"].at[c, owner], along(c, k, False))

    def core_copy(side, c, owner):
        piece = wall.at[side, c, pl.ds(4 * owner, 4)]
        return copy_of(piece, sc["core_send"].at[c, owner], sc["core_recv"].at[c, owner], partner)

    first = [pltpu.make_async_copy(tok, received.at[y, x, z_high], sc["own_sem"].at[0])]
    for c in range(2):
        half = shard.at[16 * c : 16 * c + 16]
        first.append(pltpu.make_async_copy(half, wall.at[core, c, mine[c], z], sc["own_sem"].at[1 + c]))
    fetch, held = [], []
    for i, ref in enumerate(params):
        held.append(sc[f"held{i}"])
        fetch.append(pltpu.make_async_copy(ref, held[i], sc["own_sem"].at[3 + i]))
    for copy in first + fetch:
        copy.start()
    for copy in first:
        copy.wait()

    def send():
        pl.semaphore_wait(barrier, 23)
        token_z(z_high).start()
        for c in range(2):
            loop(1, 8, lambda k: z_copy(c, k, z).start())

    last = z_high == 1

    pl.when(last)(send)
    for copy in fetch:
        copy.wait()
    comp_ref, emb, inw, stw, cw, cb, sb, dr, sg, ng = held
    comp = [comp_ref[v] for v in range(4)]
    letter_tables(
        comp, emb, inw, stw, (sb, dr, sg), sc["gate_parts"], sc["conv_in"], sc["coef"], sc["skip_rows"]
    )
    gram_tables(sc["conv_in"], cw, cb, sc["s01"], sc["s23"], sc["table"])
    pl.when(z_high == 0)(send)
    local_counts(received[y, x, z_high], sc)
    local_conv(received[y, x, z_high], comp, sc)
    for sd in range(4):
        local_decays(sd, sc)

    token_z(1 - z_high).wait_recv()
    loop(1, 16, lambda k: token_plane(k, 4 * y + x).start())
    for c in range(2):
        loop(1, 8, lambda k: z_copy(c, k, lax.rem(z + k, 8)).wait_recv())
        loop(1, 4, lambda k: second_copy(c, k, inner[c]).start())
    for c in range(2):
        loop(1, 4, lambda k: second_copy(c, k, lax.rem(inner[c] + k, 4)).wait_recv())
        loop(1, 4, lambda k: third_copy(c, k, outer[c]).start())
        core_copy(core, c, outer[c]).start()
    loop(1, 16, lambda k: token_plane(k, plane_peer(k)).wait_recv())
    for j in range(32):
        line = received[j // 8, j % 4, (j // 4) % 2]
        sc["tokens"][j : j + 1, :] = line
        sc["fourfold"][4 * j : 4 * j + 4, :] = jnp.broadcast_to(line, (4, BLOCK))

    def pass_on_third(sd):
        if sd < 2:
            for k in (1, 3) if sd == 0 else (2,):
                for c in range(2):
                    owner = lax.rem(outer[c] + k, 4)
                    third_copy(c, k, owner).wait_recv()
                    core_copy(core, c, owner).start()

    mixed = mixer(here, comp, sc["tokens"][...], cw, cb, ng, sc, pass_on_third)
    for c in range(2):
        loop(0, 4, lambda q: core_copy(1 - core, c, q).wait_recv())
    order = []
    for s in range(32):
        yy, zz, xx = s // 8, 4 * ((s // 4) % 2), s % 4
        order += [(0, 4 * yy + xx, zz), (1, 4 * xx + yy, zz)]
    for low in range(4):
        sides = [jnp.concatenate([wall[k, c, p, zz + low] for c, p, zz in order], axis=0) for k in range(2)]
        out[:, 256 * low : 256 * low + 256] = dot(mixed, jnp.concatenate(sides, axis=1)).astype(BF16)

    for c in range(2):
        loop(1, 8, lambda k: z_copy(c, k, z).wait_send())
        loop(1, 4, lambda k: second_copy(c, k, inner[c]).wait_send())
        loop(1, 4, lambda k: third_copy(c, k, outer[c]).wait_send())
        loop(0, 4, lambda q: core_copy(core, c, q).wait_send())
    token_z(z_high).wait_send()
    loop(1, 16, lambda k: token_plane(k, 4 * y + x).wait_send())


def on_device(tok, comp, emb, inw, stw, cw, cb, sb, dr, sg, ng, wout):
    params = [comp, emb, inw, stw.T, cw, cb, sb, dr, sg, ng]
    shapes = scratch(32)
    shapes["received"] = pltpu.VMEM((4, 4, 2, 1, BLOCK), jnp.int32)
    shapes["wall"] = pltpu.VMEM((2, 2, 16, 8, 16, 128), BF16)
    shapes["own_sem"] = pltpu.SemaphoreType.DMA((3 + PARAMS,))
    for name, count in (("token", (17,)), ("z", (2, 8)), ("second", (2, 4)), ("third", (2, 4)), ("core", (2, 4))):
        shapes[name + "_send"] = pltpu.SemaphoreType.DMA(count)
        shapes[name + "_recv"] = pltpu.SemaphoreType.DMA(count)
    for i, value in enumerate(params):
        space = pltpu.SMEM if value.ndim == 1 else pltpu.VMEM
        shapes[f"held{i}"] = space(value.shape, value.dtype)
    anywhere = pl.BlockSpec(memory_space=pl.ANY)
    out = pl.pallas_call(
        partial(kernel, tuple(shapes)),
        out_shape=jax.ShapeDtypeStruct((BLOCK, D), BF16),
        in_specs=[anywhere] * (PARAMS + 2),
        out_specs=pl.BlockSpec(memory_space=pltpu.VMEM),
        scratch_shapes=list(shapes.values()),
        compiler_params=pltpu.CompilerParams(
            collective_id=0, has_side_effects=True, vmem_limit_bytes=44 << 20
        ),
    )(*[pltpu.with_memory_space_constraint(v, pltpu.HBM) for v in (*params, wout, tok)])
    return out[None]


def solution(mesh):
    placed = (P("batch", "seq"),) + (P(),) * 10 + (P("seq", "batch"),)
    return jax.shard_map(
        on_device, mesh=mesh, in_specs=placed, out_specs=P("batch", "seq", None), check_vma=False
    )
```

```python
from functools import partial

import jax
import jax.numpy as jnp
from jax import lax
from jax.experimental import pallas as pl
from jax.experimental.pallas import tpu as pltpu
from jax.sharding import PartitionSpec as P

D = 1024
E = 1024
H = 16
N = 64
CH = 1152
BLOCK = 256
GRAMS = 256
ROWS = 272
LOG2E = 1.4426950408889634
EPS = 1e-05
F32 = jnp.float32
BF16 = jnp.bfloat16
HIGH = lax.Precision.HIGHEST
STRAND = (0, 1, 0, 1)
SET = (0, 1, 1, 0)
RISING = (True, True, False, False)


def iota(shape, dim):
    return lax.broadcasted_iota(jnp.int32, shape, dim)


def silu(x):
    return x * jax.nn.sigmoid(x)


def dot(a, b, **kw):
    return jnp.dot(a, b, preferred_element_type=F32, **kw)


def dot_t(a, b):
    return lax.dot_general(a, b, (((1,), (1,)), ((), ())), preferred_element_type=F32)


def letter_tables(comp, emb_ref, inw_ref, stw_ref, small_refs, gate_parts, conv_in, coef, skip_rows):
    row = iota((16, 1), 0)
    letter = jnp.where(row < 4, row, 4)
    for v in range(4):
        letter = jnp.where(row == 8 + v, comp[v], letter)
    emb = emb_ref[...].astype(F32)
    rows = jnp.zeros((16, D), F32)
    for x in range(4):
        rows = jnp.where(letter == x, emb[x : x + 1], rows)
    rows = rows.astype(BF16)
    projected = dot(rows, inw_ref[...]).astype(BF16).astype(F32)
    gate = silu(projected[:, :E])
    hi = gate.astype(BF16)
    gate_parts[0:16, :] = hi
    gate_parts[16:32, :] = (gate - hi.astype(F32)).astype(BF16)
    conv_in[...] = projected[:, E:]

    step_raw = dot_t(rows, stw_ref[...])
    lane = iota((16, 128), 1)
    spread = jnp.where((lane % 16 == iota((16, 128), 0)) & (lane < 64), 1.0, 0.0)
    step_raw = dot(step_raw, spread, precision=HIGH)
    bias_ref, rate_ref, gain_ref = small_refs
    row8 = iota((8, H), 0)
    packed = jnp.zeros((8, H), F32)
    for at, ref in ((0, bias_ref), (2, rate_ref), (4, gain_ref)):
        for d in range(2):
            packed = jnp.where(row8 == at + d, ref[d : d + 1, :], packed)
    spread_small = dot(packed, spread, precision=HIGH)
    sd = iota((1, 128), 1) // 16
    second_set = (sd == 1) | (sd == 2)
    other = sd % 2 == 1
    bias = jnp.where(second_set, spread_small[1:2], spread_small[0:1])
    rate = jnp.where(second_set, spread_small[3:4], spread_small[2:3])
    x = jnp.where(other, step_raw[8:16], step_raw[0:8]) + bias
    step = jnp.maximum(x, 0.0) + jnp.log1p(jnp.exp(-jnp.abs(x)))
    coef[...] = jnp.zeros_like(coef)
    coef[0:8, :] = -rate * step * LOG2E
    coef[8:16, :] = jnp.maximum(jnp.log(step) * LOG2E, -1e30)
    wide = jnp.where(iota((H, E), 1) // 64 == iota((H, E), 0), 1.0, 0.0)
    skip_rows[...] = dot(packed, wide, precision=HIGH)


def gram_tables(conv_in, cw_ref, cb_ref, s01, s23, table):
    letters = conv_in[0:8, :]
    for d in range(2):
        taps = [cw_ref[d, k : k + 1, :] * letters for k in range(4)]
        bias = cb_ref[d : d + 1, :]
        for x in range(4):
            s01[4 * x : 4 * x + 4, :] = bias + taps[0][x : x + 1] + taps[1][0:4]
            s23[4 * x : 4 * x + 4, :] = taps[2][x : x + 1] + taps[3][0:4]
        low = s23[...]
        for i in range(16):
            table[d, 16 * i : 16 * i + 16, :] = silu(s01[i : i + 1, :] + low).astype(BF16)


def edge_tables(edge_letters, conv_in, cw_ref, cb_ref, table):
    letters = conv_in[0:8, :]
    for d in range(2):
        taps = [cw_ref[d, k : k + 1, :] * letters for k in range(4)]
        bias = cb_ref[d : d + 1, :]
        total = jnp.broadcast_to(bias, (16, CH))
        for k in (1, 2, 3):
            for x in range(4):
                total = total + jnp.where(edge_letters[d][k] == x, taps[k][x : x + 1], 0.0)
        total = jnp.where(iota((16, 1), 0) < 8, silu(total), 0.0)
        table[d, GRAMS:ROWS, :] = total.astype(BF16)


def shifted(tokens, amount):
    lane = iota(tokens.shape, 1)
    moved = pltpu.roll(tokens, amount % BLOCK, axis=1)
    if amount > 0:
        return jnp.where(lane < amount, pltpu.roll(moved, 1, axis=0), moved)
    return jnp.where(lane >= BLOCK + amount, pltpu.roll(moved, tokens.shape[0] - 1, axis=0), moved)


def local_counts(mine, sc):
    hot = jnp.concatenate([jnp.where(mine == v, 1.0, 0.0) for v in range(4)] + [jnp.zeros((4, BLOCK), F32)], axis=0)
    upper = jnp.where(iota((BLOCK, BLOCK), 0) <= iota((BLOCK, BLOCK), 1), 1.0, 0.0)
    count = dot(hot.astype(BF16), upper.astype(BF16))
    coef = sc["coef"][...].T
    sc["run"][...] = jnp.zeros_like(sc["run"])
    for side in (0, 1):
        part = slice(32 * side, 32 * side + 32)
        power = jnp.zeros((32, BLOCK), F32)
        size = jnp.zeros((32, BLOCK), F32)
        for v in range(4):
            passed = count[v : v + 1]
            if side == 1:
                passed = passed[:, BLOCK - 1 : BLOCK] - passed + hot[v : v + 1]
            power = power + coef[part, v : v + 1] * passed
            size = size + coef[part, 8 + v : 9 + v] * hot[v : v + 1]
        sc["run"][part, :] = power
        sc["from"][part, :] = power - size
        k = iota((32, 48), 1)
        factor = jnp.zeros((32, 48), F32)
        for v in range(4):
            decay, size = coef[part, v : v + 1], coef[part, 8 + v : 9 + v]
            value = jnp.where(k < 16, 64.0 * decay, jnp.where(k < 32, decay, size))
            factor = jnp.where(k % 4 == v, value, factor)
        pieces = []
        for _ in range(3):
            pieces.append(factor.astype(BF16).astype(F32))
            factor = factor - pieces[-1]
        pieces = jnp.concatenate(pieces, axis=0)
        block = (iota((96, 48), 1) // 4) % 4
        for at in range(4):
            sc["factor"][side, at] = jnp.where(block == at, pieces, 0.0).astype(BF16)
    sc["run_t"][...] = sc["run"][...].T
    letter = jnp.broadcast_to(mine.astype(F32), (128, BLOCK)).T.astype(jnp.int32)[:, 0:32]
    for strand in range(2):
        hit = jnp.where(iota((BLOCK, 32), 1) % 16 == letter + 8 * strand, 1.0, 0.0).astype(BF16)
        sc["gate"][strand] = dot(hit, sc["gate_parts"][...])
    eye = iota((128, 128), 0) == iota((128, 128), 1)
    for d in range(2):
        for h in range(H):
            gain = sc["skip_rows"][4 + d : 5 + d, 64 * h : 64 * h + 1]
            sc["skip_eye"][16 * d + h] = jnp.where(eye, gain, 0.0).astype(BF16)
        sc["b_columns"][d, :, 0:GRAMS] = sc["table"][d, 0:GRAMS, E:CH].astype(F32).T.astype(BF16)


def local_conv(mine, comp, sc):
    others = jnp.zeros_like(mine)
    for v in range(4):
        others = jnp.where(mine == v, comp[v], others)
    lane = iota(mine.shape, 1)
    words = []
    for sd in range(4):
        letters = others if STRAND[sd] else mine
        word = letters
        for k in (1, 2, 3):
            word = word + 4**k * pltpu.roll(letters, k if RISING[sd] else BLOCK - k, axis=1)
        inside = lane >= 3 if RISING[sd] else lane < BLOCK - 3
        words.append(jnp.where(inside, word, -1).astype(F32))
    words = jnp.concatenate(words + [jnp.zeros((124, BLOCK), F32)], axis=0).T.astype(jnp.int32)
    for sd in range(4):
        hit = jnp.where(iota((BLOCK, GRAMS), 1) == words[:, sd : sd + 1], 1.0, 0.0).astype(BF16)
        sc["conved"][sd] = dot(hit, sc["table"][SET[sd], 0:GRAMS]).astype(BF16)
    other_word = jnp.zeros((1, GRAMS), jnp.int32)
    for place in (64, 16, 4, 1):
        digit = (iota((1, GRAMS), 1) // place) % 4
        for v in range(4):
            other_word = other_word + jnp.where(digit == v, comp[v] * place, 0)
    sc["swap"][...] = jnp.where(iota((GRAMS, GRAMS), 0) == other_word, 1.0, 0.0).astype(BF16)


def local_decays(sd, sc):
    left = iota((BLOCK, 128), 1) < 64
    half = BLOCK // 2
    rising = RISING[sd]
    t_at, s_at = iota((half, half), 0), iota((half, half), 1)
    reach = s_at <= t_at if rising else s_at >= t_at
    for pair in range(8):
        reached = []
        for sub in range(2):
            h = 16 * sd + 2 * pair + sub
            to = jnp.broadcast_to(sc["run_t"][:, h : h + 1], (BLOCK, 128))
            reached.append(to)
            source = sc["from"][h : h + 1, :]
            for top in (0, 1):
                for side in (0, 1):
                    ts, ss = slice(half * top, half * top + half), slice(half * side, half * side + half)
                    if top == side:
                        decay = jnp.where(reach, jnp.exp2(to[ts] - source[:, ss]), 0.0)
                    elif (side < top) == rising:
                        decay = jnp.exp2(to[ts] - source[:, ss])
                    else:
                        continue
                    sc["decay"][h, ts, ss] = decay.astype(BF16)
        sc["grow"][sd, :, 128 * pair : 128 * pair + 128] = jnp.exp2(jnp.where(left, reached[0], reached[1]))


def mixer(here, comp, tokens, cw_ref, cb_ref, ng_ref, sc, between_scans):
    blocks = tokens.shape[0]
    others = jnp.zeros_like(tokens)
    for v in range(4):
        others = jnp.where(tokens == v, comp[v], others)

    block_at, lane_at = iota(tokens.shape, 0), iota(tokens.shape, 1)
    low_edge = (block_at == 0) & (lane_at < 3)
    high_edge = (block_at == blocks - 1) & (lane_at >= BLOCK - 3)
    for strand, letters in ((0, tokens), (1, others)):
        rise = 64 * shifted(letters, 3) + 16 * shifted(letters, 2) + 4 * shifted(letters, 1) + letters
        fall = 64 * shifted(letters, -3) + 16 * shifted(letters, -2) + 4 * shifted(letters, -1) + letters
        sc["words"][strand] = jnp.where(low_edge, GRAMS + 4 * strand + lane_at, rise)
        sc["words"][2 + strand] = jnp.where(high_edge, GRAMS + 4 * strand + BLOCK - 1 - lane_at, fall)

    edge_letters = []
    row = iota((16, 1), 0)

    def letter_of(source, block, lane):
        line = source[block : block + 1, :]
        return jnp.sum(jnp.where(iota(line.shape, 1) == lane, line, 0), axis=1, keepdims=True)

    low = [[letter_of(s, 0, j) for j in range(3)] for s in (tokens, others)]
    high = [[letter_of(s, blocks - 1, BLOCK - 1 - j) for j in range(3)] for s in (tokens, others)]
    for d in range(2):
        first, second = (low[0], high[1]) if d == 0 else (high[0], low[1])
        columns = {}
        for k in (1, 2, 3):
            column = jnp.full((16, 1), 4, jnp.int32)
            for strand, letters in ((0, first), (1, second)):
                for j in range(3):
                    at = j - (3 - k)
                    if at >= 0:
                        column = jnp.where(row == 4 * strand + j, letters[at], column)
            columns[k] = column
        edge_letters.append(columns)
    edge_tables(edge_letters, sc["conv_in"], cw_ref, cb_ref, sc["table"])

    rows = 4 * blocks
    one_hot = jnp.where(sc["fourfold"][...] == iota((rows, BLOCK), 0) % 4, 1.0, 0.0)
    upper = jnp.where(iota((BLOCK, BLOCK), 0) <= iota((BLOCK, BLOCK), 1), 1.0, 0.0)
    inside = dot(one_hot.astype(BF16), upper.astype(BF16))
    total = inside[:, BLOCK - 1 : BLOCK]
    a, b = iota((rows, rows), 0), iota((rows, rows), 1)
    aj, bj = a // 4, b // 4
    between = (a % 4 == b % 4) & (((aj < bj) & (bj < here)) | ((here < bj) & (bj < aj)))
    passed = dot(jnp.where(between, 1.0, 0.0).astype(BF16), jnp.broadcast_to(total, inside.shape).astype(BF16))
    before = iota((rows, 1), 0) // 4 < here
    away = passed + jnp.where(before, total - inside, inside - one_hot)
    high = jnp.floor(away * (1.0 / 64.0))
    sc["counts"][0] = high.astype(BF16)
    sc["counts"][1] = (away - 64.0 * high).astype(BF16)
    sc["counts"][2] = one_hot.astype(BF16)

    def entry_weights(four, at, side):
        start = 16 * four if isinstance(four, int) else pl.multiple_of(16 * four, 16)
        counts = jnp.concatenate([sc["counts"][i, pl.ds(start, 16), :] for i in range(3)], axis=0)
        power = dot(sc["factor"][side, at], counts)
        return jnp.exp2(power[0:32] + power[32:64] + power[64:96])

    word_of_row = iota((GRAMS, BLOCK), 0).astype(F32).astype(BF16)
    group = 16

    def entering(step, acc):
        hits, powers = [], []
        for i in range(group):
            j = step * group + i
            side = jnp.where(j < here, 0, 1)
            words = sc["words"][2 * side, pl.ds(j, 1), :].astype(F32).astype(BF16)
            hits.append(jnp.where(word_of_row == words, jnp.ones((), BF16), jnp.zeros((), BF16)))
            power = entry_weights(step * (group // 4) + i // 4, i % 4, side)
            both = [jnp.where(j < here, power, 0.0), jnp.where(j > here, power, 0.0)]
            powers.append(jnp.concatenate(both, axis=0).astype(BF16))
        return acc + dot_t(jnp.concatenate(hits, axis=1), jnp.concatenate(powers, axis=1))

    acc = lax.fori_loop(0, blocks // group, entering, jnp.zeros((GRAMS, 64), F32)).astype(BF16)
    swapped = dot(sc["swap"][...], acc)
    lane64 = iota((GRAMS, 64), 1)
    sc["weigh"][0:GRAMS, :] = jnp.where(lane64 % 32 < 16, acc.astype(F32), swapped).astype(BF16)
    edges = []
    for side in (0, 1):
        present = here > 0 if side == 0 else here < blocks - 1
        edge = entry_weights(0, 0, 0) if side == 0 else entry_weights(blocks // 4 - 1, 3, 1)
        edges.append(jnp.where(present, edge, 0.0).astype(BF16))
    own = (iota((16, 32), 0) < 4) == (iota((16, 32), 1) < 16)
    for side in (0, 1):
        r16, l16 = iota((16, BLOCK), 0), iota((16, BLOCK), 1)
        pos = l16 if side == 0 else BLOCK - 1 - l16
        pick = jnp.where((pos < 3) & ((r16 == pos) | (r16 == 4 + pos)), 1.0, 0.0).astype(BF16)
        picked = jnp.where(own, dot_t(pick, edges[side]), 0.0)
        sc["edge"][:, 32 * side : 32 * side + 32] = picked
    sc["weigh"][GRAMS:ROWS, :] = sc["edge"][...].astype(BF16)

    for i in range(4):
        sc["local"][i : i + 1, :] = sc["words"][i, pl.ds(here, 1), :].astype(F32)
    sc["local"][4:128, :] = jnp.zeros((124, BLOCK), F32)
    local = sc["local"][...].T.astype(jnp.int32)
    for d in range(2):
        tail = sc["table"][d, GRAMS:ROWS, E:CH].astype(F32)
        tail = jnp.concatenate([tail, jnp.zeros((112, CH - E), F32)], axis=0).T
        sc["b_columns"][d, :, GRAMS:ROWS] = tail[:, 0 : ROWS - GRAMS].astype(BF16)

    for d in range(2):
        scans = [sd for sd in range(4) if SET[sd] == d]
        hits = []
        for sd in scans:
            part = slice(0, 16) if RISING[sd] else slice(BLOCK - 16, BLOCK)
            hits.append(jnp.where(iota((16, ROWS), 1) == local[part, sd : sd + 1], 1.0, 0.0))
        rows = dot(jnp.concatenate(hits, axis=0).astype(BF16), sc["table"][d]).astype(BF16)
        for i, sd in enumerate(scans):
            part = slice(0, 16) if RISING[sd] else slice(BLOCK - 16, BLOCK)
            sc["conved"][sd, part, :] = rows[16 * i : 16 * i + 16]

    for sd in range(4):
        d = SET[sd]
        tail = sc["conved"][sd, :, E:CH]
        b_rows = tail[:, :64]
        c_rows = pltpu.roll(tail.astype(F32), 64, axis=1)[:, :64].astype(BF16)
        sc["scores"][sd] = dot_t(c_rows, b_rows).astype(BF16)
        place = jnp.where(iota((64, E), 0) == 16 * sd + iota((64, E), 1) // 64, 1.0, 0.0).astype(BF16)
        weights = dot(sc["weigh"][...], place)
        weighted = weights.astype(BF16) * sc["table"][d, :, 0:E]
        state = dot(sc["b_columns"][d, 0:64, :], weighted).astype(BF16)
        sc["carried"][sd] = dot(c_rows, state)

    left = iota((BLOCK, 128), 1) < 64
    half = BLOCK // 2
    scales = []
    for sd in range(4):
        d, rising = SET[sd], RISING[sd]
        square = jnp.zeros((BLOCK, 128), F32)
        for pair in range(8):
            cols = slice(128 * pair, 128 * pair + 128)
            values = sc["conved"][sd, :, cols]
            parts = []
            for sub in range(2):
                h = 16 * sd + 2 * pair + sub
                skip = sc["skip_eye"][16 * d + 2 * pair + sub]
                rows_of = []
                for top in (True, False):
                    ts = slice(0, half) if top else slice(half, BLOCK)
                    mixing = sc["decay"][h, ts, ts] * sc["scores"][sd, ts, ts] + skip
                    if top == rising:
                        rows_of.append(dot(mixing, values[ts]))
                    else:
                        ss = slice(half, BLOCK) if top else slice(0, half)
                        far = sc["decay"][h, ts, ss] * sc["scores"][sd, ts, ss]
                        whole = [mixing, far] if top else [far, mixing]
                        rows_of.append(dot(jnp.concatenate(whole, axis=1), values))
                parts.append(jnp.concatenate(rows_of, axis=0))
            both = jnp.where(left, parts[0], parts[1]) + sc["carried"][sd, :, cols] * sc["grow"][sd, :, cols]
            gated = both * sc["gate"][STRAND[sd], :, cols]
            square = square + gated * gated
            sc["gated"][sd, :, cols] = gated
        mean = jnp.sum(square, axis=1, keepdims=True) * (1.0 / E)
        scales.append(lax.rsqrt(mean + EPS))
        between_scans(sd)
    for pair in range(8):
        cols = slice(128 * pair, 128 * pair + 128)
        ones, twos = [sc["gated"][0, :, cols] * scales[0], sc["gated"][3, :, cols] * scales[3]], [
            sc["gated"][1, :, cols] * scales[1],
            sc["gated"][2, :, cols] * scales[2],
        ]
        mixed = (ones[0] + ones[1]) * ng_ref[0:1, cols] + (twos[0] + twos[1]) * ng_ref[1:2, cols]
        sc["mixed"][:, cols] = mixed.astype(BF16)
    return sc["mixed"][...]


def scratch(blocks):
    return {
        "gate_parts": pltpu.VMEM((32, E), BF16),
        "conv_in": pltpu.VMEM((16, CH), F32),
        "coef": pltpu.VMEM((128, 128), F32),
        "skip_rows": pltpu.VMEM((8, E), F32),
        "words": pltpu.VMEM((4, blocks, BLOCK), jnp.int32),
        "s01": pltpu.VMEM((16, CH), F32),
        "s23": pltpu.VMEM((16, CH), F32),
        "table": pltpu.VMEM((2, ROWS, CH), BF16),
        "weigh": pltpu.VMEM((ROWS, 64), BF16),
        "edge": pltpu.VMEM((16, 64), F32),
        "tokens": pltpu.VMEM((blocks, BLOCK), jnp.int32),
        "run": pltpu.VMEM((128, BLOCK), F32),
        "from": pltpu.VMEM((64, BLOCK), F32),
        "local": pltpu.VMEM((128, BLOCK), F32),
        "gate": pltpu.VMEM((2, BLOCK, E), F32),
        "conved": pltpu.VMEM((4, BLOCK, CH), BF16),
        "scores": pltpu.VMEM((4, BLOCK, BLOCK), BF16),
        "swap": pltpu.VMEM((GRAMS, GRAMS), BF16),
        "skip_eye": pltpu.VMEM((32, 128, 128), BF16),
        "factor": pltpu.VMEM((2, 4, 96, 48), BF16),
        "counts": pltpu.VMEM((3, 4 * blocks, BLOCK), BF16),
        "fourfold": pltpu.VMEM((4 * blocks, BLOCK), jnp.int32),
        "run_t": pltpu.VMEM((BLOCK, 128), F32),
        "b_columns": pltpu.VMEM((2, 128, ROWS), BF16),
        "decay": pltpu.VMEM((64, BLOCK, BLOCK), BF16),
        "grow": pltpu.VMEM((4, BLOCK, E), F32),
        "carried": pltpu.VMEM((4, BLOCK, E), F32),
        "gated": pltpu.VMEM((4, BLOCK, E), F32),
        "mixed": pltpu.VMEM((BLOCK, E), BF16),
    }


MESH = pl.DeviceIdType.MESH
PARAMS = 10


def kernel(names, *refs):
    params, shard = refs[:PARAMS], refs[PARAMS]
    tok, out = refs[PARAMS + 1], refs[PARAMS + 2]
    sc = dict(zip(names, refs[PARAMS + 3 :]))
    batch, here = lax.axis_index("batch"), lax.axis_index("seq")
    z_low, core = lax.div(batch, 2), lax.rem(batch, 2)
    y, z_high, x = lax.div(here, 8), lax.rem(lax.div(here, 4), 2), lax.rem(here, 4)
    z = z_high * 4 + z_low
    received, wall = sc["received"], sc["wall"]
    partner = (z_low * 2 + 1 - core, here)
    barrier = pltpu.get_barrier_semaphore()

    def greet(device):
        pl.semaphore_signal(barrier, inc=1, device_id=device, device_id_type=MESH)

    def at(xx, yy, zz):
        return (lax.rem(zz, 4) * 2 + core, yy * 8 + lax.div(zz, 4) * 4 + xx)

    def loop(first, last, act):
        def go(k, carry):
            act(k)
            return carry

        lax.fori_loop(first, last, go, 0)

    loop(1, 8, lambda k: greet(at(x, y, lax.rem(z + k, 8))))
    loop(1, 16, lambda k: greet((batch, lax.div(lax.rem(4 * y + x + k, 16), 4) * 8 + 4 * z_high + lax.rem(x + k, 4))))
    greet(partner)

    def copy_of(piece, send, recv, device):
        return pltpu.make_async_remote_copy(piece, piece, send, recv, device, MESH)

    def token_z(owner):
        piece = received.at[y, x, owner]
        return copy_of(piece, sc["token_send"].at[0], sc["token_recv"].at[16], at(x, y, lax.rem(z + 4, 8)))

    def plane_peer(k):
        return lax.rem(4 * y + x + k, 16)

    def token_plane(k, owner):
        device = at(lax.rem(plane_peer(k), 4), lax.div(plane_peer(k), 4), z)
        piece = received.at[lax.div(owner, 4), lax.rem(owner, 4)]
        return copy_of(piece, sc["token_send"].at[k], sc["token_recv"].at[owner], device)

    mine, inner, outer = [y * 4 + x, x * 4 + y], [x, y], [y, x]

    def z_copy(c, k, owner):
        piece = wall.at[core, c, mine[c], owner]
        return copy_of(piece, sc["z_send"].at[c, k], sc["z_recv"].at[c, owner], at(x, y, lax.rem(z + k, 8)))

    def along(c, k, first):
        step_x, step_y = at(lax.rem(x + k, 4), y, z), at(x, lax.rem(y + k, 4), z)
        return step_x if (c == 0) == first else step_y

    def second_copy(c, k, owner):
        piece = wall.at[core, c, 4 * outer[c] + owner]
        return copy_of(piece, sc["second_send"].at[c, k], sc["second_recv"].at[c, owner], along(c, k, True))

    def third_copy(c, k, owner):
        piece = wall.at[core, c, pl.ds(4 * owner, 4)]
        return copy_of(piece, sc["third_send"].at[c, k], sc["third_recv"].at[c, owner], along(c, k, False))

    def core_copy(side, c, owner):
        piece = wall.at[side, c, pl.ds(4 * owner, 4)]
        return copy_of(piece, sc["core_send"].at[c, owner], sc["core_recv"].at[c, owner], partner)

    first = [pltpu.make_async_copy(tok, received.at[y, x, z_high], sc["own_sem"].at[0])]
    for c in range(2):
        half = shard.at[16 * c : 16 * c + 16]
        first.append(pltpu.make_async_copy(half, wall.at[core, c, mine[c], z], sc["own_sem"].at[1 + c]))
    fetch, held = [], []
    for i, ref in enumerate(params):
        held.append(sc[f"held{i}"])
        fetch.append(pltpu.make_async_copy(ref, held[i], sc["own_sem"].at[3 + i]))
    for copy in first + fetch:
        copy.start()
    for copy in first:
        copy.wait()

    def send():
        pl.semaphore_wait(barrier, 23)
        token_z(z_high).start()
        for c in range(2):
            loop(1, 8, lambda k: z_copy(c, k, z).start())

    last = z_high == 1

    pl.when(last)(send)
    for copy in fetch:
        copy.wait()
    comp_ref, emb, inw, stw, cw, cb, sb, dr, sg, ng = held
    comp = [comp_ref[v] for v in range(4)]
    letter_tables(
        comp, emb, inw, stw, (sb, dr, sg), sc["gate_parts"], sc["conv_in"], sc["coef"], sc["skip_rows"]
    )
    gram_tables(sc["conv_in"], cw, cb, sc["s01"], sc["s23"], sc["table"])
    pl.when(z_high == 0)(send)
    local_counts(received[y, x, z_high], sc)
    local_conv(received[y, x, z_high], comp, sc)
    for sd in range(4):
        local_decays(sd, sc)

    token_z(1 - z_high).wait_recv()
    loop(1, 16, lambda k: token_plane(k, 4 * y + x).start())
    for c in range(2):
        loop(1, 8, lambda k: z_copy(c, k, lax.rem(z + k, 8)).wait_recv())
        loop(1, 4, lambda k: second_copy(c, k, inner[c]).start())
    for c in range(2):
        loop(1, 4, lambda k: second_copy(c, k, lax.rem(inner[c] + k, 4)).wait_recv())
        loop(1, 4, lambda k: third_copy(c, k, outer[c]).start())
        core_copy(core, c, outer[c]).start()
    loop(1, 16, lambda k: token_plane(k, plane_peer(k)).wait_recv())
    for j in range(32):
        line = received[j // 8, j % 4, (j // 4) % 2]
        sc["tokens"][j : j + 1, :] = line
        sc["fourfold"][4 * j : 4 * j + 4, :] = jnp.broadcast_to(line, (4, BLOCK))

    def pass_on_third(sd):
        if sd < 2:
            for k in (1, 3) if sd == 0 else (2,):
                for c in range(2):
                    owner = lax.rem(outer[c] + k, 4)
                    third_copy(c, k, owner).wait_recv()
                    core_copy(core, c, owner).start()

    mixed = mixer(here, comp, sc["tokens"][...], cw, cb, ng, sc, pass_on_third)
    for c in range(2):
        loop(0, 4, lambda q: core_copy(1 - core, c, q).wait_recv())
    order = []
    for s in range(32):
        yy, zz, xx = s // 8, 4 * ((s // 4) % 2), s % 4
        order += [(0, 4 * yy + xx, zz), (1, 4 * xx + yy, zz)]
    for low in range(4):
        sides = [jnp.concatenate([wall[k, c, p, zz + low] for c, p, zz in order], axis=0) for k in range(2)]
        out[:, 256 * low : 256 * low + 256] = dot(mixed, jnp.concatenate(sides, axis=1)).astype(BF16)

    for c in range(2):
        loop(1, 8, lambda k: z_copy(c, k, z).wait_send())
        loop(1, 4, lambda k: second_copy(c, k, inner[c]).wait_send())
        loop(1, 4, lambda k: third_copy(c, k, outer[c]).wait_send())
        loop(0, 4, lambda q: core_copy(core, c, q).wait_send())
    token_z(z_high).wait_send()
    loop(1, 16, lambda k: token_plane(k, 4 * y + x).wait_send())


def on_device(tok, comp, emb, inw, stw, cw, cb, sb, dr, sg, ng, wout):
    params = [comp, emb, inw, stw.T, cw, cb, sb, dr, sg, ng]
    shapes = scratch(32)
    shapes["received"] = pltpu.VMEM((4, 4, 2, 1, BLOCK), jnp.int32)
    shapes["wall"] = pltpu.VMEM((2, 2, 16, 8, 16, 128), BF16)
    shapes["own_sem"] = pltpu.SemaphoreType.DMA((3 + PARAMS,))
    for name, count in (("token", (17,)), ("z", (2, 8)), ("second", (2, 4)), ("third", (2, 4)), ("core", (2, 4))):
        shapes[name + "_send"] = pltpu.SemaphoreType.DMA(count)
        shapes[name + "_recv"] = pltpu.SemaphoreType.DMA(count)
    for i, value in enumerate(params):
        space = pltpu.SMEM if value.ndim == 1 else pltpu.VMEM
        shapes[f"held{i}"] = space(value.shape, value.dtype)
    anywhere = pl.BlockSpec(memory_space=pl.ANY)
    out = pl.pallas_call(
        partial(kernel, tuple(shapes)),
        out_shape=jax.ShapeDtypeStruct((BLOCK, D), BF16),
        in_specs=[anywhere] * (PARAMS + 2),
        out_specs=pl.BlockSpec(memory_space=pltpu.VMEM),
        scratch_shapes=list(shapes.values()),
        compiler_params=pltpu.CompilerParams(
            collective_id=0, has_side_effects=True, vmem_limit_bytes=44 << 20
        ),
    )(*[pltpu.with_memory_space_constraint(v, pltpu.HBM) for v in (*params, wout, tok)])
    return out[None]


def solution(mesh):
    placed = (P("batch", "seq"),) + (P(),) * 10 + (P("seq", "batch"),)
    return jax.shard_map(
        on_device, mesh=mesh, in_specs=placed, out_specs=P("batch", "seq", None), check_vma=False
    )
```

```python
from functools import partial

import jax
import jax.numpy as jnp
from jax import lax
from jax.experimental import pallas as pl
from jax.experimental.pallas import tpu as pltpu
from jax.sharding import PartitionSpec as P

D = 1024
E = 1024
H = 16
N = 64
CH = 1152
BLOCK = 256
GRAMS = 256
ROWS = 272
LOG2E = 1.4426950408889634
EPS = 1e-05
F32 = jnp.float32
BF16 = jnp.bfloat16
HIGH = lax.Precision.HIGHEST
STRAND = (0, 1, 0, 1)
SET = (0, 1, 1, 0)
RISING = (True, True, False, False)


def iota(shape, dim):
    return lax.broadcasted_iota(jnp.int32, shape, dim)


def silu(x):
    return x * jax.nn.sigmoid(x)


def dot(a, b, **kw):
    return jnp.dot(a, b, preferred_element_type=F32, **kw)


def dot_t(a, b):
    return lax.dot_general(a, b, (((1,), (1,)), ((), ())), preferred_element_type=F32)


def letter_tables(comp, emb_ref, inw_ref, stw_ref, small_refs, gate_parts, conv_in, coef, skip_rows):
    row = iota((16, 1), 0)
    letter = jnp.where(row < 4, row, 4)
    for v in range(4):
        letter = jnp.where(row == 8 + v, comp[v], letter)
    emb = emb_ref[...].astype(F32)
    rows = jnp.zeros((16, D), F32)
    for x in range(4):
        rows = jnp.where(letter == x, emb[x : x + 1], rows)
    rows = rows.astype(BF16)
    projected = dot(rows, inw_ref[...]).astype(BF16).astype(F32)
    gate = silu(projected[:, :E])
    hi = gate.astype(BF16)
    gate_parts[0:16, :] = hi
    gate_parts[16:32, :] = (gate - hi.astype(F32)).astype(BF16)
    conv_in[...] = projected[:, E:]

    step_raw = dot_t(rows, stw_ref[...])
    lane = iota((16, 128), 1)
    spread = jnp.where((lane % 16 == iota((16, 128), 0)) & (lane < 64), 1.0, 0.0)
    step_raw = dot(step_raw, spread, precision=HIGH)
    bias_ref, rate_ref, gain_ref = small_refs
    row8 = iota((8, H), 0)
    packed = jnp.zeros((8, H), F32)
    for at, ref in ((0, bias_ref), (2, rate_ref), (4, gain_ref)):
        for d in range(2):
            packed = jnp.where(row8 == at + d, ref[d : d + 1, :], packed)
    spread_small = dot(packed, spread, precision=HIGH)
    sd = iota((1, 128), 1) // 16
    second_set = (sd == 1) | (sd == 2)
    other = sd % 2 == 1
    bias = jnp.where(second_set, spread_small[1:2], spread_small[0:1])
    rate = jnp.where(second_set, spread_small[3:4], spread_small[2:3])
    x = jnp.where(other, step_raw[8:16], step_raw[0:8]) + bias
    step = jnp.maximum(x, 0.0) + jnp.log1p(jnp.exp(-jnp.abs(x)))
    coef[...] = jnp.zeros_like(coef)
    coef[0:8, :] = -rate * step * LOG2E
    coef[8:16, :] = jnp.maximum(jnp.log(step) * LOG2E, -1e30)
    wide = jnp.where(iota((H, E), 1) // 64 == iota((H, E), 0), 1.0, 0.0)
    skip_rows[...] = dot(packed, wide, precision=HIGH)


def gram_tables(conv_in, cw_ref, cb_ref, s01, s23, table):
    letters = conv_in[0:8, :]
    for d in range(2):
        taps = [cw_ref[d, k : k + 1, :] * letters for k in range(4)]
        bias = cb_ref[d : d + 1, :]
        for x in range(4):
            s01[4 * x : 4 * x + 4, :] = bias + taps[0][x : x + 1] + taps[1][0:4]
            s23[4 * x : 4 * x + 4, :] = taps[2][x : x + 1] + taps[3][0:4]
        low = s23[...]
        for i in range(16):
            table[d, 16 * i : 16 * i + 16, :] = silu(s01[i : i + 1, :] + low).astype(BF16)


def edge_tables(edge_letters, conv_in, cw_ref, cb_ref, table):
    letters = conv_in[0:8, :]
    for d in range(2):
        taps = [cw_ref[d, k : k + 1, :] * letters for k in range(4)]
        bias = cb_ref[d : d + 1, :]
        total = jnp.broadcast_to(bias, (16, CH))
        for k in (1, 2, 3):
            for x in range(4):
                total = total + jnp.where(edge_letters[d][k] == x, taps[k][x : x + 1], 0.0)
        total = jnp.where(iota((16, 1), 0) < 8, silu(total), 0.0)
        table[d, GRAMS:ROWS, :] = total.astype(BF16)


def shifted(tokens, amount):
    lane = iota(tokens.shape, 1)
    moved = pltpu.roll(tokens, amount % BLOCK, axis=1)
    if amount > 0:
        return jnp.where(lane < amount, pltpu.roll(moved, 1, axis=0), moved)
    return jnp.where(lane >= BLOCK + amount, pltpu.roll(moved, tokens.shape[0] - 1, axis=0), moved)


def local_counts(mine, sc):
    hot = jnp.concatenate([jnp.where(mine == v, 1.0, 0.0) for v in range(4)] + [jnp.zeros((4, BLOCK), F32)], axis=0)
    upper = jnp.where(iota((BLOCK, BLOCK), 0) <= iota((BLOCK, BLOCK), 1), 1.0, 0.0)
    count = dot(hot.astype(BF16), upper.astype(BF16))
    coef = sc["coef"][...].T
    sc["run"][...] = jnp.zeros_like(sc["run"])
    for side in (0, 1):
        part = slice(32 * side, 32 * side + 32)
        power = jnp.zeros((32, BLOCK), F32)
        size = jnp.zeros((32, BLOCK), F32)
        for v in range(4):
            passed = count[v : v + 1]
            if side == 1:
                passed = passed[:, BLOCK - 1 : BLOCK] - passed + hot[v : v + 1]
            power = power + coef[part, v : v + 1] * passed
            size = size + coef[part, 8 + v : 9 + v] * hot[v : v + 1]
        sc["run"][part, :] = power
        sc["from"][part, :] = power - size
        k = iota((32, 48), 1)
        factor = jnp.zeros((32, 48), F32)
        for v in range(4):
            decay, size = coef[part, v : v + 1], coef[part, 8 + v : 9 + v]
            value = jnp.where(k < 16, 64.0 * decay, jnp.where(k < 32, decay, size))
            factor = jnp.where(k % 4 == v, value, factor)
        pieces = []
        for _ in range(3):
            pieces.append(factor.astype(BF16).astype(F32))
            factor = factor - pieces[-1]
        pieces = jnp.concatenate(pieces, axis=0)
        block = (iota((96, 48), 1) // 4) % 4
        for at in range(4):
            sc["factor"][side, at] = jnp.where(block == at, pieces, 0.0).astype(BF16)
    sc["run_t"][...] = sc["run"][...].T
    letter = jnp.broadcast_to(mine.astype(F32), (128, BLOCK)).T.astype(jnp.int32)[:, 0:32]
    for strand in range(2):
        hit = jnp.where(iota((BLOCK, 32), 1) % 16 == letter + 8 * strand, 1.0, 0.0).astype(BF16)
        sc["gate"][strand] = dot(hit, sc["gate_parts"][...])
    eye = iota((128, 128), 0) == iota((128, 128), 1)
    for d in range(2):
        for h in range(H):
            gain = sc["skip_rows"][4 + d : 5 + d, 64 * h : 64 * h + 1]
            sc["skip_eye"][16 * d + h] = jnp.where(eye, gain, 0.0).astype(BF16)
        sc["b_columns"][d, :, 0:GRAMS] = sc["table"][d, 0:GRAMS, E:CH].astype(F32).T.astype(BF16)


def local_conv(mine, comp, sc):
    others = jnp.zeros_like(mine)
    for v in range(4):
        others = jnp.where(mine == v, comp[v], others)
    lane = iota(mine.shape, 1)
    words = []
    for sd in range(4):
        letters = others if STRAND[sd] else mine
        word = letters
        for k in (1, 2, 3):
            word = word + 4**k * pltpu.roll(letters, k if RISING[sd] else BLOCK - k, axis=1)
        inside = lane >= 3 if RISING[sd] else lane < BLOCK - 3
        words.append(jnp.where(inside, word, -1).astype(F32))
    words = jnp.concatenate(words + [jnp.zeros((124, BLOCK), F32)], axis=0).T.astype(jnp.int32)
    for sd in range(4):
        hit = jnp.where(iota((BLOCK, GRAMS), 1) == words[:, sd : sd + 1], 1.0, 0.0).astype(BF16)
        sc["conved"][sd] = dot(hit, sc["table"][SET[sd], 0:GRAMS]).astype(BF16)
    other_word = jnp.zeros((1, GRAMS), jnp.int32)
    for place in (64, 16, 4, 1):
        digit = (iota((1, GRAMS), 1) // place) % 4
        for v in range(4):
            other_word = other_word + jnp.where(digit == v, comp[v] * place, 0)
    sc["swap"][...] = jnp.where(iota((GRAMS, GRAMS), 0) == other_word, 1.0, 0.0).astype(BF16)


def local_decays(sd, sc):
    left = iota((BLOCK, 128), 1) < 64
    half = BLOCK // 2
    rising = RISING[sd]
    t_at, s_at = iota((half, half), 0), iota((half, half), 1)
    reach = s_at <= t_at if rising else s_at >= t_at
    for pair in range(8):
        reached = []
        for sub in range(2):
            h = 16 * sd + 2 * pair + sub
            to = jnp.broadcast_to(sc["run_t"][:, h : h + 1], (BLOCK, 128))
            reached.append(to)
            source = sc["from"][h : h + 1, :]
            for top in (0, 1):
                for side in (0, 1):
                    ts, ss = slice(half * top, half * top + half), slice(half * side, half * side + half)
                    if top == side:
                        decay = jnp.where(reach, jnp.exp2(to[ts] - source[:, ss]), 0.0)
                    elif (side < top) == rising:
                        decay = jnp.exp2(to[ts] - source[:, ss])
                    else:
                        continue
                    sc["decay"][h, ts, ss] = decay.astype(BF16)
        sc["grow"][sd, :, 128 * pair : 128 * pair + 128] = jnp.exp2(jnp.where(left, reached[0], reached[1]))


def mixer(here, comp, tokens, cw_ref, cb_ref, ng_ref, sc, before_history, between_scans):
    blocks = tokens.shape[0]
    others = jnp.zeros_like(tokens)
    for v in range(4):
        others = jnp.where(tokens == v, comp[v], others)

    block_at, lane_at = iota(tokens.shape, 0), iota(tokens.shape, 1)
    low_edge = (block_at == 0) & (lane_at < 3)
    high_edge = (block_at == blocks - 1) & (lane_at >= BLOCK - 3)
    for strand, letters in ((0, tokens), (1, others)):
        rise = 64 * shifted(letters, 3) + 16 * shifted(letters, 2) + 4 * shifted(letters, 1) + letters
        fall = 64 * shifted(letters, -3) + 16 * shifted(letters, -2) + 4 * shifted(letters, -1) + letters
        sc["words"][strand] = jnp.where(low_edge, GRAMS + 4 * strand + lane_at, rise)
        sc["words"][2 + strand] = jnp.where(high_edge, GRAMS + 4 * strand + BLOCK - 1 - lane_at, fall)

    edge_letters = []
    row = iota((16, 1), 0)

    def letter_of(source, block, lane):
        line = source[block : block + 1, :]
        return jnp.sum(jnp.where(iota(line.shape, 1) == lane, line, 0), axis=1, keepdims=True)

    low = [[letter_of(s, 0, j) for j in range(3)] for s in (tokens, others)]
    high = [[letter_of(s, blocks - 1, BLOCK - 1 - j) for j in range(3)] for s in (tokens, others)]
    for d in range(2):
        first, second = (low[0], high[1]) if d == 0 else (high[0], low[1])
        columns = {}
        for k in (1, 2, 3):
            column = jnp.full((16, 1), 4, jnp.int32)
            for strand, letters in ((0, first), (1, second)):
                for j in range(3):
                    at = j - (3 - k)
                    if at >= 0:
                        column = jnp.where(row == 4 * strand + j, letters[at], column)
            columns[k] = column
        edge_letters.append(columns)
    edge_tables(edge_letters, sc["conv_in"], cw_ref, cb_ref, sc["table"])

    rows = 4 * blocks
    one_hot = jnp.where(sc["fourfold"][...] == iota((rows, BLOCK), 0) % 4, 1.0, 0.0)
    upper = jnp.where(iota((BLOCK, BLOCK), 0) <= iota((BLOCK, BLOCK), 1), 1.0, 0.0)
    inside = dot(one_hot.astype(BF16), upper.astype(BF16))
    total = inside[:, BLOCK - 1 : BLOCK]
    a, b = iota((rows, rows), 0), iota((rows, rows), 1)
    aj, bj = a // 4, b // 4
    between = (a % 4 == b % 4) & (((aj < bj) & (bj < here)) | ((here < bj) & (bj < aj)))
    passed = dot(jnp.where(between, 1.0, 0.0).astype(BF16), jnp.broadcast_to(total, inside.shape).astype(BF16))
    before = iota((rows, 1), 0) // 4 < here
    away = passed + jnp.where(before, total - inside, inside - one_hot)
    high = jnp.floor(away * (1.0 / 64.0))
    sc["counts"][0] = high.astype(BF16)
    sc["counts"][1] = (away - 64.0 * high).astype(BF16)
    sc["counts"][2] = one_hot.astype(BF16)

    def entry_weights(four, at, side):
        start = 16 * four if isinstance(four, int) else pl.multiple_of(16 * four, 16)
        counts = jnp.concatenate([sc["counts"][i, pl.ds(start, 16), :] for i in range(3)], axis=0)
        power = dot(sc["factor"][side, at], counts)
        return jnp.exp2(power[0:32] + power[32:64] + power[64:96])

    word_of_row = iota((GRAMS, BLOCK), 0).astype(F32).astype(BF16)
    group = 16

    def entering(step, acc):
        hits, powers = [], []
        for i in range(group):
            j = step * group + i
            side = jnp.where(j < here, 0, 1)
            words = sc["words"][2 * side, pl.ds(j, 1), :].astype(F32).astype(BF16)
            hits.append(jnp.where(word_of_row == words, jnp.ones((), BF16), jnp.zeros((), BF16)))
            power = entry_weights(step * (group // 4) + i // 4, i % 4, side)
            both = [jnp.where(j < here, power, 0.0), jnp.where(j > here, power, 0.0)]
            powers.append(jnp.concatenate(both, axis=0).astype(BF16))
        return acc + dot_t(jnp.concatenate(hits, axis=1), jnp.concatenate(powers, axis=1))

    before_history()
    acc = lax.fori_loop(0, blocks // group, entering, jnp.zeros((GRAMS, 64), F32)).astype(BF16)
    swapped = dot(sc["swap"][...], acc)
    lane64 = iota((GRAMS, 64), 1)
    sc["weigh"][0:GRAMS, :] = jnp.where(lane64 % 32 < 16, acc.astype(F32), swapped).astype(BF16)
    edges = []
    for side in (0, 1):
        present = here > 0 if side == 0 else here < blocks - 1
        edge = entry_weights(0, 0, 0) if side == 0 else entry_weights(blocks // 4 - 1, 3, 1)
        edges.append(jnp.where(present, edge, 0.0).astype(BF16))
    own = (iota((16, 32), 0) < 4) == (iota((16, 32), 1) < 16)
    for side in (0, 1):
        r16, l16 = iota((16, BLOCK), 0), iota((16, BLOCK), 1)
        pos = l16 if side == 0 else BLOCK - 1 - l16
        pick = jnp.where((pos < 3) & ((r16 == pos) | (r16 == 4 + pos)), 1.0, 0.0).astype(BF16)
        picked = jnp.where(own, dot_t(pick, edges[side]), 0.0)
        sc["edge"][:, 32 * side : 32 * side + 32] = picked
    sc["weigh"][GRAMS:ROWS, :] = sc["edge"][...].astype(BF16)

    for i in range(4):
        sc["local"][i : i + 1, :] = sc["words"][i, pl.ds(here, 1), :].astype(F32)
    sc["local"][4:128, :] = jnp.zeros((124, BLOCK), F32)
    local = sc["local"][...].T.astype(jnp.int32)
    for d in range(2):
        tail = sc["table"][d, GRAMS:ROWS, E:CH].astype(F32)
        tail = jnp.concatenate([tail, jnp.zeros((112, CH - E), F32)], axis=0).T
        sc["b_columns"][d, :, GRAMS:ROWS] = tail[:, 0 : ROWS - GRAMS].astype(BF16)

    for d in range(2):
        scans = [sd for sd in range(4) if SET[sd] == d]
        hits = []
        for sd in scans:
            part = slice(0, 16) if RISING[sd] else slice(BLOCK - 16, BLOCK)
            hits.append(jnp.where(iota((16, ROWS), 1) == local[part, sd : sd + 1], 1.0, 0.0))
        rows = dot(jnp.concatenate(hits, axis=0).astype(BF16), sc["table"][d]).astype(BF16)
        for i, sd in enumerate(scans):
            part = slice(0, 16) if RISING[sd] else slice(BLOCK - 16, BLOCK)
            sc["conved"][sd, part, :] = rows[16 * i : 16 * i + 16]

    for sd in range(4):
        d = SET[sd]
        tail = sc["conved"][sd, :, E:CH]
        b_rows = tail[:, :64]
        c_rows = pltpu.roll(tail.astype(F32), 64, axis=1)[:, :64].astype(BF16)
        sc["scores"][sd] = dot_t(c_rows, b_rows).astype(BF16)
        place = jnp.where(iota((64, E), 0) == 16 * sd + iota((64, E), 1) // 64, 1.0, 0.0).astype(BF16)
        weights = dot(sc["weigh"][...], place)
        weighted = weights.astype(BF16) * sc["table"][d, :, 0:E]
        state = dot(sc["b_columns"][d, 0:64, :], weighted).astype(BF16)
        sc["carried"][sd] = dot(c_rows, state)

    left = iota((BLOCK, 128), 1) < 64
    half = BLOCK // 2
    scales = []
    for sd in range(4):
        d, rising = SET[sd], RISING[sd]
        square = jnp.zeros((BLOCK, 128), F32)
        for pair in range(8):
            cols = slice(128 * pair, 128 * pair + 128)
            values = sc["conved"][sd, :, cols]
            parts = []
            for sub in range(2):
                h = 16 * sd + 2 * pair + sub
                skip = sc["skip_eye"][16 * d + 2 * pair + sub]
                rows_of = []
                for top in (True, False):
                    ts = slice(0, half) if top else slice(half, BLOCK)
                    mixing = sc["decay"][h, ts, ts] * sc["scores"][sd, ts, ts] + skip
                    if top == rising:
                        rows_of.append(dot(mixing, values[ts]))
                    else:
                        ss = slice(half, BLOCK) if top else slice(0, half)
                        far = sc["decay"][h, ts, ss] * sc["scores"][sd, ts, ss]
                        whole = [mixing, far] if top else [far, mixing]
                        rows_of.append(dot(jnp.concatenate(whole, axis=1), values))
                parts.append(jnp.concatenate(rows_of, axis=0))
            both = jnp.where(left, parts[0], parts[1]) + sc["carried"][sd, :, cols] * sc["grow"][sd, :, cols]
            gated = both * sc["gate"][STRAND[sd], :, cols]
            square = square + gated * gated
            sc["gated"][sd, :, cols] = gated
        mean = jnp.sum(square, axis=1, keepdims=True) * (1.0 / E)
        scales.append(lax.rsqrt(mean + EPS))
        between_scans(sd)
    for pair in range(8):
        cols = slice(128 * pair, 128 * pair + 128)
        ones, twos = [sc["gated"][0, :, cols] * scales[0], sc["gated"][3, :, cols] * scales[3]], [
            sc["gated"][1, :, cols] * scales[1],
            sc["gated"][2, :, cols] * scales[2],
        ]
        mixed = (ones[0] + ones[1]) * ng_ref[0:1, cols] + (twos[0] + twos[1]) * ng_ref[1:2, cols]
        sc["mixed"][:, cols] = mixed.astype(BF16)
    return sc["mixed"][...]


def scratch(blocks):
    return {
        "gate_parts": pltpu.VMEM((32, E), BF16),
        "conv_in": pltpu.VMEM((16, CH), F32),
        "coef": pltpu.VMEM((128, 128), F32),
        "skip_rows": pltpu.VMEM((8, E), F32),
        "words": pltpu.VMEM((4, blocks, BLOCK), jnp.int32),
        "s01": pltpu.VMEM((16, CH), F32),
        "s23": pltpu.VMEM((16, CH), F32),
        "table": pltpu.VMEM((2, ROWS, CH), BF16),
        "weigh": pltpu.VMEM((ROWS, 64), BF16),
        "edge": pltpu.VMEM((16, 64), F32),
        "tokens": pltpu.VMEM((blocks, BLOCK), jnp.int32),
        "run": pltpu.VMEM((128, BLOCK), F32),
        "from": pltpu.VMEM((64, BLOCK), F32),
        "local": pltpu.VMEM((128, BLOCK), F32),
        "gate": pltpu.VMEM((2, BLOCK, E), F32),
        "conved": pltpu.VMEM((4, BLOCK, CH), BF16),
        "scores": pltpu.VMEM((4, BLOCK, BLOCK), BF16),
        "swap": pltpu.VMEM((GRAMS, GRAMS), BF16),
        "skip_eye": pltpu.VMEM((32, 128, 128), BF16),
        "factor": pltpu.VMEM((2, 4, 96, 48), BF16),
        "counts": pltpu.VMEM((3, 4 * blocks, BLOCK), BF16),
        "fourfold": pltpu.VMEM((4 * blocks, BLOCK), jnp.int32),
        "run_t": pltpu.VMEM((BLOCK, 128), F32),
        "b_columns": pltpu.VMEM((2, 128, ROWS), BF16),
        "decay": pltpu.VMEM((64, BLOCK, BLOCK), BF16),
        "grow": pltpu.VMEM((4, BLOCK, E), F32),
        "carried": pltpu.VMEM((4, BLOCK, E), F32),
        "gated": pltpu.VMEM((4, BLOCK, E), F32),
        "mixed": pltpu.VMEM((BLOCK, E), BF16),
    }


MESH = pl.DeviceIdType.MESH
PARAMS = 10


def kernel(names, *refs):
    params, shard = refs[:PARAMS], refs[PARAMS]
    tok, out = refs[PARAMS + 1], refs[PARAMS + 2]
    sc = dict(zip(names, refs[PARAMS + 3 :]))
    batch, here = lax.axis_index("batch"), lax.axis_index("seq")
    z_low, core = lax.div(batch, 2), lax.rem(batch, 2)
    y, z_high, x = lax.div(here, 8), lax.rem(lax.div(here, 4), 2), lax.rem(here, 4)
    z = z_high * 4 + z_low
    received, wall = sc["received"], sc["wall"]
    partner = (z_low * 2 + 1 - core, here)
    barrier = pltpu.get_barrier_semaphore()

    def greet(device):
        pl.semaphore_signal(barrier, inc=1, device_id=device, device_id_type=MESH)

    def at(xx, yy, zz):
        return (lax.rem(zz, 4) * 2 + core, yy * 8 + lax.div(zz, 4) * 4 + xx)

    def loop(first, last, act):
        def go(k, carry):
            act(k)
            return carry

        lax.fori_loop(first, last, go, 0)

    loop(1, 8, lambda k: greet(at(x, y, lax.rem(z + k, 8))))
    loop(1, 16, lambda k: greet((batch, lax.div(lax.rem(4 * y + x + k, 16), 4) * 8 + 4 * z_high + lax.rem(x + k, 4))))
    greet(partner)

    def copy_of(piece, send, recv, device):
        return pltpu.make_async_remote_copy(piece, piece, send, recv, device, MESH)

    def token_z(owner):
        piece = received.at[y, x, owner]
        return copy_of(piece, sc["token_send"].at[0], sc["token_recv"].at[16], at(x, y, lax.rem(z + 4, 8)))

    def plane_peer(k):
        return lax.rem(4 * y + x + k, 16)

    def token_plane(k, owner):
        device = at(lax.rem(plane_peer(k), 4), lax.div(plane_peer(k), 4), z)
        piece = received.at[lax.div(owner, 4), lax.rem(owner, 4)]
        return copy_of(piece, sc["token_send"].at[k], sc["token_recv"].at[owner], device)

    mine, inner, outer = [y * 4 + x, x * 4 + y], [x, y], [y, x]

    def z_copy(c, k, owner):
        piece = wall.at[core, c, mine[c], owner]
        return copy_of(piece, sc["z_send"].at[c, k], sc["z_recv"].at[c, owner], at(x, y, lax.rem(z + k, 8)))

    def along(c, k, first):
        step_x, step_y = at(lax.rem(x + k, 4), y, z), at(x, lax.rem(y + k, 4), z)
        return step_x if (c == 0) == first else step_y

    def second_copy(c, k, owner):
        piece = wall.at[core, c, 4 * outer[c] + owner]
        return copy_of(piece, sc["second_send"].at[c, k], sc["second_recv"].at[c, owner], along(c, k, True))

    def third_copy(c, k, owner):
        piece = wall.at[core, c, pl.ds(4 * owner, 4)]
        return copy_of(piece, sc["third_send"].at[c, k], sc["third_recv"].at[c, owner], along(c, k, False))

    def core_copy(side, c, owner):
        piece = wall.at[side, c, pl.ds(4 * owner, 4)]
        return copy_of(piece, sc["core_send"].at[c, owner], sc["core_recv"].at[c, owner], partner)

    first = [pltpu.make_async_copy(tok, received.at[y, x, z_high], sc["own_sem"].at[0])]
    for c in range(2):
        half = shard.at[16 * c : 16 * c + 16]
        first.append(pltpu.make_async_copy(half, wall.at[core, c, mine[c], z], sc["own_sem"].at[1 + c]))
    fetch, held = [], []
    for i, ref in enumerate(params):
        held.append(sc[f"held{i}"])
        fetch.append(pltpu.make_async_copy(ref, held[i], sc["own_sem"].at[3 + i]))
    for copy in first + fetch:
        copy.start()
    for copy in first:
        copy.wait()

    def send():
        pl.semaphore_wait(barrier, 23)
        token_z(z_high).start()
        for c in range(2):
            loop(1, 8, lambda k: z_copy(c, k, z).start())

    last = z_high == 1

    pl.when(last)(send)
    for copy in fetch:
        copy.wait()
    comp_ref, emb, inw, stw, cw, cb, sb, dr, sg, ng = held
    comp = [comp_ref[v] for v in range(4)]
    letter_tables(
        comp, emb, inw, stw, (sb, dr, sg), sc["gate_parts"], sc["conv_in"], sc["coef"], sc["skip_rows"]
    )
    gram_tables(sc["conv_in"], cw, cb, sc["s01"], sc["s23"], sc["table"])
    pl.when(z_high == 0)(send)
    local_counts(received[y, x, z_high], sc)
    local_conv(received[y, x, z_high], comp, sc)
    for sd in range(4):
        local_decays(sd, sc)

    token_z(1 - z_high).wait_recv()
    loop(1, 16, lambda k: token_plane(k, 4 * y + x).start())
    for c in range(2):
        loop(1, 8, lambda k: z_copy(c, k, lax.rem(z + k, 8)).wait_recv())
        loop(1, 4, lambda k: second_copy(c, k, inner[c]).start())
    loop(1, 16, lambda k: token_plane(k, plane_peer(k)).wait_recv())
    for j in range(32):
        line = received[j // 8, j % 4, (j // 4) % 2]
        sc["tokens"][j : j + 1, :] = line
        sc["fourfold"][4 * j : 4 * j + 4, :] = jnp.broadcast_to(line, (4, BLOCK))

    def pass_on_second():
        for c in range(2):
            loop(1, 4, lambda k: second_copy(c, k, lax.rem(inner[c] + k, 4)).wait_recv())
            loop(1, 4, lambda k: third_copy(c, k, outer[c]).start())
            core_copy(core, c, outer[c]).start()

    def pass_on_third(sd):
        if sd < 2:
            for k in (1, 3) if sd == 0 else (2,):
                for c in range(2):
                    owner = lax.rem(outer[c] + k, 4)
                    third_copy(c, k, owner).wait_recv()
                    core_copy(core, c, owner).start()

    mixed = mixer(here, comp, sc["tokens"][...], cw, cb, ng, sc, pass_on_second, pass_on_third)
    for c in range(2):
        loop(0, 4, lambda q: core_copy(1 - core, c, q).wait_recv())
    order = []
    for s in range(32):
        yy, zz, xx = s // 8, 4 * ((s // 4) % 2), s % 4
        order += [(0, 4 * yy + xx, zz), (1, 4 * xx + yy, zz)]
    for low in range(4):
        sides = [jnp.concatenate([wall[k, c, p, zz + low] for c, p, zz in order], axis=0) for k in range(2)]
        out[:, 256 * low : 256 * low + 256] = dot(mixed, jnp.concatenate(sides, axis=1)).astype(BF16)

    for c in range(2):
        loop(1, 8, lambda k: z_copy(c, k, z).wait_send())
        loop(1, 4, lambda k: second_copy(c, k, inner[c]).wait_send())
        loop(1, 4, lambda k: third_copy(c, k, outer[c]).wait_send())
        loop(0, 4, lambda q: core_copy(core, c, q).wait_send())
    token_z(z_high).wait_send()
    loop(1, 16, lambda k: token_plane(k, 4 * y + x).wait_send())


def on_device(tok, comp, emb, inw, stw, cw, cb, sb, dr, sg, ng, wout):
    params = [comp, emb, inw, stw.T, cw, cb, sb, dr, sg, ng]
    shapes = scratch(32)
    shapes["received"] = pltpu.VMEM((4, 4, 2, 1, BLOCK), jnp.int32)
    shapes["wall"] = pltpu.VMEM((2, 2, 16, 8, 16, 128), BF16)
    shapes["own_sem"] = pltpu.SemaphoreType.DMA((3 + PARAMS,))
    for name, count in (("token", (17,)), ("z", (2, 8)), ("second", (2, 4)), ("third", (2, 4)), ("core", (2, 4))):
        shapes[name + "_send"] = pltpu.SemaphoreType.DMA(count)
        shapes[name + "_recv"] = pltpu.SemaphoreType.DMA(count)
    for i, value in enumerate(params):
        space = pltpu.SMEM if value.ndim == 1 else pltpu.VMEM
        shapes[f"held{i}"] = space(value.shape, value.dtype)
    anywhere = pl.BlockSpec(memory_space=pl.ANY)
    out = pl.pallas_call(
        partial(kernel, tuple(shapes)),
        out_shape=jax.ShapeDtypeStruct((BLOCK, D), BF16),
        in_specs=[anywhere] * (PARAMS + 2),
        out_specs=pl.BlockSpec(memory_space=pltpu.VMEM),
        scratch_shapes=list(shapes.values()),
        compiler_params=pltpu.CompilerParams(
            collective_id=0, has_side_effects=True, vmem_limit_bytes=44 << 20
        ),
    )(*[pltpu.with_memory_space_constraint(v, pltpu.HBM) for v in (*params, wout, tok)])
    return out[None]


def solution(mesh):
    placed = (P("batch", "seq"),) + (P(),) * 10 + (P("seq", "batch"),)
    return jax.shard_map(
        on_device, mesh=mesh, in_specs=placed, out_specs=P("batch", "seq", None), check_vma=False
    )
```
